512 devices in a mesh: dp: 16 (over z), row: 8 (over y, core), col: 4 (over x).
Axes of the slice: x: 4, y: 4, z: 16, core: 2. Of those that a mesh axis runs over, the one named last changes fastest.
Arguments:
- grad_blocks: bfloat16 [16, 4096, 1024], P('dp', 'row', 'col'), may hold values from -300 to 300
- ln_grads: bfloat16 [16, 4, 1024], P('dp', None, 'col'), may hold values from -240 to 240, as said below
- master: float32 [4096, 1024], P(('row', 'col')), may hold values from -6 to 6
- first_moment: float32 [4096, 1024], P(('row', 'col')), may hold values from -6 to 6
- second_moment: float32 [4096, 1024], P(('row', 'col')), may hold values from 0.3 to 3
- average: float32 [4096, 1024], P('row', 'col'), may hold values from -6 to 6
- ln_master: float32 [4, 1024], P(None, 'col'), may hold values from -6 to 6
- ln_first: float32 [4, 1024], P(None, 'col'), may hold values from -6 to 6
- ln_second: float32 [4, 1024], P(None, 'col'), may hold values from 0.3 to 3
- ln_average: float32 [4, 1024], P(None, 'col'), may hold values from -6 to 6
Outputs:
- average_new: float32 [4096, 1024], P('row', 'col')
- master_new: float32 [4096, 1024], P(('row', 'col'))
- first_new: float32 [4096, 1024], P(('row', 'col'))
- second_new: float32 [4096, 1024], P(('row', 'col'))
- ln_master_new: float32 [4, 1024], P(None, 'col')
- ln_first_new: float32 [4, 1024], P(None, 'col')
- ln_second_new: float32 [4, 1024], P(None, 'col')
- ln_average_new: float32 [4, 1024], P(None, 'col')
The draws below stay inside these ranges and needn't reach their ends.
Inputs may be any that keep to these rules, and one draw needn't show every extreme that they name: `ln_grads`: partial gradients of each data-parallel group.
All inputs are finite; a program needn't handle non-finite values.
Results may differ from the reference program's by a relative error of at most 0.0003.
Values may be sent and summed in bfloat16 or wider, within the bound.
A program may use at most 64 MiB of HBM per device.

```python
import math
import jax
import jax.numpy as jnp
from jax import lax

D = 1024
FF = 4096
STEP = 20
N_DP = 16


def draw_grad_blocks(key, part):
    keys = jax.random.split(key, 3)
    noise = jax.random.normal(keys[0], (N_DP, FF, D), jnp.float32)
    noise = jnp.clip(noise, -6.0, 6.0)
    row_level = jax.random.uniform(keys[1], (FF, 1), jnp.float32)
    col_level = jax.random.uniform(keys[2], (1, D), jnp.float32)
    row_trend = jnp.arange(FF, dtype=jnp.float32)[:, None] / FF
    col_trend = jnp.arange(D, dtype=jnp.float32)[None, :] / D
    scale = jnp.exp(jnp.log(10.0) * (row_level + col_level) + jnp.log(3.0) * (row_trend + col_trend) - jnp.log(3.0))
    values = jnp.clip(noise * scale[None, :, :], -300.0, 300.0)
    return values.astype(jnp.bfloat16)


def draw_ln_grads(key, part):
    keys = jax.random.split(key, 1)
    noise = jax.random.normal(keys[0], (N_DP, 4, D), jnp.float32)
    noise = jnp.clip(noise, -3.0, 3.0)
    return (80.0 * noise).astype(jnp.bfloat16)


def block_scale(rng, dims, shards, smallest, largest):
    level, own = 1.0, jax.random.fold_in(rng, 6)
    for position, parts in shards:
        draws = jnp.exp(jax.random.uniform(jax.random.fold_in(own, position), (parts,), jnp.float32, smallest / len(shards), largest / len(shards)))
        level = level * jnp.repeat(draws, dims[position] // parts).reshape([-1 if axis == position else 1 for axis in range(len(dims))])
    return level


def bell_draw(stream_key, dims, width, most, pieces=(), kind=jnp.bfloat16):
    level = block_scale(stream_key, dims, pieces, -0.22, 0.18) if pieces else 1.0
    array = jax.random.normal(stream_key, dims, jnp.float32) * width * level
    return jnp.minimum(jnp.maximum(array, -most), most).astype(kind)


def setup_inputs(seed: int = 0) -> dict:
    key_list = jax.random.split(jax.random.key(seed), 11)
    return {
        "grad_blocks": draw_grad_blocks(jax.random.fold_in(key_list[10], 71), 0),
        "ln_grads": draw_ln_grads(jax.random.fold_in(key_list[10], 71), 0),
        "master": bell_draw(key_list[2], (FF, D), 0.5, 6.0, ((0, 32),), jnp.float32),
        "first_moment": bell_draw(key_list[3], (FF, D), 0.5, 6.0, ((0, 32),), jnp.float32),
        "second_moment": jnp.clip(jnp.exp(math.log(3.0) - 2.3025851 * jax.random.uniform(key_list[4], (FF, D), jnp.float32) ** block_scale(key_list[4], (FF, D), ((0, 32),), -0.2, 0.2)), 0.3, 3.0),
        "average": bell_draw(key_list[5], (FF, D), 0.5, 6.0, ((0, 8), (1, 4)), jnp.float32),
        "ln_master": bell_draw(key_list[6], (4, D), 0.5, 6.0, ((1, 4),), jnp.float32),
        "ln_first": bell_draw(key_list[7], (4, D), 0.5, 6.0, ((1, 4),), jnp.float32),
        "ln_second": jnp.clip(jnp.exp(math.log(3.0) - 2.3025851 * jax.random.uniform(key_list[8], (4, D), jnp.float32) ** block_scale(key_list[8], (4, D), ((1, 4),), -0.2, 0.2)), 0.3, 3.0),
        "ln_average": bell_draw(key_list[9], (4, D), 0.5, 6.0, ((1, 4),), jnp.float32),
    }


beta_one = 0.9
beta_two = 0.95
learn_rate = 0.02
decay_rate = 0.1
epsilon = 1e-08
clip_rms = 1.0
ema_keep = 0.9

def adam_step(gradient, clip_scale, first, second, master, decay_weight):
    clipped = clip_scale * gradient
    first_new = beta_one * first + (1.0 - beta_one) * clipped
    second_new = beta_two * second + (1.0 - beta_two) * clipped * clipped
    direction = first_new / (1.0 - beta_one ** STEP) / (jnp.sqrt(second_new / (1.0 - beta_two ** STEP)) + epsilon)
    master_new = master - learn_rate * (direction + decay_weight * master)
    return (master_new, first_new, second_new)

def clip_factor(norm_total):
    return jnp.minimum(1.0, clip_rms * math.sqrt(FF * D + 4 * D) / jnp.sqrt(norm_total))

def reference(grad_blocks, ln_grads, master, first_moment, second_moment, average, ln_master, ln_first, ln_second, ln_average):
    gradient = lax.optimization_barrier(jnp.sum(grad_blocks.astype(jnp.float32), axis=0))
    ln_gradient = lax.optimization_barrier(jnp.sum(ln_grads.astype(jnp.float32), axis=0))
    norm_total = jnp.sum(gradient * gradient) + jnp.sum(ln_gradient * ln_gradient)
    clip_scale = clip_factor(norm_total)
    master_new, first_new, second_new = adam_step(gradient, clip_scale, first_moment, second_moment, master, decay_rate)
    ln_master_new, ln_first_new, ln_second_new = adam_step(ln_gradient, clip_scale, ln_first, ln_second, ln_master, 0.0)
    average_new = ema_keep * average + (1.0 - ema_keep) * master_new
    ln_average_new = ema_keep * ln_average + (1.0 - ema_keep) * ln_master_new
    return (average_new, master_new, first_new, second_new, ln_master_new, ln_first_new, ln_second_new, ln_average_new)
```

```python
import functools
import math

import jax
import jax.numpy as jnp
from jax import lax
from jax.experimental import pallas as pl
from jax.experimental.pallas import tpu as pltpu
from jax.sharding import PartitionSpec as P

MESH = pl.DeviceIdType.MESH

D = 1024
FF = 4096
STEP = 20


beta_one = 0.9
beta_two = 0.95
learn_rate = 0.02
decay_rate = 0.1
epsilon = 1e-08
clip_rms = 1.0
ema_keep = 0.9


def adam_step(gradient, clip_scale, first, second, master, decay_weight):
    clipped = clip_scale * gradient
    first_new = beta_one * first + (1.0 - beta_one) * clipped
    second_new = beta_two * second + (1.0 - beta_two) * clipped * clipped
    direction = (
        first_new
        / (1.0 - beta_one**STEP)
        / (jnp.sqrt(second_new / (1.0 - beta_two**STEP)) + epsilon)
    )
    master_new = master - learn_rate * (direction + decay_weight * master)
    return (master_new, first_new, second_new)


def clip_factor(norm_total):
    return jnp.minimum(1.0, clip_rms * math.sqrt(FF * D + 4 * D) / jnp.sqrt(norm_total))


def squares(gradient, ln_gradient, row_count):
    return jnp.sum(gradient * gradient) + jnp.sum(ln_gradient * ln_gradient) / row_count


def norm_kernel(n_row, n_col, x_ref, o_ref, buf, send_sem, recv_sem):
    d = lax.axis_index("dp")
    me = lax.axis_index("row") * n_col + lax.axis_index("col")
    n = n_row * n_col
    barrier = pltpu.get_barrier_semaphore()
    for j in range(1, n):
        peer = lax.rem(me + j, n)
        pl.semaphore_signal(
            barrier, inc=1, device_id=(d, peer // n_col, peer % n_col), device_id_type=MESH
        )
    pl.semaphore_wait(barrier, n - 1)
    copies = []
    for j in range(1, n):
        peer = lax.rem(me + j, n)
        copy = pltpu.make_async_remote_copy(
            src_ref=x_ref,
            dst_ref=buf.at[me],
            send_sem=send_sem.at[j],
            recv_sem=recv_sem.at[me],
            device_id=(d, peer // n_col, peer % n_col),
            device_id_type=MESH,
        )
        copy.start()
        copies.append(copy)
    buf[me] = x_ref[...]
    for j in range(1, n):
        sender = lax.rem(me + n - j, n)
        pltpu.make_async_remote_copy(
            src_ref=x_ref,
            dst_ref=buf.at[sender],
            send_sem=send_sem.at[j],
            recv_sem=recv_sem.at[sender],
            device_id=(d, sender // n_col, sender % n_col),
            device_id_type=MESH,
        ).wait_recv()
    for copy in copies:
        copy.wait_send()
    o_ref[...] = jnp.sum(buf[...], axis=0)


def group_sum(value):
    n_row, n_col = lax.axis_size("row"), lax.axis_size("col")
    n = n_row * n_col
    tile = jnp.full((8, 128), value, jnp.float32)
    out = pl.pallas_call(
        functools.partial(norm_kernel, n_row, n_col),
        out_shape=jax.ShapeDtypeStruct((8, 128), jnp.float32),
        in_specs=[pl.BlockSpec(memory_space=pltpu.VMEM)],
        out_specs=pl.BlockSpec(memory_space=pltpu.VMEM),
        scratch_shapes=[
            pltpu.VMEM((n, 8, 128), jnp.float32),
            pltpu.SemaphoreType.DMA((n,)),
            pltpu.SemaphoreType.DMA((n,)),
        ],
        compiler_params=pltpu.CompilerParams(collective_id=0, has_side_effects=True),
    )(tile)
    return out[0, 0]


def shards(
    grad_blocks,
    ln_grads,
    master,
    first_moment,
    second_moment,
    average,
    ln_master,
    ln_first,
    ln_second,
    ln_average,
):
    row_count = float(lax.axis_size("row"))
    summed, ln_gradient = lax.psum(
        (grad_blocks[0].astype(jnp.float32), ln_grads[0].astype(jnp.float32)), "dp"
    )
    gradient = lax.all_to_all(summed, "col", split_axis=0, concat_axis=1, tiled=True)
    norm_total = group_sum(squares(gradient, ln_gradient, row_count))
    clip_scale = clip_factor(norm_total)
    master_new, first_new, second_new = adam_step(
        gradient, clip_scale, first_moment, second_moment, master, decay_rate
    )
    ln_master_new, ln_first_new, ln_second_new = adam_step(
        ln_gradient, clip_scale, ln_first, ln_second, ln_master, 0.0
    )
    ln_average_new = ema_keep * ln_average + (1.0 - ema_keep) * ln_master_new
    block_master = lax.all_to_all(master_new, "col", split_axis=1, concat_axis=0, tiled=True)
    average_new = ema_keep * average + (1.0 - ema_keep) * block_master
    return (
        average_new,
        master_new,
        first_new,
        second_new,
        ln_master_new,
        ln_first_new,
        ln_second_new,
        ln_average_new,
    )


def solution(mesh):
    placed = (
        P("dp", "row", "col"),
        P("dp", None, "col"),
        P(("row", "col"), None),
        P(("row", "col"), None),
        P(("row", "col"), None),
        P("row", "col"),
        P(None, "col"),
        P(None, "col"),
        P(None, "col"),
        P(None, "col"),
    )
    return jax.shard_map(
        shards,
        mesh=mesh,
        in_specs=placed,
        out_specs=(
            P("row", "col"),
            P(("row", "col"), None),
            P(("row", "col"), None),
            P(("row", "col"), None),
            P(None, "col"),
            P(None, "col"),
            P(None, "col"),
            P(None, "col"),
        ),
        check_vma=False,
    )
```

```python
import functools
import math

import jax
import jax.numpy as jnp
from jax import lax
from jax.experimental import pallas as pl
from jax.experimental.pallas import tpu as pltpu
from jax.sharding import PartitionSpec as P

MESH = pl.DeviceIdType.MESH

D = 1024
FF = 4096
STEP = 20


beta_one = 0.9
beta_two = 0.95
learn_rate = 0.02
decay_rate = 0.1
epsilon = 1e-08
clip_rms = 1.0
ema_keep = 0.9


def adam_step(gradient, clip_scale, first, second, master, decay_weight):
    clipped = clip_scale * gradient
    first_new = beta_one * first + (1.0 - beta_one) * clipped
    second_new = beta_two * second + (1.0 - beta_two) * clipped * clipped
    direction = (
        first_new
        / (1.0 - beta_one**STEP)
        / (jnp.sqrt(second_new / (1.0 - beta_two**STEP)) + epsilon)
    )
    master_new = master - learn_rate * (direction + decay_weight * master)
    return (master_new, first_new, second_new)


def clip_factor(norm_total):
    return jnp.minimum(1.0, clip_rms * math.sqrt(FF * D + 4 * D) / jnp.sqrt(norm_total))


def squares(gradient, ln_gradient, row_count):
    return jnp.sum(gradient * gradient) + jnp.sum(ln_gradient * ln_gradient) / row_count


def norm_kernel(n_row, n_col, x_ref, o_ref, buf, send_sem, recv_sem):
    d = lax.axis_index("dp")
    me = lax.axis_index("row") * n_col + lax.axis_index("col")
    n = n_row * n_col
    barrier = pltpu.get_barrier_semaphore()
    for j in range(1, n):
        peer = lax.rem(me + j, n)
        pl.semaphore_signal(
            barrier, inc=1, device_id=(d, peer // n_col, peer % n_col), device_id_type=MESH
        )
    pl.semaphore_wait(barrier, n - 1)
    copies = []
    for j in range(1, n):
        peer = lax.rem(me + j, n)
        copy = pltpu.make_async_remote_copy(
            src_ref=x_ref,
            dst_ref=buf.at[me],
            send_sem=send_sem.at[j],
            recv_sem=recv_sem.at[me],
            device_id=(d, peer // n_col, peer % n_col),
            device_id_type=MESH,
        )
        copy.start()
        copies.append(copy)
    buf[me] = x_ref[...]
    for j in range(1, n):
        sender = lax.rem(me + n - j, n)
        pltpu.make_async_remote_copy(
            src_ref=x_ref,
            dst_ref=buf.at[sender],
            send_sem=send_sem.at[j],
            recv_sem=recv_sem.at[sender],
            device_id=(d, sender // n_col, sender % n_col),
            device_id_type=MESH,
        ).wait_recv()
    for copy in copies:
        copy.wait_send()
    o_ref[...] = jnp.sum(buf[...], axis=0)


def group_sum(value):
    n_row, n_col = lax.axis_size("row"), lax.axis_size("col")
    n = n_row * n_col
    tile = jnp.full((8, 128), value, jnp.float32)
    out = pl.pallas_call(
        functools.partial(norm_kernel, n_row, n_col),
        out_shape=jax.ShapeDtypeStruct((8, 128), jnp.float32),
        in_specs=[pl.BlockSpec(memory_space=pltpu.VMEM)],
        out_specs=pl.BlockSpec(memory_space=pltpu.VMEM),
        scratch_shapes=[
            pltpu.VMEM((n, 8, 128), jnp.float32),
            pltpu.SemaphoreType.DMA((n,)),
            pltpu.SemaphoreType.DMA((n,)),
        ],
        compiler_params=pltpu.CompilerParams(collective_id=0, has_side_effects=True),
    )(tile)
    return out[0, 0]


def reduce_kernel(n_dp, n_col, g_ref, ln_ref, g_out, ln_out, rs_buf, ag_buf, ln_buf,
                  rs_send, rs_recv, ag_send, ag_recv, ln_send, ln_recv):
    d = lax.axis_index("dp")
    r = lax.axis_index("row")
    c = lax.axis_index("col")
    n = n_dp * n_col
    me = d * n_col + c
    quarter = g_ref.shape[0] // n_col
    depth = rs_buf.shape[2]
    width = rs_buf.shape[3]
    halves = g_ref.shape[1] // width
    barrier = pltpu.get_barrier_semaphore()

    def greet(j, carry):
        peer = lax.rem(me + j, n)
        pl.semaphore_signal(
            barrier, inc=1, device_id=(peer // n_col, r, peer % n_col), device_id_type=MESH
        )
        return carry

    lax.fori_loop(1, n, greet, 0)
    pl.semaphore_wait(barrier, n - 1)

    def piece(k, q):
        rows = pl.ds(pl.multiple_of(q * quarter + (k // halves) * depth, depth), depth)
        cols = pl.ds(pl.multiple_of((k % halves) * width, width), width)
        return g_ref.at[rows, cols]

    def rs_copy(j):
        peer = lax.rem(me + j, n)
        return pltpu.make_async_remote_copy(
            src_ref=piece(peer // n_col, peer % n_col),
            dst_ref=rs_buf.at[d, c],
            send_sem=rs_send.at[j],
            recv_sem=rs_recv.at[me],
            device_id=(peer // n_col, r, peer % n_col),
            device_id_type=MESH,
        )

    def ln_copy(j):
        peer = lax.rem(d + j, n_dp)
        return pltpu.make_async_remote_copy(
            src_ref=ln_ref,
            dst_ref=ln_buf.at[d],
            send_sem=ln_send.at[j],
            recv_sem=ln_recv.at[d],
            device_id=(peer, r, c),
            device_id_type=MESH,
        )

    def start_rs(j, carry):
        rs_copy(j).start()
        return carry

    def start_ln(j, carry):
        ln_copy(j).start()
        return carry

    lax.fori_loop(1, n, start_rs, 0)
    lax.fori_loop(1, n_dp, start_ln, 0)
    rs_buf[d, c] = piece(d, c)[...]
    ln_buf[d] = ln_ref[...]

    def wait_rs(j, carry):
        src = lax.rem(me + j, n)
        pltpu.make_async_remote_copy(
            src_ref=piece(0, 0),
            dst_ref=rs_buf.at[src // n_col, src % n_col],
            send_sem=rs_send.at[j],
            recv_sem=rs_recv.at[src],
            device_id=(src // n_col, r, src % n_col),
            device_id_type=MESH,
        ).wait_recv()
        rs_copy(j).wait_send()
        return carry

    lax.fori_loop(1, n, wait_rs, 0)
    ag_buf[d] = jnp.sum(rs_buf[...].astype(jnp.float32), axis=0)

    def ag_copy(j):
        peer = lax.rem(d + j, n_dp)
        return pltpu.make_async_remote_copy(
            src_ref=ag_buf.at[d],
            dst_ref=ag_buf.at[d],
            send_sem=ag_send.at[j],
            recv_sem=ag_recv.at[d],
            device_id=(peer, r, c),
            device_id_type=MESH,
        )

    def start_ag(j, carry):
        ag_copy(j).start()
        return carry

    lax.fori_loop(1, n_dp, start_ag, 0)

    def wait_ln(j, carry):
        src = lax.rem(d + j, n_dp)
        pltpu.make_async_remote_copy(
            src_ref=ln_ref,
            dst_ref=ln_buf.at[src],
            send_sem=ln_send.at[j],
            recv_sem=ln_recv.at[src],
            device_id=(src, r, c),
            device_id_type=MESH,
        ).wait_recv()
        ln_copy(j).wait_send()
        return carry

    lax.fori_loop(1, n_dp, wait_ln, 0)
    ln_out[...] = jnp.sum(ln_buf[...].astype(jnp.float32), axis=0)

    def wait_ag(j, carry):
        src = lax.rem(d + j, n_dp)
        pltpu.make_async_remote_copy(
            src_ref=ag_buf.at[src],
            dst_ref=ag_buf.at[src],
            send_sem=ag_send.at[j],
            recv_sem=ag_recv.at[src],
            device_id=(src, r, c),
            device_id_type=MESH,
        ).wait_recv()
        ag_copy(j).wait_send()
        return carry

    lax.fori_loop(1, n_dp, wait_ag, 0)
    for k in range(n_dp):
        for q in range(n_col):
            g_out[
                pl.ds((k // halves) * depth, depth),
                pl.ds(q * halves * width + (k % halves) * width, width),
            ] = ag_buf[k, q]


def reduce_blocks(block, ln_part):
    n_dp, n_col = lax.axis_size("dp"), lax.axis_size("col")
    rows, cols = block.shape
    quarter = rows // n_col
    width = 128
    halves = cols // width
    depth = quarter * halves // n_dp
    vmem = pl.BlockSpec(memory_space=pltpu.VMEM)
    return pl.pallas_call(
        functools.partial(reduce_kernel, n_dp, n_col),
        out_shape=(
            jax.ShapeDtypeStruct((quarter, cols * n_col), jnp.float32),
            jax.ShapeDtypeStruct(ln_part.shape, jnp.float32),
        ),
        in_specs=[vmem, vmem],
        out_specs=(vmem, vmem),
        scratch_shapes=[
            pltpu.VMEM((n_dp, n_col, depth, width), block.dtype),
            pltpu.VMEM((n_dp, n_col, depth, width), jnp.float32),
            pltpu.VMEM((n_dp,) + ln_part.shape, ln_part.dtype),
            pltpu.SemaphoreType.DMA((n_dp * n_col,)),
            pltpu.SemaphoreType.DMA((n_dp * n_col,)),
            pltpu.SemaphoreType.DMA((n_dp,)),
            pltpu.SemaphoreType.DMA((n_dp,)),
            pltpu.SemaphoreType.DMA((n_dp,)),
            pltpu.SemaphoreType.DMA((n_dp,)),
        ],
        compiler_params=pltpu.CompilerParams(collective_id=1, has_side_effects=True),
    )(block, ln_part)


def shards(
    grad_blocks,
    ln_grads,
    master,
    first_moment,
    second_moment,
    average,
    ln_master,
    ln_first,
    ln_second,
    ln_average,
):
    row_count = float(lax.axis_size("row"))
    gradient, ln_gradient = reduce_blocks(grad_blocks[0], ln_grads[0])
    norm_total = group_sum(squares(gradient, ln_gradient, row_count))
    clip_scale = clip_factor(norm_total)
    master_new, first_new, second_new = adam_step(
        gradient, clip_scale, first_moment, second_moment, master, decay_rate
    )
    ln_master_new, ln_first_new, ln_second_new = adam_step(
        ln_gradient, clip_scale, ln_first, ln_second, ln_master, 0.0
    )
    ln_average_new = ema_keep * ln_average + (1.0 - ema_keep) * ln_master_new
    block_master = lax.all_to_all(master_new, "col", split_axis=1, concat_axis=0, tiled=True)
    average_new = ema_keep * average + (1.0 - ema_keep) * block_master
    return (
        average_new,
        master_new,
        first_new,
        second_new,
        ln_master_new,
        ln_first_new,
        ln_second_new,
        ln_average_new,
    )


def solution(mesh):
    placed = (
        P("dp", "row", "col"),
        P("dp", None, "col"),
        P(("row", "col"), None),
        P(("row", "col"), None),
        P(("row", "col"), None),
        P("row", "col"),
        P(None, "col"),
        P(None, "col"),
        P(None, "col"),
        P(None, "col"),
    )
    return jax.shard_map(
        shards,
        mesh=mesh,
        in_specs=placed,
        out_specs=(
            P("row", "col"),
            P(("row", "col"), None),
            P(("row", "col"), None),
            P(("row", "col"), None),
            P(None, "col"),
            P(None, "col"),
            P(None, "col"),
            P(None, "col"),
        ),
        check_vma=False,
    )
```

```python
import functools
import math

import jax
import jax.numpy as jnp
from jax import lax
from jax.experimental import pallas as pl
from jax.experimental.pallas import tpu as pltpu
from jax.sharding import PartitionSpec as P

MESH = pl.DeviceIdType.MESH

D = 1024
FF = 4096
STEP = 20


beta_one = 0.9
beta_two = 0.95
learn_rate = 0.02
decay_rate = 0.1
epsilon = 1e-08
clip_rms = 1.0
ema_keep = 0.9


def adam_step(gradient, clip_scale, first, second, master, decay_weight):
    clipped = clip_scale * gradient
    first_new = beta_one * first + (1.0 - beta_one) * clipped
    second_new = beta_two * second + (1.0 - beta_two) * clipped * clipped
    direction = (
        first_new
        / (1.0 - beta_one**STEP)
        / (jnp.sqrt(second_new / (1.0 - beta_two**STEP)) + epsilon)
    )
    master_new = master - learn_rate * (direction + decay_weight * master)
    return (master_new, first_new, second_new)


def clip_factor(norm_total):
    return jnp.minimum(1.0, clip_rms * math.sqrt(FF * D + 4 * D) / jnp.sqrt(norm_total))


def squares(gradient, ln_gradient, row_count):
    return jnp.sum(gradient * gradient) + jnp.sum(ln_gradient * ln_gradient) / row_count


def norm_kernel(n_row, n_col, x_ref, o_ref, buf, send_sem, recv_sem):
    d = lax.axis_index("dp")
    me = lax.axis_index("row") * n_col + lax.axis_index("col")
    n = n_row * n_col
    barrier = pltpu.get_barrier_semaphore()
    for j in range(1, n):
        peer = lax.rem(me + j, n)
        pl.semaphore_signal(
            barrier, inc=1, device_id=(d, peer // n_col, peer % n_col), device_id_type=MESH
        )
    pl.semaphore_wait(barrier, n - 1)
    copies = []
    for j in range(1, n):
        peer = lax.rem(me + j, n)
        copy = pltpu.make_async_remote_copy(
            src_ref=x_ref,
            dst_ref=buf.at[me],
            send_sem=send_sem.at[j],
            recv_sem=recv_sem.at[me],
            device_id=(d, peer // n_col, peer % n_col),
            device_id_type=MESH,
        )
        copy.start()
        copies.append(copy)
    buf[me] = x_ref[...]
    for j in range(1, n):
        sender = lax.rem(me + n - j, n)
        pltpu.make_async_remote_copy(
            src_ref=x_ref,
            dst_ref=buf.at[sender],
            send_sem=send_sem.at[j],
            recv_sem=recv_sem.at[sender],
            device_id=(d, sender // n_col, sender % n_col),
            device_id_type=MESH,
        ).wait_recv()
    for copy in copies:
        copy.wait_send()
    o_ref[...] = jnp.sum(buf[...], axis=0)


def group_sum(value):
    n_row, n_col = lax.axis_size("row"), lax.axis_size("col")
    n = n_row * n_col
    tile = jnp.full((8, 128), value, jnp.float32)
    out = pl.pallas_call(
        functools.partial(norm_kernel, n_row, n_col),
        out_shape=jax.ShapeDtypeStruct((8, 128), jnp.float32),
        in_specs=[pl.BlockSpec(memory_space=pltpu.VMEM)],
        out_specs=pl.BlockSpec(memory_space=pltpu.VMEM),
        scratch_shapes=[
            pltpu.VMEM((n, 8, 128), jnp.float32),
            pltpu.SemaphoreType.DMA((n,)),
            pltpu.SemaphoreType.DMA((n,)),
        ],
        compiler_params=pltpu.CompilerParams(collective_id=0, has_side_effects=True),
    )(tile)
    return out[0, 0]


def reduce_kernel(n_dp, n_col, g_ref, ln_ref, g_out, ln_out, rs_buf, ag_buf, ln_buf,
                  rs_send, rs_recv, ag_send, ag_recv, ag_lsend, ag_lrecv, ln_send, ln_recv):
    d = lax.axis_index("dp")
    r = lax.axis_index("row")
    c = lax.axis_index("col")
    n = n_dp * n_col
    me = d * n_col + c
    quarter = g_ref.shape[0] // n_col
    depth = rs_buf.shape[2]
    width = rs_buf.shape[3]
    halves = g_ref.shape[1] // width
    barrier = pltpu.get_barrier_semaphore()

    def greet(j, carry):
        peer = lax.rem(me + j, n)
        pl.semaphore_signal(
            barrier, inc=1, device_id=(peer // n_col, r, peer % n_col), device_id_type=MESH
        )
        return carry

    lax.fori_loop(1, n, greet, 0)
    pl.semaphore_wait(barrier, n - 1)

    def piece(k, q):
        rows = pl.ds(pl.multiple_of(q * quarter + (k // halves) * depth, depth), depth)
        cols = pl.ds(pl.multiple_of((k % halves) * width, width), width)
        return g_ref.at[rows, cols]

    def rs_copy(j):
        peer = lax.rem(me + j, n)
        return pltpu.make_async_remote_copy(
            src_ref=piece(peer // n_col, peer % n_col),
            dst_ref=rs_buf.at[d, c],
            send_sem=rs_send.at[j],
            recv_sem=rs_recv.at[me],
            device_id=(peer // n_col, r, peer % n_col),
            device_id_type=MESH,
        )

    def ln_copy(j):
        peer = lax.rem(d + j, n_dp)
        return pltpu.make_async_remote_copy(
            src_ref=ln_ref,
            dst_ref=ln_buf.at[d],
            send_sem=ln_send.at[j],
            recv_sem=ln_recv.at[d],
            device_id=(peer, r, c),
            device_id_type=MESH,
        )

    def start_rs(j, carry):
        rs_copy(j).start()
        return carry

    def start_ln(j, carry):
        ln_copy(j).start()
        return carry

    lax.fori_loop(1, n, start_rs, 0)
    lax.fori_loop(1, n_dp, start_ln, 0)
    rs_buf[d, c] = piece(d, c)[...]
    ln_buf[d] = ln_ref[...]

    def wait_rs(j, carry):
        src = lax.rem(me + j, n)
        pltpu.make_async_remote_copy(
            src_ref=piece(0, 0),
            dst_ref=rs_buf.at[src // n_col, src % n_col],
            send_sem=rs_send.at[j],
            recv_sem=rs_recv.at[src],
            device_id=(src // n_col, r, src % n_col),
            device_id_type=MESH,
        ).wait_recv()
        rs_copy(j).wait_send()
        return carry

    lax.fori_loop(1, n, wait_rs, 0)
    ag_buf[d] = jnp.sum(rs_buf[...].astype(jnp.float32), axis=0)

    def ring_copy(slot, step, toward, send_sem, recv_sem):
        return pltpu.make_async_remote_copy(
            src_ref=ag_buf.at[slot],
            dst_ref=ag_buf.at[slot],
            send_sem=send_sem.at[step],
            recv_sem=recv_sem.at[slot],
            device_id=(toward, r, c),
            device_id_type=MESH,
        )

    right = lax.rem(d + 1, n_dp)
    left = lax.rem(d + n_dp - 1, n_dp)
    n_right = n_dp // 2
    n_left = n_dp - 1 - n_right
    sends = []
    for step in range(1, n_right + 1):
        slot = lax.rem(d + n_dp - step + 1, n_dp)
        if step > 1:
            ring_copy(slot, step, left, ag_send, ag_recv).wait_recv()
        copy = ring_copy(slot, step, right, ag_send, ag_recv)
        copy.start()
        sends.append(copy)
        if step <= n_left:
            slot = lax.rem(d + step - 1, n_dp)
            if step > 1:
                ring_copy(slot, step, right, ag_lsend, ag_lrecv).wait_recv()
            copy = ring_copy(slot, step, left, ag_lsend, ag_lrecv)
            copy.start()
            sends.append(copy)

    def wait_ln(j, carry):
        src = lax.rem(d + j, n_dp)
        pltpu.make_async_remote_copy(
            src_ref=ln_ref,
            dst_ref=ln_buf.at[src],
            send_sem=ln_send.at[j],
            recv_sem=ln_recv.at[src],
            device_id=(src, r, c),
            device_id_type=MESH,
        ).wait_recv()
        ln_copy(j).wait_send()
        return carry

    lax.fori_loop(1, n_dp, wait_ln, 0)
    ln_out[...] = jnp.sum(ln_buf[...].astype(jnp.float32), axis=0)

    ring_copy(lax.rem(d + n_dp - n_right, n_dp), 0, left, ag_send, ag_recv).wait_recv()
    ring_copy(lax.rem(d + n_left, n_dp), 0, right, ag_lsend, ag_lrecv).wait_recv()
    for copy in sends:
        copy.wait_send()
    for k in range(n_dp):
        for q in range(n_col):
            g_out[
                pl.ds((k // halves) * depth, depth),
                pl.ds(q * halves * width + (k % halves) * width, width),
            ] = ag_buf[k, q]


def reduce_blocks(block, ln_part):
    n_dp, n_col = lax.axis_size("dp"), lax.axis_size("col")
    rows, cols = block.shape
    quarter = rows // n_col
    width = 128
    halves = cols // width
    depth = quarter * halves // n_dp
    vmem = pl.BlockSpec(memory_space=pltpu.VMEM)
    return pl.pallas_call(
        functools.partial(reduce_kernel, n_dp, n_col),
        out_shape=(
            jax.ShapeDtypeStruct((quarter, cols * n_col), jnp.float32),
            jax.ShapeDtypeStruct(ln_part.shape, jnp.float32),
        ),
        in_specs=[vmem, vmem],
        out_specs=(vmem, vmem),
        scratch_shapes=[
            pltpu.VMEM((n_dp, n_col, depth, width), block.dtype),
            pltpu.VMEM((n_dp, n_col, depth, width), jnp.float32),
            pltpu.VMEM((n_dp,) + ln_part.shape, ln_part.dtype),
            pltpu.SemaphoreType.DMA((n_dp * n_col,)),
            pltpu.SemaphoreType.DMA((n_dp * n_col,)),
            pltpu.SemaphoreType.DMA((n_dp,)),
            pltpu.SemaphoreType.DMA((n_dp,)),
            pltpu.SemaphoreType.DMA((n_dp,)),
            pltpu.SemaphoreType.DMA((n_dp,)),
            pltpu.SemaphoreType.DMA((n_dp,)),
            pltpu.SemaphoreType.DMA((n_dp,)),
        ],
        compiler_params=pltpu.CompilerParams(collective_id=1, has_side_effects=True),
    )(block, ln_part)


def shards(
    grad_blocks,
    ln_grads,
    master,
    first_moment,
    second_moment,
    average,
    ln_master,
    ln_first,
    ln_second,
    ln_average,
):
    row_count = float(lax.axis_size("row"))
    gradient, ln_gradient = reduce_blocks(grad_blocks[0], ln_grads[0])
    norm_total = group_sum(squares(gradient, ln_gradient, row_count))
    clip_scale = clip_factor(norm_total)
    master_new, first_new, second_new = adam_step(
        gradient, clip_scale, first_moment, second_moment, master, decay_rate
    )
    ln_master_new, ln_first_new, ln_second_new = adam_step(
        ln_gradient, clip_scale, ln_first, ln_second, ln_master, 0.0
    )
    ln_average_new = ema_keep * ln_average + (1.0 - ema_keep) * ln_master_new
    block_master = lax.all_to_all(master_new, "col", split_axis=1, concat_axis=0, tiled=True)
    average_new = ema_keep * average + (1.0 - ema_keep) * block_master
    return (
        average_new,
        master_new,
        first_new,
        second_new,
        ln_master_new,
        ln_first_new,
        ln_second_new,
        ln_average_new,
    )


def solution(mesh):
    placed = (
        P("dp", "row", "col"),
        P("dp", None, "col"),
        P(("row", "col"), None),
        P(("row", "col"), None),
        P(("row", "col"), None),
        P("row", "col"),
        P(None, "col"),
        P(None, "col"),
        P(None, "col"),
        P(None, "col"),
    )
    return jax.shard_map(
        shards,
        mesh=mesh,
        in_specs=placed,
        out_specs=(
            P("row", "col"),
            P(("row", "col"), None),
            P(("row", "col"), None),
            P(("row", "col"), None),
            P(None, "col"),
            P(None, "col"),
            P(None, "col"),
            P(None, "col"),
        ),
        check_vma=False,
    )
```

```python
import functools
import math

import jax
import jax.numpy as jnp
from jax import lax
from jax.experimental import pallas as pl
from jax.experimental.pallas import tpu as pltpu
from jax.sharding import PartitionSpec as P

MESH = pl.DeviceIdType.MESH

D = 1024
FF = 4096
STEP = 20


beta_one = 0.9
beta_two = 0.95
learn_rate = 0.02
decay_rate = 0.1
epsilon = 1e-08
clip_rms = 1.0
ema_keep = 0.9


def adam_step(gradient, clip_scale, first, second, master, decay_weight):
    clipped = clip_scale * gradient
    first_new = beta_one * first + (1.0 - beta_one) * clipped
    second_new = beta_two * second + (1.0 - beta_two) * clipped * clipped
    direction = (
        first_new
        / (1.0 - beta_one**STEP)
        / (jnp.sqrt(second_new / (1.0 - beta_two**STEP)) + epsilon)
    )
    master_new = master - learn_rate * (direction + decay_weight * master)
    return (master_new, first_new, second_new)


def clip_factor(norm_total):
    return jnp.minimum(1.0, clip_rms * math.sqrt(FF * D + 4 * D) / jnp.sqrt(norm_total))


def squares(gradient, ln_gradient, row_count):
    return jnp.sum(gradient * gradient) + jnp.sum(ln_gradient * ln_gradient) / row_count


def finish_kernel(n_row, n_col, g_ref, lg_ref, m_ref, f_ref, s_ref, a_ref,
                  lm_ref, lf_ref, ls_ref, la_ref,
                  a_out, m_out, f_out, s_out, lm_out, lf_out, ls_out, la_out,
                  nbuf, mbuf, n_send, n_recv, m_send, m_recv):
    d = lax.axis_index("dp")
    r = lax.axis_index("row")
    c = lax.axis_index("col")
    me = r * n_col + c
    n = n_row * n_col
    barrier = pltpu.get_barrier_semaphore()
    for j in range(1, n):
        peer = lax.rem(me + j, n)
        pl.semaphore_signal(
            barrier, inc=1, device_id=(d, peer // n_col, peer % n_col), device_id_type=MESH
        )
    pl.semaphore_wait(barrier, n - 1)
    g = g_ref[...]
    lg = lg_ref[...]
    part = jnp.sum(g * g) + jnp.sum(lg * lg) / float(n_row)
    nbuf[me] = jnp.full(nbuf.shape[1:], part, jnp.float32)

    def n_copy(j, peer, slot):
        return pltpu.make_async_remote_copy(
            src_ref=nbuf.at[slot],
            dst_ref=nbuf.at[slot],
            send_sem=n_send.at[j],
            recv_sem=n_recv.at[slot],
            device_id=(d, peer // n_col, peer % n_col),
            device_id_type=MESH,
        )

    copies = []
    for j in range(1, n):
        copy = n_copy(j, lax.rem(me + j, n), me)
        copy.start()
        copies.append(copy)
    for j in range(1, n):
        sender = lax.rem(me + n - j, n)
        n_copy(j, sender, sender).wait_recv()
    for copy in copies:
        copy.wait_send()
    norm_total = jnp.sum(nbuf[...], axis=0)[0:1, 0:1]
    clip_scale = clip_factor(norm_total)
    master_new, first_new, second_new = adam_step(
        g, clip_scale, f_ref[...], s_ref[...], m_ref[...], decay_rate
    )
    m_out[...] = master_new
    f_out[...] = first_new
    s_out[...] = second_new
    width = mbuf.shape[2]

    def m_copy(j, peer, slot):
        return pltpu.make_async_remote_copy(
            src_ref=m_out.at[:, pl.ds(pl.multiple_of(peer * width, width), width)],
            dst_ref=mbuf.at[slot],
            send_sem=m_send.at[j],
            recv_sem=m_recv.at[slot],
            device_id=(d, r, peer),
            device_id_type=MESH,
        )

    copies = []
    for j in range(1, n_col):
        copy = m_copy(j, lax.rem(c + j, n_col), c)
        copy.start()
        copies.append(copy)
    mbuf[c] = m_out[:, pl.ds(pl.multiple_of(c * width, width), width)]
    ln_master_new, ln_first_new, ln_second_new = adam_step(
        lg, clip_scale, lf_ref[...], ls_ref[...], lm_ref[...], 0.0
    )
    lm_out[...] = ln_master_new
    lf_out[...] = ln_first_new
    ls_out[...] = ln_second_new
    la_out[...] = ema_keep * la_ref[...] + (1.0 - ema_keep) * ln_master_new
    for j in range(1, n_col):
        sender = lax.rem(c + n_col - j, n_col)
        m_copy(j, sender, sender).wait_recv()
    for copy in copies:
        copy.wait_send()
    depth = mbuf.shape[1]
    for q in range(n_col):
        rows = pl.ds(q * depth, depth)
        a_out[rows, :] = ema_keep * a_ref[rows, :] + (1.0 - ema_keep) * mbuf[q]


def finish(gradient, ln_gradient, master, first, second, average, ln_master, ln_first, ln_second, ln_average):
    n_row, n_col = lax.axis_size("row"), lax.axis_size("col")
    n = n_row * n_col
    vmem = pl.BlockSpec(memory_space=pltpu.VMEM)
    outs = (average, master, first, second, ln_master, ln_first, ln_second, ln_average)
    return pl.pallas_call(
        functools.partial(finish_kernel, n_row, n_col),
        out_shape=tuple(jax.ShapeDtypeStruct(x.shape, jnp.float32) for x in outs),
        in_specs=[vmem] * 10,
        out_specs=tuple([vmem] * 8),
        scratch_shapes=[
            pltpu.VMEM((n, 8, 128), jnp.float32),
            pltpu.VMEM((n_col, master.shape[0], average.shape[1]), jnp.float32),
            pltpu.SemaphoreType.DMA((n,)),
            pltpu.SemaphoreType.DMA((n,)),
            pltpu.SemaphoreType.DMA((n_col,)),
            pltpu.SemaphoreType.DMA((n_col,)),
        ],
        compiler_params=pltpu.CompilerParams(collective_id=0, has_side_effects=True),
    )(gradient, ln_gradient, master, first, second, average, ln_master, ln_first, ln_second, ln_average)


def reduce_kernel(n_dp, n_col, g_ref, ln_ref, g_out, ln_out, rs_buf, ag_buf, ln_buf,
                  rs_send, rs_recv, ag_send, ag_recv, ln_send, ln_recv):
    d = lax.axis_index("dp")
    r = lax.axis_index("row")
    c = lax.axis_index("col")
    n = n_dp * n_col
    me = d * n_col + c
    quarter = g_ref.shape[0] // n_col
    depth = rs_buf.shape[2]
    width = rs_buf.shape[3]
    halves = g_ref.shape[1] // width
    barrier = pltpu.get_barrier_semaphore()

    def greet(j, carry):
        peer = lax.rem(me + j, n)
        pl.semaphore_signal(
            barrier, inc=1, device_id=(peer // n_col, r, peer % n_col), device_id_type=MESH
        )
        return carry

    lax.fori_loop(1, n, greet, 0)
    pl.semaphore_wait(barrier, n - 1)

    def piece(k, q):
        rows = pl.ds(pl.multiple_of(q * quarter + (k // halves) * depth, depth), depth)
        cols = pl.ds(pl.multiple_of((k % halves) * width, width), width)
        return g_ref.at[rows, cols]

    def rs_copy(j):
        peer = lax.rem(me + j, n)
        return pltpu.make_async_remote_copy(
            src_ref=piece(peer // n_col, peer % n_col),
            dst_ref=rs_buf.at[d, c],
            send_sem=rs_send.at[j],
            recv_sem=rs_recv.at[me],
            device_id=(peer // n_col, r, peer % n_col),
            device_id_type=MESH,
        )

    def ln_copy(j):
        peer = lax.rem(d + j, n_dp)
        return pltpu.make_async_remote_copy(
            src_ref=ln_ref,
            dst_ref=ln_buf.at[d],
            send_sem=ln_send.at[j],
            recv_sem=ln_recv.at[d],
            device_id=(peer, r, c),
            device_id_type=MESH,
        )

    def start_rs(j, carry):
        rs_copy(j).start()
        return carry

    def start_ln(j, carry):
        ln_copy(j).start()
        return carry

    lax.fori_loop(1, n, start_rs, 0)
    lax.fori_loop(1, n_dp, start_ln, 0)
    rs_buf[d, c] = piece(d, c)[...]
    ln_buf[d] = ln_ref[...]

    def wait_rs(j, carry):
        src = lax.rem(me + j, n)
        pltpu.make_async_remote_copy(
            src_ref=piece(0, 0),
            dst_ref=rs_buf.at[src // n_col, src % n_col],
            send_sem=rs_send.at[j],
            recv_sem=rs_recv.at[src],
            device_id=(src // n_col, r, src % n_col),
            device_id_type=MESH,
        ).wait_recv()
        rs_copy(j).wait_send()
        return carry

    lax.fori_loop(1, n, wait_rs, 0)
    ag_buf[d] = jnp.sum(rs_buf[...].astype(jnp.float32), axis=0)

    def ag_copy(j):
        peer = lax.rem(d + j, n_dp)
        return pltpu.make_async_remote_copy(
            src_ref=ag_buf.at[d],
            dst_ref=ag_buf.at[d],
            send_sem=ag_send.at[j],
            recv_sem=ag_recv.at[d],
            device_id=(peer, r, c),
            device_id_type=MESH,
        )

    def start_ag(j, carry):
        ag_copy(j).start()
        return carry

    lax.fori_loop(1, n_dp, start_ag, 0)

    def wait_ln(j, carry):
        src = lax.rem(d + j, n_dp)
        pltpu.make_async_remote_copy(
            src_ref=ln_ref,
            dst_ref=ln_buf.at[src],
            send_sem=ln_send.at[j],
            recv_sem=ln_recv.at[src],
            device_id=(src, r, c),
            device_id_type=MESH,
        ).wait_recv()
        ln_copy(j).wait_send()
        return carry

    lax.fori_loop(1, n_dp, wait_ln, 0)
    ln_out[...] = jnp.sum(ln_buf[...].astype(jnp.float32), axis=0)

    def wait_ag(j, carry):
        src = lax.rem(d + j, n_dp)
        pltpu.make_async_remote_copy(
            src_ref=ag_buf.at[src],
            dst_ref=ag_buf.at[src],
            send_sem=ag_send.at[j],
            recv_sem=ag_recv.at[src],
            device_id=(src, r, c),
            device_id_type=MESH,
        ).wait_recv()
        ag_copy(j).wait_send()
        return carry

    lax.fori_loop(1, n_dp, wait_ag, 0)
    for k in range(n_dp):
        for q in range(n_col):
            g_out[
                pl.ds((k // halves) * depth, depth),
                pl.ds(q * halves * width + (k % halves) * width, width),
            ] = ag_buf[k, q]


def reduce_blocks(block, ln_part):
    n_dp, n_col = lax.axis_size("dp"), lax.axis_size("col")
    rows, cols = block.shape
    quarter = rows // n_col
    width = 128
    halves = cols // width
    depth = quarter * halves // n_dp
    vmem = pl.BlockSpec(memory_space=pltpu.VMEM)
    return pl.pallas_call(
        functools.partial(reduce_kernel, n_dp, n_col),
        out_shape=(
            jax.ShapeDtypeStruct((quarter, cols * n_col), jnp.float32),
            jax.ShapeDtypeStruct(ln_part.shape, jnp.float32),
        ),
        in_specs=[vmem, vmem],
        out_specs=(vmem, vmem),
        scratch_shapes=[
            pltpu.VMEM((n_dp, n_col, depth, width), block.dtype),
            pltpu.VMEM((n_dp, n_col, depth, width), jnp.float32),
            pltpu.VMEM((n_dp,) + ln_part.shape, ln_part.dtype),
            pltpu.SemaphoreType.DMA((n_dp * n_col,)),
            pltpu.SemaphoreType.DMA((n_dp * n_col,)),
            pltpu.SemaphoreType.DMA((n_dp,)),
            pltpu.SemaphoreType.DMA((n_dp,)),
            pltpu.SemaphoreType.DMA((n_dp,)),
            pltpu.SemaphoreType.DMA((n_dp,)),
        ],
        compiler_params=pltpu.CompilerParams(collective_id=1, has_side_effects=True),
    )(block, ln_part)


def shards(
    grad_blocks,
    ln_grads,
    master,
    first_moment,
    second_moment,
    average,
    ln_master,
    ln_first,
    ln_second,
    ln_average,
):
    gradient, ln_gradient = reduce_blocks(grad_blocks[0], ln_grads[0])
    (
        average_new,
        master_new,
        first_new,
        second_new,
        ln_master_new,
        ln_first_new,
        ln_second_new,
        ln_average_new,
    ) = finish(
        gradient, ln_gradient, master, first_moment, second_moment, average,
        ln_master, ln_first, ln_second, ln_average,
    )
    return (
        average_new,
        master_new,
        first_new,
        second_new,
        ln_master_new,
        ln_first_new,
        ln_second_new,
        ln_average_new,
    )


def solution(mesh):
    placed = (
        P("dp", "row", "col"),
        P("dp", None, "col"),
        P(("row", "col"), None),
        P(("row", "col"), None),
        P(("row", "col"), None),
        P("row", "col"),
        P(None, "col"),
        P(None, "col"),
        P(None, "col"),
        P(None, "col"),
    )
    return jax.shard_map(
        shards,
        mesh=mesh,
        in_specs=placed,
        out_specs=(
            P("row", "col"),
            P(("row", "col"), None),
            P(("row", "col"), None),
            P(("row", "col"), None),
            P(None, "col"),
            P(None, "col"),
            P(None, "col"),
            P(None, "col"),
        ),
        check_vma=False,
    )
```

```python
import functools
import math

import jax
import jax.numpy as jnp
from jax import lax
from jax.experimental import pallas as pl
from jax.experimental.pallas import tpu as pltpu
from jax.sharding import PartitionSpec as P

MESH = pl.DeviceIdType.MESH

D = 1024
FF = 4096
STEP = 20


beta_one = 0.9
beta_two = 0.95
learn_rate = 0.02
decay_rate = 0.1
epsilon = 1e-08
clip_rms = 1.0
ema_keep = 0.9


def adam_step(gradient, clip_scale, first, second, master, decay_weight):
    clipped = clip_scale * gradient
    first_new = beta_one * first + (1.0 - beta_one) * clipped
    second_new = beta_two * second + (1.0 - beta_two) * clipped * clipped
    direction = (
        first_new
        / (1.0 - beta_one**STEP)
        / (jnp.sqrt(second_new / (1.0 - beta_two**STEP)) + epsilon)
    )
    master_new = master - learn_rate * (direction + decay_weight * master)
    return (master_new, first_new, second_new)


def clip_factor(norm_total):
    return jnp.minimum(1.0, clip_rms * math.sqrt(FF * D + 4 * D) / jnp.sqrt(norm_total))


def squares(gradient, ln_gradient, row_count):
    return jnp.sum(gradient * gradient) + jnp.sum(ln_gradient * ln_gradient) / row_count


def finish_kernel(n_row, n_col, g_ref, lg_ref, m_ref, f_ref, s_ref, c_out, b_out,
                  nbuf, mbuf, rbuf, n_send, n_recv, m_send, m_recv):
    d = lax.axis_index("dp")
    r = lax.axis_index("row")
    c = lax.axis_index("col")
    me = r * n_col + c
    n = n_row * n_col
    barrier = pltpu.get_barrier_semaphore()
    for j in range(1, n):
        peer = lax.rem(me + j, n)
        pl.semaphore_signal(
            barrier, inc=1, device_id=(d, peer // n_col, peer % n_col), device_id_type=MESH
        )
    pl.semaphore_wait(barrier, n - 1)
    g = g_ref[...]
    lg = lg_ref[...]
    part = jnp.sum(g * g) + jnp.sum(lg * lg) / float(n_row)
    nbuf[me] = jnp.full(nbuf.shape[1:], part, jnp.float32)

    def n_copy(j, peer, slot):
        return pltpu.make_async_remote_copy(
            src_ref=nbuf.at[slot],
            dst_ref=nbuf.at[slot],
            send_sem=n_send.at[j],
            recv_sem=n_recv.at[slot],
            device_id=(d, peer // n_col, peer % n_col),
            device_id_type=MESH,
        )

    copies = []
    for j in range(1, n):
        copy = n_copy(j, lax.rem(me + j, n), me)
        copy.start()
        copies.append(copy)
    for j in range(1, n):
        sender = lax.rem(me + n - j, n)
        n_copy(j, sender, sender).wait_recv()
    for copy in copies:
        copy.wait_send()
    norm_total = jnp.sum(nbuf[...], axis=0)[0:1, 0:1]
    clip_scale = clip_factor(norm_total)
    c_out[...] = jnp.broadcast_to(clip_scale, c_out.shape)
    master_new, _, _ = adam_step(g, clip_scale, f_ref[...], s_ref[...], m_ref[...], decay_rate)
    mbuf[c] = master_new
    width = b_out.shape[1]

    def m_copy(j, peer, slot):
        return pltpu.make_async_remote_copy(
            src_ref=mbuf.at[c, :, pl.ds(pl.multiple_of(peer * width, width), width)],
            dst_ref=rbuf.at[slot],
            send_sem=m_send.at[j],
            recv_sem=m_recv.at[slot],
            device_id=(d, r, peer),
            device_id_type=MESH,
        )

    copies = []
    for j in range(1, n_col):
        copy = m_copy(j, lax.rem(c + j, n_col), c)
        copy.start()
        copies.append(copy)
    rbuf[c] = mbuf[c, :, pl.ds(pl.multiple_of(c * width, width), width)]
    for j in range(1, n_col):
        sender = lax.rem(c + n_col - j, n_col)
        m_copy(j, sender, sender).wait_recv()
    for copy in copies:
        copy.wait_send()
    depth = rbuf.shape[1]
    for q in range(n_col):
        b_out[pl.ds(q * depth, depth), :] = rbuf[q]


def finish(gradient, ln_gradient, master, first, second, average):
    n_row, n_col = lax.axis_size("row"), lax.axis_size("col")
    n = n_row * n_col
    vmem = pl.BlockSpec(memory_space=pltpu.VMEM)
    rows, width = master.shape[0], average.shape[1]
    return pl.pallas_call(
        functools.partial(finish_kernel, n_row, n_col),
        out_shape=(
            jax.ShapeDtypeStruct((8, 128), jnp.float32),
            jax.ShapeDtypeStruct(average.shape, jnp.float32),
        ),
        in_specs=[vmem] * 5,
        out_specs=(vmem, vmem),
        scratch_shapes=[
            pltpu.VMEM((n, 8, 128), jnp.float32),
            pltpu.VMEM((n_col,) + master.shape, jnp.float32),
            pltpu.VMEM((n_col, rows, width), jnp.float32),
            pltpu.SemaphoreType.DMA((n,)),
            pltpu.SemaphoreType.DMA((n,)),
            pltpu.SemaphoreType.DMA((n_col,)),
            pltpu.SemaphoreType.DMA((n_col,)),
        ],
        compiler_params=pltpu.CompilerParams(collective_id=0, has_side_effects=True),
    )(gradient, ln_gradient, master, first, second)


def reduce_kernel(n_dp, n_col, g_ref, ln_ref, g_out, ln_out, rs_buf, ag_buf, ln_buf,
                  rs_send, rs_recv, ag_send, ag_recv, ln_send, ln_recv):
    d = lax.axis_index("dp")
    r = lax.axis_index("row")
    c = lax.axis_index("col")
    n = n_dp * n_col
    me = d * n_col + c
    quarter = g_ref.shape[0] // n_col
    depth = rs_buf.shape[2]
    width = rs_buf.shape[3]
    halves = g_ref.shape[1] // width
    barrier = pltpu.get_barrier_semaphore()

    def greet(j, carry):
        peer = lax.rem(me + j, n)
        pl.semaphore_signal(
            barrier, inc=1, device_id=(peer // n_col, r, peer % n_col), device_id_type=MESH
        )
        return carry

    lax.fori_loop(1, n, greet, 0)
    pl.semaphore_wait(barrier, n - 1)

    def piece(k, q):
        rows = pl.ds(pl.multiple_of(q * quarter + (k // halves) * depth, depth), depth)
        cols = pl.ds(pl.multiple_of((k % halves) * width, width), width)
        return g_ref.at[rows, cols]

    def rs_copy(j):
        peer = lax.rem(me + j, n)
        return pltpu.make_async_remote_copy(
            src_ref=piece(peer // n_col, peer % n_col),
            dst_ref=rs_buf.at[d, c],
            send_sem=rs_send.at[j],
            recv_sem=rs_recv.at[me],
            device_id=(peer // n_col, r, peer % n_col),
            device_id_type=MESH,
        )

    def ln_copy(j):
        peer = lax.rem(d + j, n_dp)
        return pltpu.make_async_remote_copy(
            src_ref=ln_ref,
            dst_ref=ln_buf.at[d],
            send_sem=ln_send.at[j],
            recv_sem=ln_recv.at[d],
            device_id=(peer, r, c),
            device_id_type=MESH,
        )

    def start_rs(j, carry):
        rs_copy(j).start()
        return carry

    def start_ln(j, carry):
        ln_copy(j).start()
        return carry

    lax.fori_loop(1, n, start_rs, 0)
    lax.fori_loop(1, n_dp, start_ln, 0)
    rs_buf[d, c] = piece(d, c)[...]
    ln_buf[d] = ln_ref[...]

    def wait_rs(j, carry):
        src = lax.rem(me + j, n)
        pltpu.make_async_remote_copy(
            src_ref=piece(0, 0),
            dst_ref=rs_buf.at[src // n_col, src % n_col],
            send_sem=rs_send.at[j],
            recv_sem=rs_recv.at[src],
            device_id=(src // n_col, r, src % n_col),
            device_id_type=MESH,
        ).wait_recv()
        rs_copy(j).wait_send()
        return carry

    lax.fori_loop(1, n, wait_rs, 0)
    ag_buf[d] = jnp.sum(rs_buf[...].astype(jnp.float32), axis=0)

    def ag_copy(j):
        peer = lax.rem(d + j, n_dp)
        return pltpu.make_async_remote_copy(
            src_ref=ag_buf.at[d],
            dst_ref=ag_buf.at[d],
            send_sem=ag_send.at[j],
            recv_sem=ag_recv.at[d],
            device_id=(peer, r, c),
            device_id_type=MESH,
        )

    def start_ag(j, carry):
        ag_copy(j).start()
        return carry

    lax.fori_loop(1, n_dp, start_ag, 0)

    def wait_ln(j, carry):
        src = lax.rem(d + j, n_dp)
        pltpu.make_async_remote_copy(
            src_ref=ln_ref,
            dst_ref=ln_buf.at[src],
            send_sem=ln_send.at[j],
            recv_sem=ln_recv.at[src],
            device_id=(src, r, c),
            device_id_type=MESH,
        ).wait_recv()
        ln_copy(j).wait_send()
        return carry

    lax.fori_loop(1, n_dp, wait_ln, 0)
    ln_out[...] = jnp.sum(ln_buf[...].astype(jnp.float32), axis=0)

    def wait_ag(j, carry):
        src = lax.rem(d + j, n_dp)
        pltpu.make_async_remote_copy(
            src_ref=ag_buf.at[src],
            dst_ref=ag_buf.at[src],
            send_sem=ag_send.at[j],
            recv_sem=ag_recv.at[src],
            device_id=(src, r, c),
            device_id_type=MESH,
        ).wait_recv()
        ag_copy(j).wait_send()
        return carry

    lax.fori_loop(1, n_dp, wait_ag, 0)
    for k in range(n_dp):
        for q in range(n_col):
            g_out[
                pl.ds((k // halves) * depth, depth),
                pl.ds(q * halves * width + (k % halves) * width, width),
            ] = ag_buf[k, q]


def reduce_blocks(block, ln_part):
    n_dp, n_col = lax.axis_size("dp"), lax.axis_size("col")
    rows, cols = block.shape
    quarter = rows // n_col
    width = 128
    halves = cols // width
    depth = quarter * halves // n_dp
    vmem = pl.BlockSpec(memory_space=pltpu.VMEM)
    return pl.pallas_call(
        functools.partial(reduce_kernel, n_dp, n_col),
        out_shape=(
            jax.ShapeDtypeStruct((quarter, cols * n_col), jnp.float32),
            jax.ShapeDtypeStruct(ln_part.shape, jnp.float32),
        ),
        in_specs=[vmem, vmem],
        out_specs=(vmem, vmem),
        scratch_shapes=[
            pltpu.VMEM((n_dp, n_col, depth, width), block.dtype),
            pltpu.VMEM((n_dp, n_col, depth, width), jnp.float32),
            pltpu.VMEM((n_dp,) + ln_part.shape, ln_part.dtype),
            pltpu.SemaphoreType.DMA((n_dp * n_col,)),
            pltpu.SemaphoreType.DMA((n_dp * n_col,)),
            pltpu.SemaphoreType.DMA((n_dp,)),
            pltpu.SemaphoreType.DMA((n_dp,)),
            pltpu.SemaphoreType.DMA((n_dp,)),
            pltpu.SemaphoreType.DMA((n_dp,)),
        ],
        compiler_params=pltpu.CompilerParams(collective_id=1, has_side_effects=True),
    )(block, ln_part)


def shards(
    grad_blocks,
    ln_grads,
    master,
    first_moment,
    second_moment,
    average,
    ln_master,
    ln_first,
    ln_second,
    ln_average,
):
    gradient, ln_gradient = reduce_blocks(grad_blocks[0], ln_grads[0])
    clip_tile, block_master = finish(
        gradient, ln_gradient, master, first_moment, second_moment, average
    )
    clip_scale = clip_tile[0, 0]
    master_new, first_new, second_new = adam_step(
        gradient, clip_scale, first_moment, second_moment, master, decay_rate
    )
    ln_master_new, ln_first_new, ln_second_new = adam_step(
        ln_gradient, clip_scale, ln_first, ln_second, ln_master, 0.0
    )
    ln_average_new = ema_keep * ln_average + (1.0 - ema_keep) * ln_master_new
    average_new = ema_keep * average + (1.0 - ema_keep) * block_master
    return (
        average_new,
        master_new,
        first_new,
        second_new,
        ln_master_new,
        ln_first_new,
        ln_second_new,
        ln_average_new,
    )


def solution(mesh):
    placed = (
        P("dp", "row", "col"),
        P("dp", None, "col"),
        P(("row", "col"), None),
        P(("row", "col"), None),
        P(("row", "col"), None),
        P("row", "col"),
        P(None, "col"),
        P(None, "col"),
        P(None, "col"),
        P(None, "col"),
    )
    return jax.shard_map(
        shards,
        mesh=mesh,
        in_specs=placed,
        out_specs=(
            P("row", "col"),
            P(("row", "col"), None),
            P(("row", "col"), None),
            P(("row", "col"), None),
            P(None, "col"),
            P(None, "col"),
            P(None, "col"),
            P(None, "col"),
        ),
        check_vma=False,
    )
```

```python
import functools
import math

import jax
import jax.numpy as jnp
from jax import lax
from jax.experimental import pallas as pl
from jax.experimental.pallas import tpu as pltpu
from jax.sharding import PartitionSpec as P

MESH = pl.DeviceIdType.MESH

D = 1024
FF = 4096
STEP = 20


beta_one = 0.9
beta_two = 0.95
learn_rate = 0.02
decay_rate = 0.1
epsilon = 1e-08
clip_rms = 1.0
ema_keep = 0.9


def adam_step(gradient, clip_scale, first, second, master, decay_weight):
    clipped = clip_scale * gradient
    first_new = beta_one * first + (1.0 - beta_one) * clipped
    second_new = beta_two * second + (1.0 - beta_two) * clipped * clipped
    direction = (
        first_new
        / (1.0 - beta_one**STEP)
        / (jnp.sqrt(second_new / (1.0 - beta_two**STEP)) + epsilon)
    )
    master_new = master - learn_rate * (direction + decay_weight * master)
    return (master_new, first_new, second_new)


def clip_factor(norm_total):
    return jnp.minimum(1.0, clip_rms * math.sqrt(FF * D + 4 * D) / jnp.sqrt(norm_total))


def squares(gradient, ln_gradient, row_count):
    return jnp.sum(gradient * gradient) + jnp.sum(ln_gradient * ln_gradient) / row_count


def finish_kernel(n_row, n_col, g_ref, lg_ref, m_ref, f_ref, s_ref, c_out, b_out,
                  nbuf, mbuf, rbuf, n_send, n_recv, m_send, m_recv):
    d = lax.axis_index("dp")
    r = lax.axis_index("row")
    c = lax.axis_index("col")
    me = r * n_col + c
    n = n_row * n_col
    barrier = pltpu.get_barrier_semaphore()
    for j in range(1, n):
        peer = lax.rem(me + j, n)
        pl.semaphore_signal(
            barrier, inc=1, device_id=(d, peer // n_col, peer % n_col), device_id_type=MESH
        )
    pl.semaphore_wait(barrier, n - 1)
    g = g_ref[...]
    lg = lg_ref[...]
    part = jnp.sum(g * g) + jnp.sum(lg * lg) / float(n_row)
    nbuf[me] = jnp.full(nbuf.shape[1:], part, jnp.float32)

    def n_copy(j, peer, slot):
        return pltpu.make_async_remote_copy(
            src_ref=nbuf.at[slot],
            dst_ref=nbuf.at[slot],
            send_sem=n_send.at[j],
            recv_sem=n_recv.at[slot],
            device_id=(d, peer // n_col, peer % n_col),
            device_id_type=MESH,
        )

    copies = []
    for j in range(1, n):
        copy = n_copy(j, lax.rem(me + j, n), me)
        copy.start()
        copies.append(copy)
    for j in range(1, n):
        sender = lax.rem(me + n - j, n)
        n_copy(j, sender, sender).wait_recv()
    for copy in copies:
        copy.wait_send()
    norm_total = jnp.sum(nbuf[...], axis=0)[0:1, 0:1]
    clip_scale = clip_factor(norm_total)
    c_out[...] = jnp.broadcast_to(clip_scale, c_out.shape)
    master_new, _, _ = adam_step(g, clip_scale, f_ref[...], s_ref[...], m_ref[...], decay_rate)
    mbuf[c] = master_new
    width = b_out.shape[1]

    def m_copy(j, peer, slot):
        return pltpu.make_async_remote_copy(
            src_ref=mbuf.at[c, :, pl.ds(pl.multiple_of(peer * width, width), width)],
            dst_ref=rbuf.at[slot],
            send_sem=m_send.at[j],
            recv_sem=m_recv.at[slot],
            device_id=(d, r, peer),
            device_id_type=MESH,
        )

    copies = []
    for j in range(1, n_col):
        copy = m_copy(j, lax.rem(c + j, n_col), c)
        copy.start()
        copies.append(copy)
    rbuf[c] = mbuf[c, :, pl.ds(pl.multiple_of(c * width, width), width)]
    for j in range(1, n_col):
        sender = lax.rem(c + n_col - j, n_col)
        m_copy(j, sender, sender).wait_recv()
    for copy in copies:
        copy.wait_send()
    depth = rbuf.shape[1]
    for q in range(n_col):
        b_out[pl.ds(q * depth, depth), :] = rbuf[q]


def finish(gradient, ln_gradient, master, first, second, average):
    n_row, n_col = lax.axis_size("row"), lax.axis_size("col")
    n = n_row * n_col
    vmem = pl.BlockSpec(memory_space=pltpu.VMEM)
    rows, width = master.shape[0], average.shape[1]
    return pl.pallas_call(
        functools.partial(finish_kernel, n_row, n_col),
        out_shape=(
            jax.ShapeDtypeStruct((8, 128), jnp.float32),
            jax.ShapeDtypeStruct(average.shape, jnp.float32),
        ),
        in_specs=[vmem] * 5,
        out_specs=(vmem, vmem),
        scratch_shapes=[
            pltpu.VMEM((n, 8, 128), jnp.float32),
            pltpu.VMEM((n_col,) + master.shape, jnp.float32),
            pltpu.VMEM((n_col, rows, width), jnp.float32),
            pltpu.SemaphoreType.DMA((n,)),
            pltpu.SemaphoreType.DMA((n,)),
            pltpu.SemaphoreType.DMA((n_col,)),
            pltpu.SemaphoreType.DMA((n_col,)),
        ],
        compiler_params=pltpu.CompilerParams(collective_id=0, has_side_effects=True),
    )(gradient, ln_gradient, master, first, second)


def reduce_kernel(n_dp, n_col, g_ref, ln_ref, g_out, ln_out, rs_buf, ag_buf, ln_buf,
                  rs_send, rs_recv, ag_send, ag_recv, ln_send, ln_recv):
    d = lax.axis_index("dp")
    r = lax.axis_index("row")
    c = lax.axis_index("col")
    n = n_dp * n_col
    me = d * n_col + c
    quarter = g_ref.shape[0] // n_col
    depth = rs_buf.shape[2]
    width = rs_buf.shape[3]
    halves = g_ref.shape[1] // width
    barrier = pltpu.get_barrier_semaphore()

    def greet(j, carry):
        peer = lax.rem(me + j, n)
        pl.semaphore_signal(
            barrier, inc=1, device_id=(peer // n_col, r, peer % n_col), device_id_type=MESH
        )
        return carry

    lax.fori_loop(1, n, greet, 0)
    pl.semaphore_wait(barrier, n - 1)

    def piece(k, q):
        rows = pl.ds(pl.multiple_of(q * quarter + (k // halves) * depth, depth), depth)
        cols = pl.ds(pl.multiple_of((k % halves) * width, width), width)
        return g_ref.at[rows, cols]

    def rs_copy(j):
        peer = lax.rem(me + j, n)
        return pltpu.make_async_remote_copy(
            src_ref=piece(peer // n_col, peer % n_col),
            dst_ref=rs_buf.at[d, c],
            send_sem=rs_send.at[j],
            recv_sem=rs_recv.at[me],
            device_id=(peer // n_col, r, peer % n_col),
            device_id_type=MESH,
        )

    def ln_copy(j):
        peer = lax.rem(d + j, n_dp)
        return pltpu.make_async_remote_copy(
            src_ref=ln_ref,
            dst_ref=ln_buf.at[d],
            send_sem=ln_send.at[j],
            recv_sem=ln_recv.at[d],
            device_id=(peer, r, c),
            device_id_type=MESH,
        )

    def start_rs(j, carry):
        rs_copy(j).start()
        return carry

    def start_ln(j, carry):
        ln_copy(j).start()
        return carry

    lax.fori_loop(1, n, start_rs, 0)
    lax.fori_loop(1, n_dp, start_ln, 0)
    rs_buf[d, c] = piece(d, c)[...]
    ln_buf[d] = ln_ref[...]

    def wait_rs(j, carry):
        src = lax.rem(me + j, n)
        pltpu.make_async_remote_copy(
            src_ref=piece(0, 0),
            dst_ref=rs_buf.at[src // n_col, src % n_col],
            send_sem=rs_send.at[j],
            recv_sem=rs_recv.at[src],
            device_id=(src // n_col, r, src % n_col),
            device_id_type=MESH,
        ).wait_recv()
        rs_copy(j).wait_send()
        return carry

    lax.fori_loop(1, n, wait_rs, 0)
    ag_buf[d] = jnp.sum(rs_buf[...].astype(jnp.float32), axis=0)

    def ag_copy(slot, j, peer):
        return pltpu.make_async_remote_copy(
            src_ref=ag_buf.at[slot],
            dst_ref=ag_buf.at[slot],
            send_sem=ag_send.at[j],
            recv_sem=ag_recv.at[slot],
            device_id=(peer, r, c),
            device_id_type=MESH,
        )

    def arrive(slot):
        ag_copy(slot, 0, slot).wait_recv()

    reach = 3
    n_right = n_dp // 2
    n_left = n_dp - 1 - n_right
    sends = []
    waited = set()
    for leg in range(0, n_right, reach):
        for sign, span in ((1, n_right), (-1, n_left)):
            if leg >= span:
                continue
            back = (n_dp - sign * leg) % n_dp
            slot = lax.rem(d + back, n_dp)
            if leg:
                arrive(slot)
                waited.add(back)
            for hop in range(1, min(reach, span - leg) + 1):
                peer = lax.rem(d + (n_dp + sign * hop) % n_dp, n_dp)
                copy = ag_copy(slot, len(sends), peer)
                copy.start()
                sends.append(copy)

    def wait_ln(j, carry):
        src = lax.rem(d + j, n_dp)
        pltpu.make_async_remote_copy(
            src_ref=ln_ref,
            dst_ref=ln_buf.at[src],
            send_sem=ln_send.at[j],
            recv_sem=ln_recv.at[src],
            device_id=(src, r, c),
            device_id_type=MESH,
        ).wait_recv()
        ln_copy(j).wait_send()
        return carry

    lax.fori_loop(1, n_dp, wait_ln, 0)
    ln_out[...] = jnp.sum(ln_buf[...].astype(jnp.float32), axis=0)

    for back in range(1, n_dp):
        if back not in waited:
            arrive(lax.rem(d + back, n_dp))
    for copy in sends:
        copy.wait_send()
    for k in range(n_dp):
        for q in range(n_col):
            g_out[
                pl.ds((k // halves) * depth, depth),
                pl.ds(q * halves * width + (k % halves) * width, width),
            ] = ag_buf[k, q]


def reduce_blocks(block, ln_part):
    n_dp, n_col = lax.axis_size("dp"), lax.axis_size("col")
    rows, cols = block.shape
    quarter = rows // n_col
    width = 128
    halves = cols // width
    depth = quarter * halves // n_dp
    vmem = pl.BlockSpec(memory_space=pltpu.VMEM)
    return pl.pallas_call(
        functools.partial(reduce_kernel, n_dp, n_col),
        out_shape=(
            jax.ShapeDtypeStruct((quarter, cols * n_col), jnp.float32),
            jax.ShapeDtypeStruct(ln_part.shape, jnp.float32),
        ),
        in_specs=[vmem, vmem],
        out_specs=(vmem, vmem),
        scratch_shapes=[
            pltpu.VMEM((n_dp, n_col, depth, width), block.dtype),
            pltpu.VMEM((n_dp, n_col, depth, width), jnp.float32),
            pltpu.VMEM((n_dp,) + ln_part.shape, ln_part.dtype),
            pltpu.SemaphoreType.DMA((n_dp * n_col,)),
            pltpu.SemaphoreType.DMA((n_dp * n_col,)),
            pltpu.SemaphoreType.DMA((n_dp,)),
            pltpu.SemaphoreType.DMA((n_dp,)),
            pltpu.SemaphoreType.DMA((n_dp,)),
            pltpu.SemaphoreType.DMA((n_dp,)),
        ],
        compiler_params=pltpu.CompilerParams(collective_id=1, has_side_effects=True),
    )(block, ln_part)


def shards(
    grad_blocks,
    ln_grads,
    master,
    first_moment,
    second_moment,
    average,
    ln_master,
    ln_first,
    ln_second,
    ln_average,
):
    gradient, ln_gradient = reduce_blocks(grad_blocks[0], ln_grads[0])
    clip_tile, block_master = finish(
        gradient, ln_gradient, master, first_moment, second_moment, average
    )
    clip_scale = clip_tile[0, 0]
    master_new, first_new, second_new = adam_step(
        gradient, clip_scale, first_moment, second_moment, master, decay_rate
    )
    ln_master_new, ln_first_new, ln_second_new = adam_step(
        ln_gradient, clip_scale, ln_first, ln_second, ln_master, 0.0
    )
    ln_average_new = ema_keep * ln_average + (1.0 - ema_keep) * ln_master_new
    average_new = ema_keep * average + (1.0 - ema_keep) * block_master
    return (
        average_new,
        master_new,
        first_new,
        second_new,
        ln_master_new,
        ln_first_new,
        ln_second_new,
        ln_average_new,
    )


def solution(mesh):
    placed = (
        P("dp", "row", "col"),
        P("dp", None, "col"),
        P(("row", "col"), None),
        P(("row", "col"), None),
        P(("row", "col"), None),
        P("row", "col"),
        P(None, "col"),
        P(None, "col"),
        P(None, "col"),
        P(None, "col"),
    )
    return jax.shard_map(
        shards,
        mesh=mesh,
        in_specs=placed,
        out_specs=(
            P("row", "col"),
            P(("row", "col"), None),
            P(("row", "col"), None),
            P(("row", "col"), None),
            P(None, "col"),
            P(None, "col"),
            P(None, "col"),
            P(None, "col"),
        ),
        check_vma=False,
    )
```

```python
import functools
import math

import jax
import jax.numpy as jnp
from jax import lax
from jax.experimental import pallas as pl
from jax.experimental.pallas import tpu as pltpu
from jax.sharding import PartitionSpec as P

MESH = pl.DeviceIdType.MESH

D = 1024
FF = 4096
STEP = 20


beta_one = 0.9
beta_two = 0.95
learn_rate = 0.02
decay_rate = 0.1
epsilon = 1e-08
clip_rms = 1.0
ema_keep = 0.9


def adam_step(gradient, clip_scale, first, second, master, decay_weight):
    clipped = clip_scale * gradient
    first_new = beta_one * first + (1.0 - beta_one) * clipped
    second_new = beta_two * second + (1.0 - beta_two) * clipped * clipped
    direction = (
        first_new
        / (1.0 - beta_one**STEP)
        / (jnp.sqrt(second_new / (1.0 - beta_two**STEP)) + epsilon)
    )
    master_new = master - learn_rate * (direction + decay_weight * master)
    return (master_new, first_new, second_new)


def clip_factor(norm_total):
    return jnp.minimum(1.0, clip_rms * math.sqrt(FF * D + 4 * D) / jnp.sqrt(norm_total))


def squares(gradient, ln_gradient, row_count):
    return jnp.sum(gradient * gradient) + jnp.sum(ln_gradient * ln_gradient) / row_count


def finish_part(n_row, n_col, g_ref, lg_ref, m_ref, f_ref, s_ref, c_out, b_out,
                nbuf, mbuf, rbuf, n_send, n_recv, m_send, m_recv):
    d = lax.axis_index("dp")
    r = lax.axis_index("row")
    c = lax.axis_index("col")
    me = r * n_col + c
    n = n_row * n_col
    g = g_ref[...]
    lg = lg_ref[...]
    part = jnp.sum(g * g) + jnp.sum(lg * lg) / float(n_row)
    nbuf[me] = jnp.full(nbuf.shape[1:], part, jnp.float32)

    def n_copy(j, peer, slot):
        return pltpu.make_async_remote_copy(
            src_ref=nbuf.at[slot],
            dst_ref=nbuf.at[slot],
            send_sem=n_send.at[j],
            recv_sem=n_recv.at[slot],
            device_id=(d, peer // n_col, peer % n_col),
            device_id_type=MESH,
        )

    copies = []
    for j in range(1, n):
        copy = n_copy(j, lax.rem(me + j, n), me)
        copy.start()
        copies.append(copy)
    for j in range(1, n):
        sender = lax.rem(me + n - j, n)
        n_copy(j, sender, sender).wait_recv()
    for copy in copies:
        copy.wait_send()
    norm_total = jnp.sum(nbuf[...], axis=0)[0:1, 0:1]
    clip_scale = clip_factor(norm_total)
    c_out[...] = jnp.broadcast_to(clip_scale, c_out.shape)
    master_new, _, _ = adam_step(g, clip_scale, f_ref[...], s_ref[...], m_ref[...], decay_rate)
    mbuf[c] = master_new
    width = b_out.shape[1]

    def m_copy(j, peer, slot):
        return pltpu.make_async_remote_copy(
            src_ref=mbuf.at[c, :, pl.ds(pl.multiple_of(peer * width, width), width)],
            dst_ref=rbuf.at[slot],
            send_sem=m_send.at[j],
            recv_sem=m_recv.at[slot],
            device_id=(d, r, peer),
            device_id_type=MESH,
        )

    copies = []
    for j in range(1, n_col):
        copy = m_copy(j, lax.rem(c + j, n_col), c)
        copy.start()
        copies.append(copy)
    rbuf[c] = mbuf[c, :, pl.ds(pl.multiple_of(c * width, width), width)]
    for j in range(1, n_col):
        sender = lax.rem(c + n_col - j, n_col)
        m_copy(j, sender, sender).wait_recv()
    for copy in copies:
        copy.wait_send()
    depth = rbuf.shape[1]
    for q in range(n_col):
        b_out[pl.ds(q * depth, depth), :] = rbuf[q]


def reduce_kernel(n_dp, n_row, n_col, g_ref, ln_ref, m_ref, f_ref, s_ref,
                  g_out, ln_out, c_out, b_out, rs_buf, ag_buf, ln_buf,
                  rs_send, rs_recv, ag_send, ag_recv, ln_send, ln_recv,
                  nbuf, mbuf, rbuf, n_send, n_recv, m_send, m_recv):
    d = lax.axis_index("dp")
    r = lax.axis_index("row")
    c = lax.axis_index("col")
    n = n_dp * n_col
    me = d * n_col + c
    quarter = g_ref.shape[0] // n_col
    depth = rs_buf.shape[2]
    width = rs_buf.shape[3]
    halves = g_ref.shape[1] // width
    barrier = pltpu.get_barrier_semaphore()

    def greet(j, carry):
        peer = lax.rem(me + j, n)
        pl.semaphore_signal(
            barrier, inc=1, device_id=(peer // n_col, r, peer % n_col), device_id_type=MESH
        )
        return carry

    lax.fori_loop(1, n, greet, 0)

    def greet_row(j, carry):
        peer = lax.rem(r + 1 + j // n_col, n_row)
        pl.semaphore_signal(
            barrier, inc=1, device_id=(d, peer, j % n_col), device_id_type=MESH
        )
        return carry

    lax.fori_loop(0, (n_row - 1) * n_col, greet_row, 0)
    pl.semaphore_wait(barrier, n - 1 + (n_row - 1) * n_col)

    def piece(k, q):
        rows = pl.ds(pl.multiple_of(q * quarter + (k // halves) * depth, depth), depth)
        cols = pl.ds(pl.multiple_of((k % halves) * width, width), width)
        return g_ref.at[rows, cols]

    def rs_copy(j):
        peer = lax.rem(me + j, n)
        return pltpu.make_async_remote_copy(
            src_ref=piece(peer // n_col, peer % n_col),
            dst_ref=rs_buf.at[d, c],
            send_sem=rs_send.at[j],
            recv_sem=rs_recv.at[me],
            device_id=(peer // n_col, r, peer % n_col),
            device_id_type=MESH,
        )

    def ln_copy(j):
        peer = lax.rem(d + j, n_dp)
        return pltpu.make_async_remote_copy(
            src_ref=ln_ref,
            dst_ref=ln_buf.at[d],
            send_sem=ln_send.at[j],
            recv_sem=ln_recv.at[d],
            device_id=(peer, r, c),
            device_id_type=MESH,
        )

    def start_rs(j, carry):
        rs_copy(j).start()
        return carry

    def start_ln(j, carry):
        ln_copy(j).start()
        return carry

    lax.fori_loop(1, n, start_rs, 0)
    lax.fori_loop(1, n_dp, start_ln, 0)
    rs_buf[d, c] = piece(d, c)[...]
    ln_buf[d] = ln_ref[...]

    def wait_rs(j, carry):
        src = lax.rem(me + j, n)
        pltpu.make_async_remote_copy(
            src_ref=piece(0, 0),
            dst_ref=rs_buf.at[src // n_col, src % n_col],
            send_sem=rs_send.at[j],
            recv_sem=rs_recv.at[src],
            device_id=(src // n_col, r, src % n_col),
            device_id_type=MESH,
        ).wait_recv()
        rs_copy(j).wait_send()
        return carry

    lax.fori_loop(1, n, wait_rs, 0)
    ag_buf[d] = jnp.sum(rs_buf[...].astype(jnp.float32), axis=0)

    def ag_copy(slot, j, peer):
        return pltpu.make_async_remote_copy(
            src_ref=ag_buf.at[slot],
            dst_ref=ag_buf.at[slot],
            send_sem=ag_send.at[j],
            recv_sem=ag_recv.at[slot],
            device_id=(peer, r, c),
            device_id_type=MESH,
        )

    def arrive(slot):
        ag_copy(slot, 0, slot).wait_recv()

    reach = 3
    n_right = n_dp // 2
    n_left = n_dp - 1 - n_right
    sends = []
    waited = set()
    for leg in range(0, n_right, reach):
        for sign, span in ((1, n_right), (-1, n_left)):
            if leg >= span:
                continue
            back = (n_dp - sign * leg) % n_dp
            slot = lax.rem(d + back, n_dp)
            if leg:
                arrive(slot)
                waited.add(back)
            for hop in range(1, min(reach, span - leg) + 1):
                peer = lax.rem(d + (n_dp + sign * hop) % n_dp, n_dp)
                copy = ag_copy(slot, len(sends), peer)
                copy.start()
                sends.append(copy)

    def wait_ln(j, carry):
        src = lax.rem(d + j, n_dp)
        pltpu.make_async_remote_copy(
            src_ref=ln_ref,
            dst_ref=ln_buf.at[src],
            send_sem=ln_send.at[j],
            recv_sem=ln_recv.at[src],
            device_id=(src, r, c),
            device_id_type=MESH,
        ).wait_recv()
        ln_copy(j).wait_send()
        return carry

    lax.fori_loop(1, n_dp, wait_ln, 0)
    ln_out[...] = jnp.sum(ln_buf[...].astype(jnp.float32), axis=0)

    for back in range(1, n_dp):
        if back not in waited:
            arrive(lax.rem(d + back, n_dp))
    for copy in sends:
        copy.wait_send()
    for k in range(n_dp):
        for q in range(n_col):
            g_out[
                pl.ds((k // halves) * depth, depth),
                pl.ds(q * halves * width + (k % halves) * width, width),
            ] = ag_buf[k, q]
    finish_part(n_row, n_col, g_out, ln_out, m_ref, f_ref, s_ref, c_out, b_out,
                nbuf, mbuf, rbuf, n_send, n_recv, m_send, m_recv)


def reduce_blocks(block, ln_part, master, first, second, average):
    n_dp, n_row, n_col = lax.axis_size("dp"), lax.axis_size("row"), lax.axis_size("col")
    rows, cols = block.shape
    quarter = rows // n_col
    width = 128
    halves = cols // width
    depth = quarter * halves // n_dp
    n = n_row * n_col
    vmem = pl.BlockSpec(memory_space=pltpu.VMEM)
    return pl.pallas_call(
        functools.partial(reduce_kernel, n_dp, n_row, n_col),
        out_shape=(
            jax.ShapeDtypeStruct((quarter, cols * n_col), jnp.float32),
            jax.ShapeDtypeStruct(ln_part.shape, jnp.float32),
            jax.ShapeDtypeStruct((8, 128), jnp.float32),
            jax.ShapeDtypeStruct(average.shape, jnp.float32),
        ),
        in_specs=[vmem] * 5,
        out_specs=(vmem, vmem, vmem, vmem),
        scratch_shapes=[
            pltpu.VMEM((n_dp, n_col, depth, width), block.dtype),
            pltpu.VMEM((n_dp, n_col, depth, width), jnp.float32),
            pltpu.VMEM((n_dp,) + ln_part.shape, ln_part.dtype),
            pltpu.SemaphoreType.DMA((n_dp * n_col,)),
            pltpu.SemaphoreType.DMA((n_dp * n_col,)),
            pltpu.SemaphoreType.DMA((n_dp,)),
            pltpu.SemaphoreType.DMA((n_dp,)),
            pltpu.SemaphoreType.DMA((n_dp,)),
            pltpu.SemaphoreType.DMA((n_dp,)),
            pltpu.VMEM((n, 8, 128), jnp.float32),
            pltpu.VMEM((n_col,) + master.shape, jnp.float32),
            pltpu.VMEM((n_col, master.shape[0], average.shape[1]), jnp.float32),
            pltpu.SemaphoreType.DMA((n,)),
            pltpu.SemaphoreType.DMA((n,)),
            pltpu.SemaphoreType.DMA((n_col,)),
            pltpu.SemaphoreType.DMA((n_col,)),
        ],
        compiler_params=pltpu.CompilerParams(collective_id=1, has_side_effects=True),
    )(block, ln_part, master, first, second)


def shards(
    grad_blocks,
    ln_grads,
    master,
    first_moment,
    second_moment,
    average,
    ln_master,
    ln_first,
    ln_second,
    ln_average,
):
    gradient, ln_gradient, clip_tile, block_master = reduce_blocks(
        grad_blocks[0], ln_grads[0], master, first_moment, second_moment, average
    )
    clip_scale = clip_tile[0, 0]
    master_new, first_new, second_new = adam_step(
        gradient, clip_scale, first_moment, second_moment, master, decay_rate
    )
    ln_master_new, ln_first_new, ln_second_new = adam_step(
        ln_gradient, clip_scale, ln_first, ln_second, ln_master, 0.0
    )
    ln_average_new = ema_keep * ln_average + (1.0 - ema_keep) * ln_master_new
    average_new = ema_keep * average + (1.0 - ema_keep) * block_master
    return (
        average_new,
        master_new,
        first_new,
        second_new,
        ln_master_new,
        ln_first_new,
        ln_second_new,
        ln_average_new,
    )


def solution(mesh):
    placed = (
        P("dp", "row", "col"),
        P("dp", None, "col"),
        P(("row", "col"), None),
        P(("row", "col"), None),
        P(("row", "col"), None),
        P("row", "col"),
        P(None, "col"),
        P(None, "col"),
        P(None, "col"),
        P(None, "col"),
    )
    return jax.shard_map(
        shards,
        mesh=mesh,
        in_specs=placed,
        out_specs=(
            P("row", "col"),
            P(("row", "col"), None),
            P(("row", "col"), None),
            P(("row", "col"), None),
            P(None, "col"),
            P(None, "col"),
            P(None, "col"),
            P(None, "col"),
        ),
        check_vma=False,
    )
```

```python
import functools
import math

import jax
import jax.numpy as jnp
from jax import lax
from jax.experimental import pallas as pl
from jax.experimental.pallas import tpu as pltpu
from jax.sharding import PartitionSpec as P

MESH = pl.DeviceIdType.MESH

D = 1024
FF = 4096
STEP = 20


beta_one = 0.9
beta_two = 0.95
learn_rate = 0.02
decay_rate = 0.1
epsilon = 1e-08
clip_rms = 1.0
ema_keep = 0.9


def adam_step(gradient, clip_scale, first, second, master, decay_weight):
    clipped = clip_scale * gradient
    first_new = beta_one * first + (1.0 - beta_one) * clipped
    second_new = beta_two * second + (1.0 - beta_two) * clipped * clipped
    direction = (
        first_new
        / (1.0 - beta_one**STEP)
        / (jnp.sqrt(second_new / (1.0 - beta_two**STEP)) + epsilon)
    )
    master_new = master - learn_rate * (direction + decay_weight * master)
    return (master_new, first_new, second_new)


def clip_factor(norm_total):
    return jnp.minimum(1.0, clip_rms * math.sqrt(FF * D + 4 * D) / jnp.sqrt(norm_total))


def squares(gradient, ln_gradient, row_count):
    return jnp.sum(gradient * gradient) + jnp.sum(ln_gradient * ln_gradient) / row_count


def finish_part(n_row, n_col, g_ref, lg_ref, m_ref, f_ref, s_ref, c_out, b_out,
                nbuf, mbuf, rbuf, n_send, n_recv, m_send, m_recv):
    d = lax.axis_index("dp")
    r = lax.axis_index("row")
    c = lax.axis_index("col")
    me = r * n_col + c
    n = n_row * n_col
    g = g_ref[...]
    lg = lg_ref[...]
    part = jnp.sum(g * g) + jnp.sum(lg * lg) / float(n_row)
    nbuf[me] = jnp.full(nbuf.shape[1:], part, jnp.float32)

    def n_copy(j, peer, slot):
        return pltpu.make_async_remote_copy(
            src_ref=nbuf.at[slot],
            dst_ref=nbuf.at[slot],
            send_sem=n_send.at[j],
            recv_sem=n_recv.at[slot],
            device_id=(d, peer // n_col, peer % n_col),
            device_id_type=MESH,
        )

    copies = []
    for j in range(1, n):
        copy = n_copy(j, lax.rem(me + j, n), me)
        copy.start()
        copies.append(copy)
    for j in range(1, n):
        sender = lax.rem(me + n - j, n)
        n_copy(j, sender, sender).wait_recv()
    for copy in copies:
        copy.wait_send()
    norm_total = jnp.sum(nbuf[...], axis=0)[0:1, 0:1]
    clip_scale = clip_factor(norm_total)
    c_out[...] = jnp.broadcast_to(clip_scale, c_out.shape)
    master_new, _, _ = adam_step(g, clip_scale, f_ref[...], s_ref[...], m_ref[...], decay_rate)
    mbuf[c] = master_new
    width = b_out.shape[1]

    def m_copy(j, peer, slot):
        return pltpu.make_async_remote_copy(
            src_ref=mbuf.at[c, :, pl.ds(pl.multiple_of(peer * width, width), width)],
            dst_ref=rbuf.at[slot],
            send_sem=m_send.at[j],
            recv_sem=m_recv.at[slot],
            device_id=(d, r, peer),
            device_id_type=MESH,
        )

    copies = []
    for j in range(1, n_col):
        copy = m_copy(j, lax.rem(c + j, n_col), c)
        copy.start()
        copies.append(copy)
    rbuf[c] = mbuf[c, :, pl.ds(pl.multiple_of(c * width, width), width)]
    for j in range(1, n_col):
        sender = lax.rem(c + n_col - j, n_col)
        m_copy(j, sender, sender).wait_recv()
    for copy in copies:
        copy.wait_send()
    depth = rbuf.shape[1]
    for q in range(n_col):
        b_out[pl.ds(q * depth, depth), :] = rbuf[q]


def reduce_kernel(n_dp, n_row, n_col, g_ref, ln_ref, m_ref, f_ref, s_ref,
                  g_out, ln_out, c_out, b_out, rs_buf, ag_buf, ln_buf,
                  rs_send, rs_recv, ag_send, ag_recv, ln_send, ln_recv,
                  nbuf, mbuf, rbuf, n_send, n_recv, m_send, m_recv):
    d = lax.axis_index("dp")
    r = lax.axis_index("row")
    c = lax.axis_index("col")
    n = n_dp * n_col
    me = d * n_col + c
    quarter = g_ref.shape[0] // n_col
    depth = rs_buf.shape[2]
    width = rs_buf.shape[3]
    halves = g_ref.shape[1] // width
    barrier = pltpu.get_barrier_semaphore()

    def greet(j, carry):
        peer = lax.rem(me + j, n)
        pl.semaphore_signal(
            barrier, inc=1, device_id=(peer // n_col, r, peer % n_col), device_id_type=MESH
        )
        return carry

    lax.fori_loop(1, n, greet, 0)

    def greet_row(j, carry):
        peer = lax.rem(r + 1 + j // n_col, n_row)
        pl.semaphore_signal(
            barrier, inc=1, device_id=(d, peer, j % n_col), device_id_type=MESH
        )
        return carry

    lax.fori_loop(0, (n_row - 1) * n_col, greet_row, 0)
    pl.semaphore_wait(barrier, n - 1 + (n_row - 1) * n_col)

    def piece(k, q):
        rows = pl.ds(pl.multiple_of(q * quarter + (k // halves) * depth, depth), depth)
        cols = pl.ds(pl.multiple_of((k % halves) * width, width), width)
        return g_ref.at[rows, cols]

    def rs_copy(j):
        peer = lax.rem(me + j, n)
        return pltpu.make_async_remote_copy(
            src_ref=piece(peer // n_col, peer % n_col),
            dst_ref=rs_buf.at[d, c],
            send_sem=rs_send.at[j],
            recv_sem=rs_recv.at[me],
            device_id=(peer // n_col, r, peer % n_col),
            device_id_type=MESH,
        )

    def ln_copy(j):
        peer = lax.rem(d + j, n_dp)
        return pltpu.make_async_remote_copy(
            src_ref=ln_ref,
            dst_ref=ln_buf.at[d],
            send_sem=ln_send.at[j],
            recv_sem=ln_recv.at[d],
            device_id=(peer, r, c),
            device_id_type=MESH,
        )

    def start_rs(j, carry):
        rs_copy(j).start()
        return carry

    def start_ln(j, carry):
        ln_copy(j).start()
        return carry

    lax.fori_loop(1, n, start_rs, 0)
    lax.fori_loop(1, n_dp, start_ln, 0)
    rs_buf[d, c] = piece(d, c)[...]
    ln_buf[d] = ln_ref[...]

    def wait_rs(j, carry):
        src = lax.rem(me + j, n)
        pltpu.make_async_remote_copy(
            src_ref=piece(0, 0),
            dst_ref=rs_buf.at[src // n_col, src % n_col],
            send_sem=rs_send.at[j],
            recv_sem=rs_recv.at[src],
            device_id=(src // n_col, r, src % n_col),
            device_id_type=MESH,
        ).wait_recv()
        rs_copy(j).wait_send()
        return carry

    lax.fori_loop(1, n, wait_rs, 0)
    ag_buf[d] = jnp.sum(rs_buf[...].astype(jnp.float32), axis=0)

    def ag_copy(slot, j, peer):
        return pltpu.make_async_remote_copy(
            src_ref=ag_buf.at[slot],
            dst_ref=ag_buf.at[slot],
            send_sem=ag_send.at[j],
            recv_sem=ag_recv.at[slot],
            device_id=(peer, r, c),
            device_id_type=MESH,
        )

    def arrive(slot):
        ag_copy(slot, 0, slot).wait_recv()

    reach = 3
    n_right = n_dp // 2
    n_left = n_dp - 1 - n_right
    sends = []
    waited = set()
    for leg in range(0, n_right, reach):
        for sign, span in ((1, n_right), (-1, n_left)):
            if leg >= span:
                continue
            back = (n_dp - sign * leg) % n_dp
            slot = lax.rem(d + back, n_dp)
            if leg:
                arrive(slot)
                waited.add(back)
            for hop in range(1, min(reach, span - leg) + 1):
                peer = lax.rem(d + (n_dp + sign * hop) % n_dp, n_dp)
                copy = ag_copy(slot, len(sends), peer)
                copy.start()
                sends.append(copy)

    def wait_ln(j, carry):
        src = lax.rem(d + j, n_dp)
        pltpu.make_async_remote_copy(
            src_ref=ln_ref,
            dst_ref=ln_buf.at[src],
            send_sem=ln_send.at[j],
            recv_sem=ln_recv.at[src],
            device_id=(src, r, c),
            device_id_type=MESH,
        ).wait_recv()
        ln_copy(j).wait_send()
        return carry

    lax.fori_loop(1, n_dp, wait_ln, 0)
    ln_out[...] = jnp.sum(ln_buf[...].astype(jnp.float32), axis=0)

    for back in range(1, n_dp):
        if back not in waited:
            arrive(lax.rem(d + back, n_dp))
    for copy in sends:
        copy.wait_send()
    for k in range(n_dp):
        for q in range(n_col):
            g_out[
                pl.ds((k // halves) * depth, depth),
                pl.ds(q * halves * width + (k % halves) * width, width),
            ] = ag_buf[k, q]
    finish_part(n_row, n_col, g_out, ln_out, m_ref, f_ref, s_ref, c_out, b_out,
                nbuf, mbuf, rbuf, n_send, n_recv, m_send, m_recv)


def reduce_blocks(block, ln_part, master, first, second, average):
    n_dp, n_row, n_col = lax.axis_size("dp"), lax.axis_size("row"), lax.axis_size("col")
    rows, cols = block.shape
    quarter = rows // n_col
    width = 128
    halves = cols // width
    depth = quarter * halves // n_dp
    n = n_row * n_col
    vmem = pl.BlockSpec(memory_space=pltpu.VMEM)
    return pl.pallas_call(
        functools.partial(reduce_kernel, n_dp, n_row, n_col),
        out_shape=(
            jax.ShapeDtypeStruct((quarter, cols * n_col), jnp.float32),
            jax.ShapeDtypeStruct(ln_part.shape, jnp.float32),
            jax.ShapeDtypeStruct((8, 128), jnp.float32),
            jax.ShapeDtypeStruct(average.shape, jnp.float32),
        ),
        in_specs=[vmem] * 5,
        out_specs=(vmem, vmem, vmem, vmem),
        scratch_shapes=[
            pltpu.VMEM((n_dp, n_col, depth, width), block.dtype),
            pltpu.VMEM((n_dp, n_col, depth, width), jnp.float32),
            pltpu.VMEM((n_dp,) + ln_part.shape, ln_part.dtype),
            pltpu.SemaphoreType.DMA((n_dp * n_col,)),
            pltpu.SemaphoreType.DMA((n_dp * n_col,)),
            pltpu.SemaphoreType.DMA((n_dp,)),
            pltpu.SemaphoreType.DMA((n_dp,)),
            pltpu.SemaphoreType.DMA((n_dp,)),
            pltpu.SemaphoreType.DMA((n_dp,)),
            pltpu.VMEM((n, 8, 128), jnp.float32),
            pltpu.VMEM((n_col,) + master.shape, jnp.float32),
            pltpu.VMEM((n_col, master.shape[0], average.shape[1]), jnp.float32),
            pltpu.SemaphoreType.DMA((n,)),
            pltpu.SemaphoreType.DMA((n,)),
            pltpu.SemaphoreType.DMA((n_col,)),
            pltpu.SemaphoreType.DMA((n_col,)),
        ],
        compiler_params=pltpu.CompilerParams(collective_id=1, has_side_effects=True),
    )(block, ln_part, master, first, second)


def apply_kernel(c_ref, g_ref, m_ref, f_ref, s_ref, a_ref, b_ref, lg_ref, lm_ref, lf_ref, ls_ref,
                 la_ref, a_out, m_out, f_out, s_out, lm_out, lf_out, ls_out, la_out,
                 flat, block, small, sems):
    clip_scale = c_ref[0:1, 0:1]
    master_new, first_new, second_new = adam_step(
        g_ref[...], clip_scale, f_ref[...], s_ref[...], m_ref[...], decay_rate
    )
    flat[0] = master_new
    flat[1] = first_new
    flat[2] = second_new
    block[...] = ema_keep * a_ref[...] + (1.0 - ema_keep) * b_ref[...]
    ln_master_new, ln_first_new, ln_second_new = adam_step(
        lg_ref[...], clip_scale, lf_ref[...], ls_ref[...], lm_ref[...], 0.0
    )
    small[0] = ln_master_new
    small[1] = ln_first_new
    small[2] = ln_second_new
    small[3] = ema_keep * la_ref[...] + (1.0 - ema_keep) * ln_master_new
    copies = [
        pltpu.make_async_copy(flat.at[0], m_out, sems.at[0]),
        pltpu.make_async_copy(flat.at[1], f_out, sems.at[1]),
        pltpu.make_async_copy(flat.at[2], s_out, sems.at[2]),
        pltpu.make_async_copy(block, a_out, sems.at[3]),
        pltpu.make_async_copy(small.at[0], lm_out, sems.at[4]),
        pltpu.make_async_copy(small.at[1], lf_out, sems.at[5]),
        pltpu.make_async_copy(small.at[2], ls_out, sems.at[6]),
        pltpu.make_async_copy(small.at[3], la_out, sems.at[7]),
    ]
    for copy in copies:
        copy.start()
    for copy in copies:
        copy.wait()


def apply_update(clip_tile, gradient, master, first, second, average, block_master,
                 ln_gradient, ln_master, ln_first, ln_second, ln_average):
    vmem = pl.BlockSpec(memory_space=pltpu.VMEM)
    anywhere = pl.BlockSpec(memory_space=pl.ANY)
    outs = (average, master, first, second, ln_master, ln_first, ln_second, ln_average)
    return pl.pallas_call(
        apply_kernel,
        out_shape=tuple(jax.ShapeDtypeStruct(x.shape, jnp.float32) for x in outs),
        in_specs=[vmem] * 12,
        out_specs=tuple([anywhere] * 8),
        scratch_shapes=[
            pltpu.VMEM((3,) + master.shape, jnp.float32),
            pltpu.VMEM(average.shape, jnp.float32),
            pltpu.VMEM((4,) + ln_master.shape, jnp.float32),
            pltpu.SemaphoreType.DMA((8,)),
        ],
    )(clip_tile, gradient, master, first, second, average, block_master,
      ln_gradient, ln_master, ln_first, ln_second, ln_average)


def shards(
    grad_blocks,
    ln_grads,
    master,
    first_moment,
    second_moment,
    average,
    ln_master,
    ln_first,
    ln_second,
    ln_average,
):
    gradient, ln_gradient, clip_tile, block_master = reduce_blocks(
        grad_blocks[0], ln_grads[0], master, first_moment, second_moment, average
    )
    (
        average_new,
        master_new,
        first_new,
        second_new,
        ln_master_new,
        ln_first_new,
        ln_second_new,
        ln_average_new,
    ) = apply_update(
        clip_tile, gradient, master, first_moment, second_moment, average, block_master,
        ln_gradient, ln_master, ln_first, ln_second, ln_average,
    )
    return (
        average_new,
        master_new,
        first_new,
        second_new,
        ln_master_new,
        ln_first_new,
        ln_second_new,
        ln_average_new,
    )


def solution(mesh):
    placed = (
        P("dp", "row", "col"),
        P("dp", None, "col"),
        P(("row", "col"), None),
        P(("row", "col"), None),
        P(("row", "col"), None),
        P("row", "col"),
        P(None, "col"),
        P(None, "col"),
        P(None, "col"),
        P(None, "col"),
    )
    return jax.shard_map(
        shards,
        mesh=mesh,
        in_specs=placed,
        out_specs=(
            P("row", "col"),
            P(("row", "col"), None),
            P(("row", "col"), None),
            P(("row", "col"), None),
            P(None, "col"),
            P(None, "col"),
            P(None, "col"),
            P(None, "col"),
        ),
        check_vma=False,
    )
```

```python
import functools
import math

import jax
import jax.numpy as jnp
from jax import lax
from jax.experimental import pallas as pl
from jax.experimental.pallas import tpu as pltpu
from jax.sharding import PartitionSpec as P

MESH = pl.DeviceIdType.MESH

D = 1024
FF = 4096
STEP = 20


beta_one = 0.9
beta_two = 0.95
learn_rate = 0.02
decay_rate = 0.1
epsilon = 1e-08
clip_rms = 1.0
ema_keep = 0.9


def adam_step(gradient, clip_scale, first, second, master, decay_weight):
    clipped = clip_scale * gradient
    first_new = beta_one * first + (1.0 - beta_one) * clipped
    second_new = beta_two * second + (1.0 - beta_two) * clipped * clipped
    direction = (
        first_new
        / (1.0 - beta_one**STEP)
        / (jnp.sqrt(second_new / (1.0 - beta_two**STEP)) + epsilon)
    )
    master_new = master - learn_rate * (direction + decay_weight * master)
    return (master_new, first_new, second_new)


def clip_factor(norm_total):
    return jnp.minimum(1.0, clip_rms * math.sqrt(FF * D + 4 * D) / jnp.sqrt(norm_total))


def squares(gradient, ln_gradient, row_count):
    return jnp.sum(gradient * gradient) + jnp.sum(ln_gradient * ln_gradient) / row_count


def finish_part(n_col, g_ref, m_ref, f_ref, s_ref, c_out, b_out, norm_total,
                mbuf, rbuf, m_send, m_recv):
    d = lax.axis_index("dp")
    r = lax.axis_index("row")
    c = lax.axis_index("col")
    g = g_ref[...]
    clip_scale = clip_factor(norm_total)
    c_out[...] = jnp.broadcast_to(clip_scale, c_out.shape)
    master_new, _, _ = adam_step(g, clip_scale, f_ref[...], s_ref[...], m_ref[...], decay_rate)
    mbuf[c] = master_new
    width = b_out.shape[1]

    def m_copy(j, peer, slot):
        return pltpu.make_async_remote_copy(
            src_ref=mbuf.at[c, :, pl.ds(pl.multiple_of(peer * width, width), width)],
            dst_ref=rbuf.at[slot],
            send_sem=m_send.at[j],
            recv_sem=m_recv.at[slot],
            device_id=(d, r, peer),
            device_id_type=MESH,
        )

    copies = []
    for j in range(1, n_col):
        copy = m_copy(j, lax.rem(c + j, n_col), c)
        copy.start()
        copies.append(copy)
    rbuf[c] = mbuf[c, :, pl.ds(pl.multiple_of(c * width, width), width)]
    for j in range(1, n_col):
        sender = lax.rem(c + n_col - j, n_col)
        m_copy(j, sender, sender).wait_recv()
    for copy in copies:
        copy.wait_send()
    depth = rbuf.shape[1]
    for q in range(n_col):
        b_out[pl.ds(q * depth, depth), :] = rbuf[q]


def reduce_kernel(n_dp, n_row, n_col, g_ref, ln_ref, m_ref, f_ref, s_ref,
                  g_out, ln_out, c_out, b_out, rs_buf, ag_buf, ln_buf,
                  rs_send, rs_recv, ag_send, ag_recv, ln_send, ln_recv,
                  nbuf, mbuf, rbuf, n_send, n_recv, m_send, m_recv, pbuf, p_send, p_recv):
    d = lax.axis_index("dp")
    r = lax.axis_index("row")
    c = lax.axis_index("col")
    n = n_dp * n_col
    me = d * n_col + c
    quarter = g_ref.shape[0] // n_col
    depth = rs_buf.shape[2]
    width = rs_buf.shape[3]
    halves = g_ref.shape[1] // width
    barrier = pltpu.get_barrier_semaphore()

    def greet(j, carry):
        peer = lax.rem(me + j, n)
        pl.semaphore_signal(
            barrier, inc=1, device_id=(peer // n_col, r, peer % n_col), device_id_type=MESH
        )
        return carry

    lax.fori_loop(1, n, greet, 0)

    def greet_row(j, carry):
        peer = lax.rem(r + 1 + j // n_col, n_row)
        pl.semaphore_signal(
            barrier, inc=1, device_id=(d, peer, j % n_col), device_id_type=MESH
        )
        return carry

    lax.fori_loop(0, (n_row - 1) * n_col, greet_row, 0)
    pl.semaphore_wait(barrier, n - 1 + (n_row - 1) * n_col)

    def piece(k, q):
        rows = pl.ds(pl.multiple_of(q * quarter + (k // halves) * depth, depth), depth)
        cols = pl.ds(pl.multiple_of((k % halves) * width, width), width)
        return g_ref.at[rows, cols]

    def rs_copy(j):
        peer = lax.rem(me + j, n)
        return pltpu.make_async_remote_copy(
            src_ref=piece(peer // n_col, peer % n_col),
            dst_ref=rs_buf.at[d, c],
            send_sem=rs_send.at[j],
            recv_sem=rs_recv.at[me],
            device_id=(peer // n_col, r, peer % n_col),
            device_id_type=MESH,
        )

    def ln_copy(j):
        peer = lax.rem(d + j, n_dp)
        return pltpu.make_async_remote_copy(
            src_ref=ln_ref,
            dst_ref=ln_buf.at[d],
            send_sem=ln_send.at[j],
            recv_sem=ln_recv.at[d],
            device_id=(peer, r, c),
            device_id_type=MESH,
        )

    def start_rs(j, carry):
        rs_copy(j).start()
        return carry

    def start_ln(j, carry):
        ln_copy(j).start()
        return carry

    lax.fori_loop(1, n, start_rs, 0)
    lax.fori_loop(1, n_dp, start_ln, 0)
    rs_buf[d, c] = piece(d, c)[...]
    ln_buf[d] = ln_ref[...]

    def wait_rs(j, carry):
        src = lax.rem(me + j, n)
        pltpu.make_async_remote_copy(
            src_ref=piece(0, 0),
            dst_ref=rs_buf.at[src // n_col, src % n_col],
            send_sem=rs_send.at[j],
            recv_sem=rs_recv.at[src],
            device_id=(src // n_col, r, src % n_col),
            device_id_type=MESH,
        ).wait_recv()
        rs_copy(j).wait_send()
        return carry

    lax.fori_loop(1, n, wait_rs, 0)
    def wait_ln(j, carry):
        src = lax.rem(d + j, n_dp)
        pltpu.make_async_remote_copy(
            src_ref=ln_ref,
            dst_ref=ln_buf.at[src],
            send_sem=ln_send.at[j],
            recv_sem=ln_recv.at[src],
            device_id=(src, r, c),
            device_id_type=MESH,
        ).wait_recv()
        ln_copy(j).wait_send()
        return carry

    lax.fori_loop(1, n_dp, wait_ln, 0)
    ln_out[...] = jnp.sum(ln_buf[...].astype(jnp.float32), axis=0)

    ag_buf[d] = jnp.sum(rs_buf[...].astype(jnp.float32), axis=0)

    def ag_copy(slot, j, peer):
        return pltpu.make_async_remote_copy(
            src_ref=ag_buf.at[slot],
            dst_ref=ag_buf.at[slot],
            send_sem=ag_send.at[j],
            recv_sem=ag_recv.at[slot],
            device_id=(peer, r, c),
            device_id_type=MESH,
        )

    def arrive(slot):
        ag_copy(slot, 0, slot).wait_recv()

    n_rc = n_row * n_col
    me_rc = r * n_col + c

    def n_copy(j, peer, slot):
        return pltpu.make_async_remote_copy(
            src_ref=nbuf.at[slot],
            dst_ref=nbuf.at[slot],
            send_sem=n_send.at[j],
            recv_sem=n_recv.at[slot],
            device_id=(d, peer // n_col, peer % n_col),
            device_id_type=MESH,
        )

    def p_copy(j, peer, slot):
        return pltpu.make_async_remote_copy(
            src_ref=pbuf.at[slot],
            dst_ref=pbuf.at[slot],
            send_sem=p_send.at[j],
            recv_sem=p_recv.at[slot],
            device_id=(peer, r, c),
            device_id_type=MESH,
        )

    reach = 3
    n_right = n_dp // 2
    n_left = n_dp - 1 - n_right
    sends = []
    waited = set()
    n_copies = []
    for leg in range(0, n_right, reach):
        for sign, span in ((1, n_right), (-1, n_left)):
            if leg >= span:
                continue
            back = (n_dp - sign * leg) % n_dp
            slot = lax.rem(d + back, n_dp)
            if leg:
                arrive(slot)
                waited.add(back)
            for hop in range(1, min(reach, span - leg) + 1):
                peer = lax.rem(d + (n_dp + sign * hop) % n_dp, n_dp)
                copy = ag_copy(slot, len(sends), peer)
                copy.start()
                sends.append(copy)
        if leg == 0:
            lg = ln_out[...]
            own = ag_buf[d]
            part = jnp.sum(own * own) + (d == 0).astype(jnp.float32) * (
                jnp.sum(lg * lg) / float(n_row)
            )
            nbuf[me_rc] = jnp.full(nbuf.shape[1:], part, jnp.float32)
            for j in range(1, n_rc):
                copy = n_copy(j, lax.rem(me_rc + j, n_rc), me_rc)
                copy.start()
                n_copies.append(copy)

    for j in range(1, n_rc):
        sender = lax.rem(me_rc + n_rc - j, n_rc)
        n_copy(j, sender, sender).wait_recv()
    for copy in n_copies:
        copy.wait_send()
    pbuf[d] = jnp.sum(nbuf[...], axis=0)
    p_copies = []
    for j in range(1, n_dp):
        copy = p_copy(j, lax.rem(d + j, n_dp), d)
        copy.start()
        p_copies.append(copy)
    for back in range(1, n_dp):
        if back not in waited:
            arrive(lax.rem(d + back, n_dp))
    for copy in sends:
        copy.wait_send()
    for j in range(1, n_dp):
        sender = lax.rem(d + n_dp - j, n_dp)
        p_copy(j, sender, sender).wait_recv()
    for copy in p_copies:
        copy.wait_send()
    norm_total = jnp.sum(pbuf[...], axis=0)[0:1, 0:1]
    for k in range(n_dp):
        for q in range(n_col):
            g_out[
                pl.ds((k // halves) * depth, depth),
                pl.ds(q * halves * width + (k % halves) * width, width),
            ] = ag_buf[k, q]
    finish_part(n_col, g_out, m_ref, f_ref, s_ref, c_out, b_out, norm_total,
                mbuf, rbuf, m_send, m_recv)


def reduce_blocks(block, ln_part, master, first, second, average):
    n_dp, n_row, n_col = lax.axis_size("dp"), lax.axis_size("row"), lax.axis_size("col")
    rows, cols = block.shape
    quarter = rows // n_col
    width = 128
    halves = cols // width
    depth = quarter * halves // n_dp
    n = n_row * n_col
    vmem = pl.BlockSpec(memory_space=pltpu.VMEM)
    return pl.pallas_call(
        functools.partial(reduce_kernel, n_dp, n_row, n_col),
        out_shape=(
            jax.ShapeDtypeStruct((quarter, cols * n_col), jnp.float32),
            jax.ShapeDtypeStruct(ln_part.shape, jnp.float32),
            jax.ShapeDtypeStruct((8, 128), jnp.float32),
            jax.ShapeDtypeStruct(average.shape, jnp.float32),
        ),
        in_specs=[vmem] * 5,
        out_specs=(vmem, vmem, vmem, vmem),
        scratch_shapes=[
            pltpu.VMEM((n_dp, n_col, depth, width), block.dtype),
            pltpu.VMEM((n_dp, n_col, depth, width), jnp.float32),
            pltpu.VMEM((n_dp,) + ln_part.shape, ln_part.dtype),
            pltpu.SemaphoreType.DMA((n_dp * n_col,)),
            pltpu.SemaphoreType.DMA((n_dp * n_col,)),
            pltpu.SemaphoreType.DMA((n_dp,)),
            pltpu.SemaphoreType.DMA((n_dp,)),
            pltpu.SemaphoreType.DMA((n_dp,)),
            pltpu.SemaphoreType.DMA((n_dp,)),
            pltpu.VMEM((n, 8, 128), jnp.float32),
            pltpu.VMEM((n_col,) + master.shape, jnp.float32),
            pltpu.VMEM((n_col, master.shape[0], average.shape[1]), jnp.float32),
            pltpu.SemaphoreType.DMA((n,)),
            pltpu.SemaphoreType.DMA((n,)),
            pltpu.SemaphoreType.DMA((n_col,)),
            pltpu.SemaphoreType.DMA((n_col,)),
            pltpu.VMEM((n_dp, 8, 128), jnp.float32),
            pltpu.SemaphoreType.DMA((n_dp,)),
            pltpu.SemaphoreType.DMA((n_dp,)),
        ],
        compiler_params=pltpu.CompilerParams(collective_id=1, has_side_effects=True),
    )(block, ln_part, master, first, second)


def apply_kernel(c_ref, g_ref, m_ref, f_ref, s_ref, a_ref, b_ref, lg_ref, lm_ref, lf_ref, ls_ref,
                 la_ref, a_out, m_out, f_out, s_out, lm_out, lf_out, ls_out, la_out,
                 flat, block, small, sems):
    clip_scale = c_ref[0:1, 0:1]
    master_new, first_new, second_new = adam_step(
        g_ref[...], clip_scale, f_ref[...], s_ref[...], m_ref[...], decay_rate
    )
    flat[0] = master_new
    flat[1] = first_new
    flat[2] = second_new
    block[...] = ema_keep * a_ref[...] + (1.0 - ema_keep) * b_ref[...]
    ln_master_new, ln_first_new, ln_second_new = adam_step(
        lg_ref[...], clip_scale, lf_ref[...], ls_ref[...], lm_ref[...], 0.0
    )
    small[0] = ln_master_new
    small[1] = ln_first_new
    small[2] = ln_second_new
    small[3] = ema_keep * la_ref[...] + (1.0 - ema_keep) * ln_master_new
    copies = [
        pltpu.make_async_copy(flat.at[0], m_out, sems.at[0]),
        pltpu.make_async_copy(flat.at[1], f_out, sems.at[1]),
        pltpu.make_async_copy(flat.at[2], s_out, sems.at[2]),
        pltpu.make_async_copy(block, a_out, sems.at[3]),
        pltpu.make_async_copy(small.at[0], lm_out, sems.at[4]),
        pltpu.make_async_copy(small.at[1], lf_out, sems.at[5]),
        pltpu.make_async_copy(small.at[2], ls_out, sems.at[6]),
        pltpu.make_async_copy(small.at[3], la_out, sems.at[7]),
    ]
    for copy in copies:
        copy.start()
    for copy in copies:
        copy.wait()


def apply_update(clip_tile, gradient, master, first, second, average, block_master,
                 ln_gradient, ln_master, ln_first, ln_second, ln_average):
    vmem = pl.BlockSpec(memory_space=pltpu.VMEM)
    anywhere = pl.BlockSpec(memory_space=pl.ANY)
    outs = (average, master, first, second, ln_master, ln_first, ln_second, ln_average)
    return pl.pallas_call(
        apply_kernel,
        out_shape=tuple(jax.ShapeDtypeStruct(x.shape, jnp.float32) for x in outs),
        in_specs=[vmem] * 12,
        out_specs=tuple([anywhere] * 8),
        scratch_shapes=[
            pltpu.VMEM((3,) + master.shape, jnp.float32),
            pltpu.VMEM(average.shape, jnp.float32),
            pltpu.VMEM((4,) + ln_master.shape, jnp.float32),
            pltpu.SemaphoreType.DMA((8,)),
        ],
    )(clip_tile, gradient, master, first, second, average, block_master,
      ln_gradient, ln_master, ln_first, ln_second, ln_average)


def shards(
    grad_blocks,
    ln_grads,
    master,
    first_moment,
    second_moment,
    average,
    ln_master,
    ln_first,
    ln_second,
    ln_average,
):
    gradient, ln_gradient, clip_tile, block_master = reduce_blocks(
        grad_blocks[0], ln_grads[0], master, first_moment, second_moment, average
    )
    (
        average_new,
        master_new,
        first_new,
        second_new,
        ln_master_new,
        ln_first_new,
        ln_second_new,
        ln_average_new,
    ) = apply_update(
        clip_tile, gradient, master, first_moment, second_moment, average, block_master,
        ln_gradient, ln_master, ln_first, ln_second, ln_average,
    )
    return (
        average_new,
        master_new,
        first_new,
        second_new,
        ln_master_new,
        ln_first_new,
        ln_second_new,
        ln_average_new,
    )


def solution(mesh):
    placed = (
        P("dp", "row", "col"),
        P("dp", None, "col"),
        P(("row", "col"), None),
        P(("row", "col"), None),
        P(("row", "col"), None),
        P("row", "col"),
        P(None, "col"),
        P(None, "col"),
        P(None, "col"),
        P(None, "col"),
    )
    return jax.shard_map(
        shards,
        mesh=mesh,
        in_specs=placed,
        out_specs=(
            P("row", "col"),
            P(("row", "col"), None),
            P(("row", "col"), None),
            P(("row", "col"), None),
            P(None, "col"),
            P(None, "col"),
            P(None, "col"),
            P(None, "col"),
        ),
        check_vma=False,
    )
```

```python
import functools
import math

import jax
import jax.numpy as jnp
from jax import lax
from jax.experimental import pallas as pl
from jax.experimental.pallas import tpu as pltpu
from jax.sharding import PartitionSpec as P

MESH = pl.DeviceIdType.MESH

D = 1024
FF = 4096
STEP = 20


beta_one = 0.9
beta_two = 0.95
learn_rate = 0.02
decay_rate = 0.1
epsilon = 1e-08
clip_rms = 1.0
ema_keep = 0.9


def adam_step(gradient, clip_scale, first, second, master, decay_weight):
    clipped = clip_scale * gradient
    first_new = beta_one * first + (1.0 - beta_one) * clipped
    second_new = beta_two * second + (1.0 - beta_two) * clipped * clipped
    direction = (
        first_new
        / (1.0 - beta_one**STEP)
        / (jnp.sqrt(second_new / (1.0 - beta_two**STEP)) + epsilon)
    )
    master_new = master - learn_rate * (direction + decay_weight * master)
    return (master_new, first_new, second_new)


def clip_factor(norm_total):
    return jnp.minimum(1.0, clip_rms * math.sqrt(FF * D + 4 * D) / jnp.sqrt(norm_total))


def squares(gradient, ln_gradient, row_count):
    return jnp.sum(gradient * gradient) + jnp.sum(ln_gradient * ln_gradient) / row_count


def finish_part(n_col, g_ref, m_ref, f_ref, s_ref, c_out, b_out, norm_total,
                mbuf, rbuf, m_send, m_recv):
    d = lax.axis_index("dp")
    r = lax.axis_index("row")
    c = lax.axis_index("col")
    g = g_ref[...]
    clip_scale = clip_factor(norm_total)
    c_out[...] = jnp.broadcast_to(clip_scale, c_out.shape)
    master_new, _, _ = adam_step(g, clip_scale, f_ref[...], s_ref[...], m_ref[...], decay_rate)
    mbuf[c] = master_new
    width = b_out.shape[1]

    def m_copy(j, peer, slot):
        return pltpu.make_async_remote_copy(
            src_ref=mbuf.at[c, :, pl.ds(pl.multiple_of(peer * width, width), width)],
            dst_ref=rbuf.at[slot],
            send_sem=m_send.at[j],
            recv_sem=m_recv.at[slot],
            device_id=(d, r, peer),
            device_id_type=MESH,
        )

    copies = []
    for j in range(1, n_col):
        copy = m_copy(j, lax.rem(c + j, n_col), c)
        copy.start()
        copies.append(copy)
    rbuf[c] = mbuf[c, :, pl.ds(pl.multiple_of(c * width, width), width)]
    for j in range(1, n_col):
        sender = lax.rem(c + n_col - j, n_col)
        m_copy(j, sender, sender).wait_recv()
    for copy in copies:
        copy.wait_send()
    depth = rbuf.shape[1]
    for q in range(n_col):
        b_out[pl.ds(q * depth, depth), :] = rbuf[q]


def reduce_kernel(n_dp, n_row, n_col, g_ref, ln_ref, m_ref, f_ref, s_ref,
                  g_out, ln_out, c_out, b_out, rs_buf, ag_buf, ln_buf,
                  rs_send, rs_recv, ag_send, ag_recv, ln_send, ln_recv,
                  nbuf, mbuf, rbuf, n_send, n_recv, m_send, m_recv, pbuf, p_send, p_recv):
    d = lax.axis_index("dp")
    r = lax.axis_index("row")
    c = lax.axis_index("col")
    n = n_dp * n_col
    me = d * n_col + c
    quarter = g_ref.shape[0] // n_col
    depth = rs_buf.shape[2]
    width = rs_buf.shape[3]
    halves = g_ref.shape[1] // width
    barrier = pltpu.get_barrier_semaphore()

    def greet(j, carry):
        peer = lax.rem(me + j, n)
        pl.semaphore_signal(
            barrier, inc=1, device_id=(peer // n_col, r, peer % n_col), device_id_type=MESH
        )
        return carry

    lax.fori_loop(1, n, greet, 0)

    def greet_row(j, carry):
        peer = lax.rem(r + 1 + j // n_col, n_row)
        pl.semaphore_signal(
            barrier, inc=1, device_id=(d, peer, j % n_col), device_id_type=MESH
        )
        return carry

    lax.fori_loop(0, (n_row - 1) * n_col, greet_row, 0)
    pl.semaphore_wait(barrier, n - 1 + (n_row - 1) * n_col)

    def piece(k, q):
        rows = pl.ds(pl.multiple_of(q * quarter + (k // halves) * depth, depth), depth)
        cols = pl.ds(pl.multiple_of((k % halves) * width, width), width)
        return g_ref.at[rows, cols]

    def rs_copy(j):
        peer = lax.rem(me + j, n)
        return pltpu.make_async_remote_copy(
            src_ref=piece(peer // n_col, peer % n_col),
            dst_ref=rs_buf.at[d, c],
            send_sem=rs_send.at[j],
            recv_sem=rs_recv.at[me],
            device_id=(peer // n_col, r, peer % n_col),
            device_id_type=MESH,
        )

    def ln_copy(j):
        peer = lax.rem(d + j, n_dp)
        return pltpu.make_async_remote_copy(
            src_ref=ln_ref,
            dst_ref=ln_buf.at[d],
            send_sem=ln_send.at[j],
            recv_sem=ln_recv.at[d],
            device_id=(peer, r, c),
            device_id_type=MESH,
        )

    def start_rs(j, carry):
        rs_copy(j).start()
        return carry

    def start_ln(j, carry):
        ln_copy(j).start()
        return carry

    lax.fori_loop(1, n, start_rs, 0)
    lax.fori_loop(1, n_dp, start_ln, 0)
    rs_buf[d, c] = piece(d, c)[...]
    ln_buf[d] = ln_ref[...]

    def wait_rs(j, carry):
        src = lax.rem(me + j, n)
        pltpu.make_async_remote_copy(
            src_ref=piece(0, 0),
            dst_ref=rs_buf.at[src // n_col, src % n_col],
            send_sem=rs_send.at[j],
            recv_sem=rs_recv.at[src],
            device_id=(src // n_col, r, src % n_col),
            device_id_type=MESH,
        ).wait_recv()
        rs_copy(j).wait_send()
        return carry

    lax.fori_loop(1, n, wait_rs, 0)
    def wait_ln(j, carry):
        src = lax.rem(d + j, n_dp)
        pltpu.make_async_remote_copy(
            src_ref=ln_ref,
            dst_ref=ln_buf.at[src],
            send_sem=ln_send.at[j],
            recv_sem=ln_recv.at[src],
            device_id=(src, r, c),
            device_id_type=MESH,
        ).wait_recv()
        ln_copy(j).wait_send()
        return carry

    lax.fori_loop(1, n_dp, wait_ln, 0)
    ln_out[...] = jnp.sum(ln_buf[...].astype(jnp.float32), axis=0)

    ag_buf[d] = jnp.sum(rs_buf[...].astype(jnp.float32), axis=0)

    def ag_copy(slot, j, peer):
        return pltpu.make_async_remote_copy(
            src_ref=ag_buf.at[slot],
            dst_ref=ag_buf.at[slot],
            send_sem=ag_send.at[j],
            recv_sem=ag_recv.at[slot],
            device_id=(peer, r, c),
            device_id_type=MESH,
        )

    def arrive(slot):
        ag_copy(slot, 0, slot).wait_recv()

    n_rc = n_row * n_col
    me_rc = r * n_col + c

    def n_copy(j, peer, slot):
        return pltpu.make_async_remote_copy(
            src_ref=nbuf.at[slot],
            dst_ref=nbuf.at[slot],
            send_sem=n_send.at[j],
            recv_sem=n_recv.at[slot],
            device_id=(d, peer // n_col, peer % n_col),
            device_id_type=MESH,
        )

    def p_copy(j, peer, slot):
        return pltpu.make_async_remote_copy(
            src_ref=pbuf.at[slot],
            dst_ref=pbuf.at[slot],
            send_sem=p_send.at[j],
            recv_sem=p_recv.at[slot],
            device_id=(peer, r, c),
            device_id_type=MESH,
        )

    reach = 4
    n_right = n_dp // 2
    n_left = n_dp - 1 - n_right
    sends = []
    waited = set()
    n_copies = []
    for leg in range(0, n_right, reach):
        for sign, span in ((1, n_right), (-1, n_left)):
            if leg >= span:
                continue
            back = (n_dp - sign * leg) % n_dp
            slot = lax.rem(d + back, n_dp)
            if leg:
                arrive(slot)
                waited.add(back)
            for hop in range(1, min(reach, span - leg) + 1):
                peer = lax.rem(d + (n_dp + sign * hop) % n_dp, n_dp)
                copy = ag_copy(slot, len(sends), peer)
                copy.start()
                sends.append(copy)
        if leg == 0:
            lg = ln_out[...]
            own = ag_buf[d]
            part = jnp.sum(own * own) + (d == 0).astype(jnp.float32) * (
                jnp.sum(lg * lg) / float(n_row)
            )
            nbuf[me_rc] = jnp.full(nbuf.shape[1:], part, jnp.float32)
            for j in range(1, n_rc):
                copy = n_copy(j, lax.rem(me_rc + j, n_rc), me_rc)
                copy.start()
                n_copies.append(copy)

    for j in range(1, n_rc):
        sender = lax.rem(me_rc + n_rc - j, n_rc)
        n_copy(j, sender, sender).wait_recv()
    for copy in n_copies:
        copy.wait_send()
    pbuf[d] = jnp.sum(nbuf[...], axis=0)
    p_copies = []
    for j in range(1, n_dp):
        copy = p_copy(j, lax.rem(d + j, n_dp), d)
        copy.start()
        p_copies.append(copy)
    for back in range(1, n_dp):
        if back not in waited:
            arrive(lax.rem(d + back, n_dp))
    for copy in sends:
        copy.wait_send()
    for j in range(1, n_dp):
        sender = lax.rem(d + n_dp - j, n_dp)
        p_copy(j, sender, sender).wait_recv()
    for copy in p_copies:
        copy.wait_send()
    norm_total = jnp.sum(pbuf[...], axis=0)[0:1, 0:1]
    for k in range(n_dp):
        for q in range(n_col):
            g_out[
                pl.ds((k // halves) * depth, depth),
                pl.ds(q * halves * width + (k % halves) * width, width),
            ] = ag_buf[k, q]
    finish_part(n_col, g_out, m_ref, f_ref, s_ref, c_out, b_out, norm_total,
                mbuf, rbuf, m_send, m_recv)


def reduce_blocks(block, ln_part, master, first, second, average):
    n_dp, n_row, n_col = lax.axis_size("dp"), lax.axis_size("row"), lax.axis_size("col")
    rows, cols = block.shape
    quarter = rows // n_col
    width = 128
    halves = cols // width
    depth = quarter * halves // n_dp
    n = n_row * n_col
    vmem = pl.BlockSpec(memory_space=pltpu.VMEM)
    return pl.pallas_call(
        functools.partial(reduce_kernel, n_dp, n_row, n_col),
        out_shape=(
            jax.ShapeDtypeStruct((quarter, cols * n_col), jnp.float32),
            jax.ShapeDtypeStruct(ln_part.shape, jnp.float32),
            jax.ShapeDtypeStruct((8, 128), jnp.float32),
            jax.ShapeDtypeStruct(average.shape, jnp.float32),
        ),
        in_specs=[vmem] * 5,
        out_specs=(vmem, vmem, vmem, vmem),
        scratch_shapes=[
            pltpu.VMEM((n_dp, n_col, depth, width), block.dtype),
            pltpu.VMEM((n_dp, n_col, depth, width), jnp.float32),
            pltpu.VMEM((n_dp,) + ln_part.shape, ln_part.dtype),
            pltpu.SemaphoreType.DMA((n_dp * n_col,)),
            pltpu.SemaphoreType.DMA((n_dp * n_col,)),
            pltpu.SemaphoreType.DMA((n_dp,)),
            pltpu.SemaphoreType.DMA((n_dp,)),
            pltpu.SemaphoreType.DMA((n_dp,)),
            pltpu.SemaphoreType.DMA((n_dp,)),
            pltpu.VMEM((n, 8, 128), jnp.float32),
            pltpu.VMEM((n_col,) + master.shape, jnp.float32),
            pltpu.VMEM((n_col, master.shape[0], average.shape[1]), jnp.float32),
            pltpu.SemaphoreType.DMA((n,)),
            pltpu.SemaphoreType.DMA((n,)),
            pltpu.SemaphoreType.DMA((n_col,)),
            pltpu.SemaphoreType.DMA((n_col,)),
            pltpu.VMEM((n_dp, 8, 128), jnp.float32),
            pltpu.SemaphoreType.DMA((n_dp,)),
            pltpu.SemaphoreType.DMA((n_dp,)),
        ],
        compiler_params=pltpu.CompilerParams(collective_id=1, has_side_effects=True),
    )(block, ln_part, master, first, second)


def apply_kernel(c_ref, g_ref, m_ref, f_ref, s_ref, a_ref, b_ref, lg_ref, lm_ref, lf_ref, ls_ref,
                 la_ref, a_out, m_out, f_out, s_out, lm_out, lf_out, ls_out, la_out,
                 flat, block, small, sems):
    clip_scale = c_ref[0:1, 0:1]
    master_new, first_new, second_new = adam_step(
        g_ref[...], clip_scale, f_ref[...], s_ref[...], m_ref[...], decay_rate
    )
    flat[0] = master_new
    flat[1] = first_new
    flat[2] = second_new
    block[...] = ema_keep * a_ref[...] + (1.0 - ema_keep) * b_ref[...]
    ln_master_new, ln_first_new, ln_second_new = adam_step(
        lg_ref[...], clip_scale, lf_ref[...], ls_ref[...], lm_ref[...], 0.0
    )
    small[0] = ln_master_new
    small[1] = ln_first_new
    small[2] = ln_second_new
    small[3] = ema_keep * la_ref[...] + (1.0 - ema_keep) * ln_master_new
    copies = [
        pltpu.make_async_copy(flat.at[0], m_out, sems.at[0]),
        pltpu.make_async_copy(flat.at[1], f_out, sems.at[1]),
        pltpu.make_async_copy(flat.at[2], s_out, sems.at[2]),
        pltpu.make_async_copy(block, a_out, sems.at[3]),
        pltpu.make_async_copy(small.at[0], lm_out, sems.at[4]),
        pltpu.make_async_copy(small.at[1], lf_out, sems.at[5]),
        pltpu.make_async_copy(small.at[2], ls_out, sems.at[6]),
        pltpu.make_async_copy(small.at[3], la_out, sems.at[7]),
    ]
    for copy in copies:
        copy.start()
    for copy in copies:
        copy.wait()


def apply_update(clip_tile, gradient, master, first, second, average, block_master,
                 ln_gradient, ln_master, ln_first, ln_second, ln_average):
    vmem = pl.BlockSpec(memory_space=pltpu.VMEM)
    anywhere = pl.BlockSpec(memory_space=pl.ANY)
    outs = (average, master, first, second, ln_master, ln_first, ln_second, ln_average)
    return pl.pallas_call(
        apply_kernel,
        out_shape=tuple(jax.ShapeDtypeStruct(x.shape, jnp.float32) for x in outs),
        in_specs=[vmem] * 12,
        out_specs=tuple([anywhere] * 8),
        scratch_shapes=[
            pltpu.VMEM((3,) + master.shape, jnp.float32),
            pltpu.VMEM(average.shape, jnp.float32),
            pltpu.VMEM((4,) + ln_master.shape, jnp.float32),
            pltpu.SemaphoreType.DMA((8,)),
        ],
    )(clip_tile, gradient, master, first, second, average, block_master,
      ln_gradient, ln_master, ln_first, ln_second, ln_average)


def shards(
    grad_blocks,
    ln_grads,
    master,
    first_moment,
    second_moment,
    average,
    ln_master,
    ln_first,
    ln_second,
    ln_average,
):
    gradient, ln_gradient, clip_tile, block_master = reduce_blocks(
        grad_blocks[0], ln_grads[0], master, first_moment, second_moment, average
    )
    (
        average_new,
        master_new,
        first_new,
        second_new,
        ln_master_new,
        ln_first_new,
        ln_second_new,
        ln_average_new,
    ) = apply_update(
        clip_tile, gradient, master, first_moment, second_moment, average, block_master,
        ln_gradient, ln_master, ln_first, ln_second, ln_average,
    )
    return (
        average_new,
        master_new,
        first_new,
        second_new,
        ln_master_new,
        ln_first_new,
        ln_second_new,
        ln_average_new,
    )


def solution(mesh):
    placed = (
        P("dp", "row", "col"),
        P("dp", None, "col"),
        P(("row", "col"), None),
        P(("row", "col"), None),
        P(("row", "col"), None),
        P("row", "col"),
        P(None, "col"),
        P(None, "col"),
        P(None, "col"),
        P(None, "col"),
    )
    return jax.shard_map(
        shards,
        mesh=mesh,
        in_specs=placed,
        out_specs=(
            P("row", "col"),
            P(("row", "col"), None),
            P(("row", "col"), None),
            P(("row", "col"), None),
            P(None, "col"),
            P(None, "col"),
            P(None, "col"),
            P(None, "col"),
        ),
        check_vma=False,
    )
```

```python
import functools
import math

import jax
import jax.numpy as jnp
from jax import lax
from jax.experimental import pallas as pl
from jax.experimental.pallas import tpu as pltpu
from jax.sharding import PartitionSpec as P

MESH = pl.DeviceIdType.MESH

D = 1024
FF = 4096
STEP = 20


beta_one = 0.9
beta_two = 0.95
learn_rate = 0.02
decay_rate = 0.1
epsilon = 1e-08
clip_rms = 1.0
ema_keep = 0.9


def adam_step(gradient, clip_scale, first, second, master, decay_weight):
    clipped = clip_scale * gradient
    first_new = beta_one * first + (1.0 - beta_one) * clipped
    second_new = beta_two * second + (1.0 - beta_two) * clipped * clipped
    direction = (
        first_new
        / (1.0 - beta_one**STEP)
        / (jnp.sqrt(second_new / (1.0 - beta_two**STEP)) + epsilon)
    )
    master_new = master - learn_rate * (direction + decay_weight * master)
    return (master_new, first_new, second_new)


def clip_factor(norm_total):
    return jnp.minimum(1.0, clip_rms * math.sqrt(FF * D + 4 * D) / jnp.sqrt(norm_total))


def squares(gradient, ln_gradient, row_count):
    return jnp.sum(gradient * gradient) + jnp.sum(ln_gradient * ln_gradient) / row_count


def finish_part(n_col, g_ref, m_ref, f_ref, s_ref, c_out, b_out, norm_total,
                mbuf, rbuf, m_send, m_recv):
    d = lax.axis_index("dp")
    r = lax.axis_index("row")
    c = lax.axis_index("col")
    g = g_ref[...]
    clip_scale = clip_factor(norm_total)
    c_out[...] = jnp.broadcast_to(clip_scale, c_out.shape)
    master_new, _, _ = adam_step(g, clip_scale, f_ref[...], s_ref[...], m_ref[...], decay_rate)
    mbuf[c] = master_new
    width = b_out.shape[1]

    def m_copy(j, peer, slot):
        return pltpu.make_async_remote_copy(
            src_ref=mbuf.at[c, :, pl.ds(pl.multiple_of(peer * width, width), width)],
            dst_ref=rbuf.at[slot],
            send_sem=m_send.at[j],
            recv_sem=m_recv.at[slot],
            device_id=(d, r, peer),
            device_id_type=MESH,
        )

    copies = []
    for j in range(1, n_col):
        copy = m_copy(j, lax.rem(c + j, n_col), c)
        copy.start()
        copies.append(copy)
    rbuf[c] = mbuf[c, :, pl.ds(pl.multiple_of(c * width, width), width)]
    for j in range(1, n_col):
        sender = lax.rem(c + n_col - j, n_col)
        m_copy(j, sender, sender).wait_recv()
    for copy in copies:
        copy.wait_send()
    depth = rbuf.shape[1]
    for q in range(n_col):
        b_out[pl.ds(q * depth, depth), :] = rbuf[q]


def reduce_kernel(n_dp, n_row, n_col, g_ref, ln_ref, m_ref, f_ref, s_ref,
                  g_out, ln_out, c_out, b_out, rs_buf, ag_buf, ln_buf,
                  rs_send, rs_recv, ag_send, ag_recv, ln_send, ln_recv,
                  nbuf, mbuf, rbuf, n_send, n_recv, m_send, m_recv, pbuf, p_send, p_recv):
    d = lax.axis_index("dp")
    r = lax.axis_index("row")
    c = lax.axis_index("col")
    n = n_dp * n_col
    me = d * n_col + c
    quarter = g_ref.shape[0] // n_col
    depth = rs_buf.shape[2]
    width = rs_buf.shape[3]
    halves = g_ref.shape[1] // width
    barrier = pltpu.get_barrier_semaphore()

    def greet(j, carry):
        peer = lax.rem(me + j, n)
        pl.semaphore_signal(
            barrier, inc=1, device_id=(peer // n_col, r, peer % n_col), device_id_type=MESH
        )
        return carry

    lax.fori_loop(1, n, greet, 0)

    def greet_row(j, carry):
        peer = lax.rem(r + 1 + j // n_col, n_row)
        pl.semaphore_signal(
            barrier, inc=1, device_id=(d, peer, j % n_col), device_id_type=MESH
        )
        return carry

    lax.fori_loop(0, (n_row - 1) * n_col, greet_row, 0)
    pl.semaphore_wait(barrier, n - 1 + (n_row - 1) * n_col)

    def piece(k, q):
        rows = pl.ds(pl.multiple_of(q * quarter + (k // halves) * depth, depth), depth)
        cols = pl.ds(pl.multiple_of((k % halves) * width, width), width)
        return g_ref.at[rows, cols]

    def rs_copy(j):
        peer = lax.rem(me + j, n)
        return pltpu.make_async_remote_copy(
            src_ref=piece(peer // n_col, peer % n_col),
            dst_ref=rs_buf.at[d, c],
            send_sem=rs_send.at[j],
            recv_sem=rs_recv.at[me],
            device_id=(peer // n_col, r, peer % n_col),
            device_id_type=MESH,
        )

    def ln_copy(j):
        peer = lax.rem(d + j, n_dp)
        return pltpu.make_async_remote_copy(
            src_ref=ln_ref,
            dst_ref=ln_buf.at[d],
            send_sem=ln_send.at[j],
            recv_sem=ln_recv.at[d],
            device_id=(peer, r, c),
            device_id_type=MESH,
        )

    def start_rs(j, carry):
        rs_copy(j).start()
        return carry

    def start_ln(j, carry):
        ln_copy(j).start()
        return carry

    lax.fori_loop(1, n, start_rs, 0)
    lax.fori_loop(1, n_dp, start_ln, 0)
    rs_buf[d, c] = piece(d, c)[...]
    ln_buf[d] = ln_ref[...]

    def wait_rs(j, carry):
        src = lax.rem(me + j, n)
        pltpu.make_async_remote_copy(
            src_ref=piece(0, 0),
            dst_ref=rs_buf.at[src // n_col, src % n_col],
            send_sem=rs_send.at[j],
            recv_sem=rs_recv.at[src],
            device_id=(src // n_col, r, src % n_col),
            device_id_type=MESH,
        ).wait_recv()
        rs_copy(j).wait_send()
        return carry

    lax.fori_loop(1, n, wait_rs, 0)
    def wait_ln(j, carry):
        src = lax.rem(d + j, n_dp)
        pltpu.make_async_remote_copy(
            src_ref=ln_ref,
            dst_ref=ln_buf.at[src],
            send_sem=ln_send.at[j],
            recv_sem=ln_recv.at[src],
            device_id=(src, r, c),
            device_id_type=MESH,
        ).wait_recv()
        ln_copy(j).wait_send()
        return carry

    lax.fori_loop(1, n_dp, wait_ln, 0)
    ln_out[...] = jnp.sum(ln_buf[...].astype(jnp.float32), axis=0)

    ag_buf[d] = jnp.sum(rs_buf[...].astype(jnp.float32), axis=0)

    def ag_copy(slot, j, peer):
        return pltpu.make_async_remote_copy(
            src_ref=ag_buf.at[slot],
            dst_ref=ag_buf.at[slot],
            send_sem=ag_send.at[j],
            recv_sem=ag_recv.at[slot],
            device_id=(peer, r, c),
            device_id_type=MESH,
        )

    def arrive(slot):
        ag_copy(slot, 0, slot).wait_recv()

    n_rc = n_row * n_col
    me_rc = r * n_col + c

    def n_copy(j, peer, slot):
        return pltpu.make_async_remote_copy(
            src_ref=nbuf.at[slot],
            dst_ref=nbuf.at[slot],
            send_sem=n_send.at[j],
            recv_sem=n_recv.at[slot],
            device_id=(d, peer // n_col, peer % n_col),
            device_id_type=MESH,
        )

    def p_copy(j, peer, slot):
        return pltpu.make_async_remote_copy(
            src_ref=pbuf.at[slot],
            dst_ref=pbuf.at[slot],
            send_sem=p_send.at[j],
            recv_sem=p_recv.at[slot],
            device_id=(peer, r, c),
            device_id_type=MESH,
        )

    reach = 2
    n_right = n_dp // 2
    n_left = n_dp - 1 - n_right
    sends = []
    waited = set()
    n_copies = []
    for leg in range(0, n_right, reach):
        for sign, span in ((1, n_right), (-1, n_left)):
            if leg >= span:
                continue
            back = (n_dp - sign * leg) % n_dp
            slot = lax.rem(d + back, n_dp)
            if leg:
                arrive(slot)
                waited.add(back)
            for hop in range(1, min(reach, span - leg) + 1):
                peer = lax.rem(d + (n_dp + sign * hop) % n_dp, n_dp)
                copy = ag_copy(slot, len(sends), peer)
                copy.start()
                sends.append(copy)
        if leg == 0:
            lg = ln_out[...]
            own = ag_buf[d]
            part = jnp.sum(own * own) + (d == 0).astype(jnp.float32) * (
                jnp.sum(lg * lg) / float(n_row)
            )
            nbuf[me_rc] = jnp.full(nbuf.shape[1:], part, jnp.float32)
            for j in range(1, n_rc):
                copy = n_copy(j, lax.rem(me_rc + j, n_rc), me_rc)
                copy.start()
                n_copies.append(copy)

    for j in range(1, n_rc):
        sender = lax.rem(me_rc + n_rc - j, n_rc)
        n_copy(j, sender, sender).wait_recv()
    for copy in n_copies:
        copy.wait_send()
    pbuf[d] = jnp.sum(nbuf[...], axis=0)
    p_copies = []
    for j in range(1, n_dp):
        copy = p_copy(j, lax.rem(d + j, n_dp), d)
        copy.start()
        p_copies.append(copy)
    for back in range(1, n_dp):
        if back not in waited:
            arrive(lax.rem(d + back, n_dp))
    for copy in sends:
        copy.wait_send()
    for j in range(1, n_dp):
        sender = lax.rem(d + n_dp - j, n_dp)
        p_copy(j, sender, sender).wait_recv()
    for copy in p_copies:
        copy.wait_send()
    norm_total = jnp.sum(pbuf[...], axis=0)[0:1, 0:1]
    for k in range(n_dp):
        for q in range(n_col):
            g_out[
                pl.ds((k // halves) * depth, depth),
                pl.ds(q * halves * width + (k % halves) * width, width),
            ] = ag_buf[k, q]
    finish_part(n_col, g_out, m_ref, f_ref, s_ref, c_out, b_out, norm_total,
                mbuf, rbuf, m_send, m_recv)


def reduce_blocks(block, ln_part, master, first, second, average):
    n_dp, n_row, n_col = lax.axis_size("dp"), lax.axis_size("row"), lax.axis_size("col")
    rows, cols = block.shape
    quarter = rows // n_col
    width = 128
    halves = cols // width
    depth = quarter * halves // n_dp
    n = n_row * n_col
    vmem = pl.BlockSpec(memory_space=pltpu.VMEM)
    return pl.pallas_call(
        functools.partial(reduce_kernel, n_dp, n_row, n_col),
        out_shape=(
            jax.ShapeDtypeStruct((quarter, cols * n_col), jnp.float32),
            jax.ShapeDtypeStruct(ln_part.shape, jnp.float32),
            jax.ShapeDtypeStruct((8, 128), jnp.float32),
            jax.ShapeDtypeStruct(average.shape, jnp.float32),
        ),
        in_specs=[vmem] * 5,
        out_specs=(vmem, vmem, vmem, vmem),
        scratch_shapes=[
            pltpu.VMEM((n_dp, n_col, depth, width), block.dtype),
            pltpu.VMEM((n_dp, n_col, depth, width), jnp.float32),
            pltpu.VMEM((n_dp,) + ln_part.shape, ln_part.dtype),
            pltpu.SemaphoreType.DMA((n_dp * n_col,)),
            pltpu.SemaphoreType.DMA((n_dp * n_col,)),
            pltpu.SemaphoreType.DMA((n_dp,)),
            pltpu.SemaphoreType.DMA((n_dp,)),
            pltpu.SemaphoreType.DMA((n_dp,)),
            pltpu.SemaphoreType.DMA((n_dp,)),
            pltpu.VMEM((n, 8, 128), jnp.float32),
            pltpu.VMEM((n_col,) + master.shape, jnp.float32),
            pltpu.VMEM((n_col, master.shape[0], average.shape[1]), jnp.float32),
            pltpu.SemaphoreType.DMA((n,)),
            pltpu.SemaphoreType.DMA((n,)),
            pltpu.SemaphoreType.DMA((n_col,)),
            pltpu.SemaphoreType.DMA((n_col,)),
            pltpu.VMEM((n_dp, 8, 128), jnp.float32),
            pltpu.SemaphoreType.DMA((n_dp,)),
            pltpu.SemaphoreType.DMA((n_dp,)),
        ],
        compiler_params=pltpu.CompilerParams(collective_id=1, has_side_effects=True),
    )(block, ln_part, master, first, second)


def apply_kernel(c_ref, g_ref, m_ref, f_ref, s_ref, a_ref, b_ref, lg_ref, lm_ref, lf_ref, ls_ref,
                 la_ref, a_out, m_out, f_out, s_out, lm_out, lf_out, ls_out, la_out,
                 flat, block, small, sems):
    clip_scale = c_ref[0:1, 0:1]
    master_new, first_new, second_new = adam_step(
        g_ref[...], clip_scale, f_ref[...], s_ref[...], m_ref[...], decay_rate
    )
    flat[0] = master_new
    flat[1] = first_new
    flat[2] = second_new
    block[...] = ema_keep * a_ref[...] + (1.0 - ema_keep) * b_ref[...]
    ln_master_new, ln_first_new, ln_second_new = adam_step(
        lg_ref[...], clip_scale, lf_ref[...], ls_ref[...], lm_ref[...], 0.0
    )
    small[0] = ln_master_new
    small[1] = ln_first_new
    small[2] = ln_second_new
    small[3] = ema_keep * la_ref[...] + (1.0 - ema_keep) * ln_master_new
    copies = [
        pltpu.make_async_copy(flat.at[0], m_out, sems.at[0]),
        pltpu.make_async_copy(flat.at[1], f_out, sems.at[1]),
        pltpu.make_async_copy(flat.at[2], s_out, sems.at[2]),
        pltpu.make_async_copy(block, a_out, sems.at[3]),
        pltpu.make_async_copy(small.at[0], lm_out, sems.at[4]),
        pltpu.make_async_copy(small.at[1], lf_out, sems.at[5]),
        pltpu.make_async_copy(small.at[2], ls_out, sems.at[6]),
        pltpu.make_async_copy(small.at[3], la_out, sems.at[7]),
    ]
    for copy in copies:
        copy.start()
    for copy in copies:
        copy.wait()


def apply_update(clip_tile, gradient, master, first, second, average, block_master,
                 ln_gradient, ln_master, ln_first, ln_second, ln_average):
    vmem = pl.BlockSpec(memory_space=pltpu.VMEM)
    anywhere = pl.BlockSpec(memory_space=pl.ANY)
    outs = (average, master, first, second, ln_master, ln_first, ln_second, ln_average)
    return pl.pallas_call(
        apply_kernel,
        out_shape=tuple(jax.ShapeDtypeStruct(x.shape, jnp.float32) for x in outs),
        in_specs=[vmem] * 12,
        out_specs=tuple([anywhere] * 8),
        scratch_shapes=[
            pltpu.VMEM((3,) + master.shape, jnp.float32),
            pltpu.VMEM(average.shape, jnp.float32),
            pltpu.VMEM((4,) + ln_master.shape, jnp.float32),
            pltpu.SemaphoreType.DMA((8,)),
        ],
    )(clip_tile, gradient, master, first, second, average, block_master,
      ln_gradient, ln_master, ln_first, ln_second, ln_average)


def shards(
    grad_blocks,
    ln_grads,
    master,
    first_moment,
    second_moment,
    average,
    ln_master,
    ln_first,
    ln_second,
    ln_average,
):
    gradient, ln_gradient, clip_tile, block_master = reduce_blocks(
        grad_blocks[0], ln_grads[0], master, first_moment, second_moment, average
    )
    (
        average_new,
        master_new,
        first_new,
        second_new,
        ln_master_new,
        ln_first_new,
        ln_second_new,
        ln_average_new,
    ) = apply_update(
        clip_tile, gradient, master, first_moment, second_moment, average, block_master,
        ln_gradient, ln_master, ln_first, ln_second, ln_average,
    )
    return (
        average_new,
        master_new,
        first_new,
        second_new,
        ln_master_new,
        ln_first_new,
        ln_second_new,
        ln_average_new,
    )


def solution(mesh):
    placed = (
        P("dp", "row", "col"),
        P("dp", None, "col"),
        P(("row", "col"), None),
        P(("row", "col"), None),
        P(("row", "col"), None),
        P("row", "col"),
        P(None, "col"),
        P(None, "col"),
        P(None, "col"),
        P(None, "col"),
    )
    return jax.shard_map(
        shards,
        mesh=mesh,
        in_specs=placed,
        out_specs=(
            P("row", "col"),
            P(("row", "col"), None),
            P(("row", "col"), None),
            P(("row", "col"), None),
            P(None, "col"),
            P(None, "col"),
            P(None, "col"),
            P(None, "col"),
        ),
        check_vma=False,
    )
```

```python
import functools
import math

import jax
import jax.numpy as jnp
from jax import lax
from jax.experimental import pallas as pl
from jax.experimental.pallas import tpu as pltpu
from jax.sharding import PartitionSpec as P

MESH = pl.DeviceIdType.MESH

D = 1024
FF = 4096
STEP = 20


beta_one = 0.9
beta_two = 0.95
learn_rate = 0.02
decay_rate = 0.1
epsilon = 1e-08
clip_rms = 1.0
ema_keep = 0.9


def adam_step(gradient, clip_scale, first, second, master, decay_weight):
    clipped = clip_scale * gradient
    first_new = beta_one * first + (1.0 - beta_one) * clipped
    second_new = beta_two * second + (1.0 - beta_two) * clipped * clipped
    direction = (
        first_new
        / (1.0 - beta_one**STEP)
        / (jnp.sqrt(second_new / (1.0 - beta_two**STEP)) + epsilon)
    )
    master_new = master - learn_rate * (direction + decay_weight * master)
    return (master_new, first_new, second_new)


def clip_factor(norm_total):
    return jnp.minimum(1.0, clip_rms * math.sqrt(FF * D + 4 * D) / jnp.sqrt(norm_total))


def squares(gradient, ln_gradient, row_count):
    return jnp.sum(gradient * gradient) + jnp.sum(ln_gradient * ln_gradient) / row_count


def finish_part(n_col, g_ref, m_ref, f_ref, s_ref, c_out, b_out, norm_total,
                mbuf, rbuf, m_send, m_recv):
    d = lax.axis_index("dp")
    r = lax.axis_index("row")
    c = lax.axis_index("col")
    clip_scale = clip_factor(norm_total)
    c_out[...] = jnp.broadcast_to(clip_scale, c_out.shape)
    width = b_out.shape[1]

    def chunk(peer):
        cols = pl.ds(pl.multiple_of(peer * width, width), width)
        master_new, _, _ = adam_step(
            g_ref[:, cols], clip_scale, f_ref[:, cols], s_ref[:, cols], m_ref[:, cols], decay_rate
        )
        return master_new

    def m_copy(j, peer, slot):
        return pltpu.make_async_remote_copy(
            src_ref=mbuf.at[peer],
            dst_ref=rbuf.at[slot],
            send_sem=m_send.at[j],
            recv_sem=m_recv.at[slot],
            device_id=(d, r, peer),
            device_id_type=MESH,
        )

    copies = []
    for j in range(1, n_col):
        peer = lax.rem(c + j, n_col)
        mbuf[peer] = chunk(peer)
        copy = m_copy(j, peer, c)
        copy.start()
        copies.append(copy)
    rbuf[c] = chunk(c)
    for j in range(1, n_col):
        sender = lax.rem(c + n_col - j, n_col)
        m_copy(j, sender, sender).wait_recv()
    for copy in copies:
        copy.wait_send()
    depth = rbuf.shape[1]
    for q in range(n_col):
        b_out[pl.ds(q * depth, depth), :] = rbuf[q]


def reduce_kernel(n_dp, n_row, n_col, g_ref, ln_ref, m_ref, f_ref, s_ref,
                  g_out, ln_out, c_out, b_out, rs_buf, ag_buf, ln_buf,
                  rs_send, rs_recv, ag_send, ag_recv, ln_send, ln_recv,
                  nbuf, mbuf, rbuf, n_send, n_recv, m_send, m_recv, pbuf, p_send, p_recv):
    d = lax.axis_index("dp")
    r = lax.axis_index("row")
    c = lax.axis_index("col")
    n = n_dp * n_col
    me = d * n_col + c
    quarter = g_ref.shape[0] // n_col
    depth = rs_buf.shape[2]
    width = rs_buf.shape[3]
    halves = g_ref.shape[1] // width
    barrier = pltpu.get_barrier_semaphore()

    def greet(j, carry):
        peer = lax.rem(me + j, n)
        pl.semaphore_signal(
            barrier, inc=1, device_id=(peer // n_col, r, peer % n_col), device_id_type=MESH
        )
        return carry

    lax.fori_loop(1, n, greet, 0)

    def greet_row(j, carry):
        peer = lax.rem(r + 1 + j // n_col, n_row)
        pl.semaphore_signal(
            barrier, inc=1, device_id=(d, peer, j % n_col), device_id_type=MESH
        )
        return carry

    lax.fori_loop(0, (n_row - 1) * n_col, greet_row, 0)
    pl.semaphore_wait(barrier, n - 1 + (n_row - 1) * n_col)

    def piece(k, q):
        rows = pl.ds(pl.multiple_of(q * quarter + (k // halves) * depth, depth), depth)
        cols = pl.ds(pl.multiple_of((k % halves) * width, width), width)
        return g_ref.at[rows, cols]

    def rs_copy(j):
        peer = lax.rem(me + j, n)
        return pltpu.make_async_remote_copy(
            src_ref=piece(peer // n_col, peer % n_col),
            dst_ref=rs_buf.at[d, c],
            send_sem=rs_send.at[j],
            recv_sem=rs_recv.at[me],
            device_id=(peer // n_col, r, peer % n_col),
            device_id_type=MESH,
        )

    def ln_copy(j):
        peer = lax.rem(d + j, n_dp)
        return pltpu.make_async_remote_copy(
            src_ref=ln_ref,
            dst_ref=ln_buf.at[d],
            send_sem=ln_send.at[j],
            recv_sem=ln_recv.at[d],
            device_id=(peer, r, c),
            device_id_type=MESH,
        )

    def start_rs(j, carry):
        rs_copy(j).start()
        return carry

    def start_ln(j, carry):
        ln_copy(j).start()
        return carry

    lax.fori_loop(1, n, start_rs, 0)
    lax.fori_loop(1, n_dp, start_ln, 0)
    rs_buf[d, c] = piece(d, c)[...]
    ln_buf[d] = ln_ref[...]

    def wait_rs(j, carry):
        src = lax.rem(me + j, n)
        pltpu.make_async_remote_copy(
            src_ref=piece(0, 0),
            dst_ref=rs_buf.at[src // n_col, src % n_col],
            send_sem=rs_send.at[j],
            recv_sem=rs_recv.at[src],
            device_id=(src // n_col, r, src % n_col),
            device_id_type=MESH,
        ).wait_recv()
        rs_copy(j).wait_send()
        return carry

    lax.fori_loop(1, n, wait_rs, 0)
    def wait_ln(j, carry):
        src = lax.rem(d + j, n_dp)
        pltpu.make_async_remote_copy(
            src_ref=ln_ref,
            dst_ref=ln_buf.at[src],
            send_sem=ln_send.at[j],
            recv_sem=ln_recv.at[src],
            device_id=(src, r, c),
            device_id_type=MESH,
        ).wait_recv()
        ln_copy(j).wait_send()
        return carry

    lax.fori_loop(1, n_dp, wait_ln, 0)
    ln_out[...] = jnp.sum(ln_buf[...].astype(jnp.float32), axis=0)

    ag_buf[d] = jnp.sum(rs_buf[...].astype(jnp.float32), axis=0)

    def ag_copy(slot, j, peer):
        return pltpu.make_async_remote_copy(
            src_ref=ag_buf.at[slot],
            dst_ref=ag_buf.at[slot],
            send_sem=ag_send.at[j],
            recv_sem=ag_recv.at[slot],
            device_id=(peer, r, c),
            device_id_type=MESH,
        )

    def arrive(slot):
        ag_copy(slot, 0, slot).wait_recv()

    n_rc = n_row * n_col
    me_rc = r * n_col + c

    def n_copy(j, peer, slot):
        return pltpu.make_async_remote_copy(
            src_ref=nbuf.at[slot],
            dst_ref=nbuf.at[slot],
            send_sem=n_send.at[j],
            recv_sem=n_recv.at[slot],
            device_id=(d, peer // n_col, peer % n_col),
            device_id_type=MESH,
        )

    def p_copy(j, peer, slot):
        return pltpu.make_async_remote_copy(
            src_ref=pbuf.at[slot],
            dst_ref=pbuf.at[slot],
            send_sem=p_send.at[j],
            recv_sem=p_recv.at[slot],
            device_id=(peer, r, c),
            device_id_type=MESH,
        )

    reach = 3
    n_right = n_dp // 2
    n_left = n_dp - 1 - n_right
    sends = []
    waited = set()
    n_copies = []
    for leg in range(0, n_right, reach):
        for sign, span in ((1, n_right), (-1, n_left)):
            if leg >= span:
                continue
            back = (n_dp - sign * leg) % n_dp
            slot = lax.rem(d + back, n_dp)
            if leg:
                arrive(slot)
                waited.add(back)
            for hop in range(1, min(reach, span - leg) + 1):
                peer = lax.rem(d + (n_dp + sign * hop) % n_dp, n_dp)
                copy = ag_copy(slot, len(sends), peer)
                copy.start()
                sends.append(copy)
        if leg == 0:
            lg = ln_out[...]
            own = ag_buf[d]
            part = jnp.sum(own * own) + (d == 0).astype(jnp.float32) * (
                jnp.sum(lg * lg) / float(n_row)
            )
            nbuf[me_rc] = jnp.full(nbuf.shape[1:], part, jnp.float32)
            for j in range(1, n_rc):
                copy = n_copy(j, lax.rem(me_rc + j, n_rc), me_rc)
                copy.start()
                n_copies.append(copy)

    for j in range(1, n_rc):
        sender = lax.rem(me_rc + n_rc - j, n_rc)
        n_copy(j, sender, sender).wait_recv()
    for copy in n_copies:
        copy.wait_send()
    pbuf[d] = jnp.sum(nbuf[...], axis=0)
    p_copies = []
    for j in range(1, n_dp):
        copy = p_copy(j, lax.rem(d + j, n_dp), d)
        copy.start()
        p_copies.append(copy)
    for back in range(1, n_dp):
        if back not in waited:
            arrive(lax.rem(d + back, n_dp))
    for copy in sends:
        copy.wait_send()
    for j in range(1, n_dp):
        sender = lax.rem(d + n_dp - j, n_dp)
        p_copy(j, sender, sender).wait_recv()
    for copy in p_copies:
        copy.wait_send()
    norm_total = jnp.sum(pbuf[...], axis=0)[0:1, 0:1]
    for k in range(n_dp):
        for q in range(n_col):
            g_out[
                pl.ds((k // halves) * depth, depth),
                pl.ds(q * halves * width + (k % halves) * width, width),
            ] = ag_buf[k, q]
    finish_part(n_col, g_out, m_ref, f_ref, s_ref, c_out, b_out, norm_total,
                mbuf, rbuf, m_send, m_recv)


def reduce_blocks(block, ln_part, master, first, second, average):
    n_dp, n_row, n_col = lax.axis_size("dp"), lax.axis_size("row"), lax.axis_size("col")
    rows, cols = block.shape
    quarter = rows // n_col
    width = 128
    halves = cols // width
    depth = quarter * halves // n_dp
    n = n_row * n_col
    vmem = pl.BlockSpec(memory_space=pltpu.VMEM)
    return pl.pallas_call(
        functools.partial(reduce_kernel, n_dp, n_row, n_col),
        out_shape=(
            jax.ShapeDtypeStruct((quarter, cols * n_col), jnp.float32),
            jax.ShapeDtypeStruct(ln_part.shape, jnp.float32),
            jax.ShapeDtypeStruct((8, 128), jnp.float32),
            jax.ShapeDtypeStruct(average.shape, jnp.float32),
        ),
        in_specs=[vmem] * 5,
        out_specs=(vmem, vmem, vmem, vmem),
        scratch_shapes=[
            pltpu.VMEM((n_dp, n_col, depth, width), block.dtype),
            pltpu.VMEM((n_dp, n_col, depth, width), jnp.float32),
            pltpu.VMEM((n_dp,) + ln_part.shape, ln_part.dtype),
            pltpu.SemaphoreType.DMA((n_dp * n_col,)),
            pltpu.SemaphoreType.DMA((n_dp * n_col,)),
            pltpu.SemaphoreType.DMA((n_dp,)),
            pltpu.SemaphoreType.DMA((n_dp,)),
            pltpu.SemaphoreType.DMA((n_dp,)),
            pltpu.SemaphoreType.DMA((n_dp,)),
            pltpu.VMEM((n, 8, 128), jnp.float32),
            pltpu.VMEM((n_col, master.shape[0], average.shape[1]), jnp.float32),
            pltpu.VMEM((n_col, master.shape[0], average.shape[1]), jnp.float32),
            pltpu.SemaphoreType.DMA((n,)),
            pltpu.SemaphoreType.DMA((n,)),
            pltpu.SemaphoreType.DMA((n_col,)),
            pltpu.SemaphoreType.DMA((n_col,)),
            pltpu.VMEM((n_dp, 8, 128), jnp.float32),
            pltpu.SemaphoreType.DMA((n_dp,)),
            pltpu.SemaphoreType.DMA((n_dp,)),
        ],
        compiler_params=pltpu.CompilerParams(collective_id=1, has_side_effects=True),
    )(block, ln_part, master, first, second)


def apply_kernel(c_ref, g_ref, m_ref, f_ref, s_ref, a_ref, b_ref, lg_ref, lm_ref, lf_ref, ls_ref,
                 la_ref, a_out, m_out, f_out, s_out, lm_out, lf_out, ls_out, la_out,
                 flat, block, small, sems):
    clip_scale = c_ref[0:1, 0:1]
    master_new, first_new, second_new = adam_step(
        g_ref[...], clip_scale, f_ref[...], s_ref[...], m_ref[...], decay_rate
    )
    flat[0] = master_new
    flat[1] = first_new
    flat[2] = second_new
    copies = [
        pltpu.make_async_copy(flat.at[0], m_out, sems.at[0]),
        pltpu.make_async_copy(flat.at[1], f_out, sems.at[1]),
        pltpu.make_async_copy(flat.at[2], s_out, sems.at[2]),
    ]
    for copy in copies:
        copy.start()
    block[...] = ema_keep * a_ref[...] + (1.0 - ema_keep) * b_ref[...]
    copy = pltpu.make_async_copy(block, a_out, sems.at[3])
    copy.start()
    copies.append(copy)
    ln_master_new, ln_first_new, ln_second_new = adam_step(
        lg_ref[...], clip_scale, lf_ref[...], ls_ref[...], lm_ref[...], 0.0
    )
    small[0] = ln_master_new
    small[1] = ln_first_new
    small[2] = ln_second_new
    small[3] = ema_keep * la_ref[...] + (1.0 - ema_keep) * ln_master_new
    for i, out in enumerate((lm_out, lf_out, ls_out, la_out)):
        copy = pltpu.make_async_copy(small.at[i], out, sems.at[4 + i])
        copy.start()
        copies.append(copy)
    for copy in copies:
        copy.wait()


def apply_update(clip_tile, gradient, master, first, second, average, block_master,
                 ln_gradient, ln_master, ln_first, ln_second, ln_average):
    vmem = pl.BlockSpec(memory_space=pltpu.VMEM)
    anywhere = pl.BlockSpec(memory_space=pl.ANY)
    outs = (average, master, first, second, ln_master, ln_first, ln_second, ln_average)
    return pl.pallas_call(
        apply_kernel,
        out_shape=tuple(jax.ShapeDtypeStruct(x.shape, jnp.float32) for x in outs),
        in_specs=[vmem] * 12,
        out_specs=tuple([anywhere] * 8),
        scratch_shapes=[
            pltpu.VMEM((3,) + master.shape, jnp.float32),
            pltpu.VMEM(average.shape, jnp.float32),
            pltpu.VMEM((4,) + ln_master.shape, jnp.float32),
            pltpu.SemaphoreType.DMA((8,)),
        ],
    )(clip_tile, gradient, master, first, second, average, block_master,
      ln_gradient, ln_master, ln_first, ln_second, ln_average)


def shards(
    grad_blocks,
    ln_grads,
    master,
    first_moment,
    second_moment,
    average,
    ln_master,
    ln_first,
    ln_second,
    ln_average,
):
    gradient, ln_gradient, clip_tile, block_master = reduce_blocks(
        grad_blocks[0], ln_grads[0], master, first_moment, second_moment, average
    )
    (
        average_new,
        master_new,
        first_new,
        second_new,
        ln_master_new,
        ln_first_new,
        ln_second_new,
        ln_average_new,
    ) = apply_update(
        clip_tile, gradient, master, first_moment, second_moment, average, block_master,
        ln_gradient, ln_master, ln_first, ln_second, ln_average,
    )
    return (
        average_new,
        master_new,
        first_new,
        second_new,
        ln_master_new,
        ln_first_new,
        ln_second_new,
        ln_average_new,
    )


def solution(mesh):
    placed = (
        P("dp", "row", "col"),
        P("dp", None, "col"),
        P(("row", "col"), None),
        P(("row", "col"), None),
        P(("row", "col"), None),
        P("row", "col"),
        P(None, "col"),
        P(None, "col"),
        P(None, "col"),
        P(None, "col"),
    )
    return jax.shard_map(
        shards,
        mesh=mesh,
        in_specs=placed,
        out_specs=(
            P("row", "col"),
            P(("row", "col"), None),
            P(("row", "col"), None),
            P(("row", "col"), None),
            P(None, "col"),
            P(None, "col"),
            P(None, "col"),
            P(None, "col"),
        ),
        check_vma=False,
    )
```

```python
import functools
import math

import jax
import jax.numpy as jnp
from jax import lax
from jax.experimental import pallas as pl
from jax.experimental.pallas import tpu as pltpu
from jax.sharding import PartitionSpec as P

MESH = pl.DeviceIdType.MESH

D = 1024
FF = 4096
STEP = 20


beta_one = 0.9
beta_two = 0.95
learn_rate = 0.02
decay_rate = 0.1
epsilon = 1e-08
clip_rms = 1.0
ema_keep = 0.9


def adam_step(gradient, clip_scale, first, second, master, decay_weight):
    clipped = clip_scale * gradient
    first_new = beta_one * first + (1.0 - beta_one) * clipped
    second_new = beta_two * second + (1.0 - beta_two) * clipped * clipped
    direction = (
        first_new
        / (1.0 - beta_one**STEP)
        / (jnp.sqrt(second_new / (1.0 - beta_two**STEP)) + epsilon)
    )
    master_new = master - learn_rate * (direction + decay_weight * master)
    return (master_new, first_new, second_new)


def clip_factor(norm_total):
    return jnp.minimum(1.0, clip_rms * math.sqrt(FF * D + 4 * D) / jnp.sqrt(norm_total))


def squares(gradient, ln_gradient, row_count):
    return jnp.sum(gradient * gradient) + jnp.sum(ln_gradient * ln_gradient) / row_count


def finish_part(n_col, g_ref, m_ref, f_ref, s_ref, c_out, b_out, norm_total,
                mbuf, rbuf, m_send, m_recv):
    d = lax.axis_index("dp")
    r = lax.axis_index("row")
    c = lax.axis_index("col")
    clip_scale = clip_factor(norm_total)
    c_out[...] = jnp.broadcast_to(clip_scale, c_out.shape)
    width = b_out.shape[1]

    def chunk(peer):
        cols = pl.ds(pl.multiple_of(peer * width, width), width)
        master_new, _, _ = adam_step(
            g_ref[:, cols], clip_scale, f_ref[:, cols], s_ref[:, cols], m_ref[:, cols], decay_rate
        )
        return master_new

    def m_copy(j, peer, slot):
        return pltpu.make_async_remote_copy(
            src_ref=mbuf.at[peer],
            dst_ref=rbuf.at[slot],
            send_sem=m_send.at[j],
            recv_sem=m_recv.at[slot],
            device_id=(d, r, peer),
            device_id_type=MESH,
        )

    copies = []
    for j in range(1, n_col):
        peer = lax.rem(c + j, n_col)
        mbuf[peer] = chunk(peer)
        copy = m_copy(j, peer, c)
        copy.start()
        copies.append(copy)
    rbuf[c] = chunk(c)
    for j in range(1, n_col):
        sender = lax.rem(c + n_col - j, n_col)
        m_copy(j, sender, sender).wait_recv()
    for copy in copies:
        copy.wait_send()
    depth = rbuf.shape[1]
    for q in range(n_col):
        b_out[pl.ds(q * depth, depth), :] = rbuf[q]


def reduce_kernel(n_dp, n_row, n_col, g_ref, ln_ref, m_ref, f_ref, s_ref,
                  g_out, ln_out, c_out, b_out, rs_buf, ag_buf, ln_buf,
                  rs_send, rs_recv, ag_send, ag_recv, ln_send, ln_recv,
                  nbuf, mbuf, rbuf, n_send, n_recv, m_send, m_recv, pbuf, p_send, p_recv):
    d = lax.axis_index("dp")
    r = lax.axis_index("row")
    c = lax.axis_index("col")
    n = n_dp * n_col
    me = d * n_col + c
    quarter = g_ref.shape[0] // n_col
    depth = rs_buf.shape[2]
    width = rs_buf.shape[3]
    halves = g_ref.shape[1] // width
    barrier = pltpu.get_barrier_semaphore()

    def greet(j, carry):
        peer = lax.rem(me + j, n)
        pl.semaphore_signal(
            barrier, inc=1, device_id=(peer // n_col, r, peer % n_col), device_id_type=MESH
        )
        return carry

    lax.fori_loop(1, n, greet, 0)

    def greet_row(j, carry):
        peer = lax.rem(r + 1 + j // n_col, n_row)
        pl.semaphore_signal(
            barrier, inc=1, device_id=(d, peer, j % n_col), device_id_type=MESH
        )
        return carry

    lax.fori_loop(0, (n_row - 1) * n_col, greet_row, 0)
    pl.semaphore_wait(barrier, n - 1 + (n_row - 1) * n_col)

    def piece(k, q):
        rows = pl.ds(pl.multiple_of(q * quarter + (k // halves) * depth, depth), depth)
        cols = pl.ds(pl.multiple_of((k % halves) * width, width), width)
        return g_ref.at[rows, cols]

    def rs_copy(j):
        zi = j // n_col
        half = n_dp // 2
        size = half - (zi + 1) // 2
        below = (1 - zi % 2) * ((zi + n_dp - 1) // n_dp)
        k = lax.rem(d + size * (1 - 2 * below) + n_dp, n_dp)
        q = lax.rem(c + (j + 1) % n_col, n_col)
        return pltpu.make_async_remote_copy(
            src_ref=piece(k, q),
            dst_ref=rs_buf.at[d, c],
            send_sem=rs_send.at[j],
            recv_sem=rs_recv.at[me],
            device_id=(k, r, q),
            device_id_type=MESH,
        )

    def ln_copy(j):
        peer = lax.rem(d + j, n_dp)
        return pltpu.make_async_remote_copy(
            src_ref=ln_ref,
            dst_ref=ln_buf.at[d],
            send_sem=ln_send.at[j],
            recv_sem=ln_recv.at[d],
            device_id=(peer, r, c),
            device_id_type=MESH,
        )

    def start_rs(j, carry):
        rs_copy(j).start()
        return carry

    def start_ln(j, carry):
        ln_copy(j).start()
        return carry

    lax.fori_loop(0, n - 1, start_rs, 0)
    lax.fori_loop(1, n_dp, start_ln, 0)
    rs_buf[d, c] = piece(d, c)[...]
    ln_buf[d] = ln_ref[...]

    def wait_rs(j, carry):
        src = lax.rem(me + j, n)
        pltpu.make_async_remote_copy(
            src_ref=piece(0, 0),
            dst_ref=rs_buf.at[src // n_col, src % n_col],
            send_sem=rs_send.at[j],
            recv_sem=rs_recv.at[src],
            device_id=(src // n_col, r, src % n_col),
            device_id_type=MESH,
        ).wait_recv()
        rs_copy(j - 1).wait_send()
        return carry

    lax.fori_loop(1, n, wait_rs, 0)
    def wait_ln(j, carry):
        src = lax.rem(d + j, n_dp)
        pltpu.make_async_remote_copy(
            src_ref=ln_ref,
            dst_ref=ln_buf.at[src],
            send_sem=ln_send.at[j],
            recv_sem=ln_recv.at[src],
            device_id=(src, r, c),
            device_id_type=MESH,
        ).wait_recv()
        ln_copy(j).wait_send()
        return carry

    lax.fori_loop(1, n_dp, wait_ln, 0)
    ln_out[...] = jnp.sum(ln_buf[...].astype(jnp.float32), axis=0)

    ag_buf[d] = jnp.sum(rs_buf[...].astype(jnp.float32), axis=0)

    def ag_copy(slot, j, peer):
        return pltpu.make_async_remote_copy(
            src_ref=ag_buf.at[slot],
            dst_ref=ag_buf.at[slot],
            send_sem=ag_send.at[j],
            recv_sem=ag_recv.at[slot],
            device_id=(peer, r, c),
            device_id_type=MESH,
        )

    def arrive(slot):
        ag_copy(slot, 0, slot).wait_recv()

    n_rc = n_row * n_col
    me_rc = r * n_col + c

    def n_copy(j, peer, slot):
        return pltpu.make_async_remote_copy(
            src_ref=nbuf.at[slot],
            dst_ref=nbuf.at[slot],
            send_sem=n_send.at[j],
            recv_sem=n_recv.at[slot],
            device_id=(d, peer // n_col, peer % n_col),
            device_id_type=MESH,
        )

    def p_copy(j, peer, slot):
        return pltpu.make_async_remote_copy(
            src_ref=pbuf.at[slot],
            dst_ref=pbuf.at[slot],
            send_sem=p_send.at[j],
            recv_sem=p_recv.at[slot],
            device_id=(peer, r, c),
            device_id_type=MESH,
        )

    reach = 3
    n_right = n_dp // 2
    n_left = n_dp - 1 - n_right
    sends = []
    waited = set()
    n_copies = []
    for leg in range(0, n_right, reach):
        for sign, span in ((1, n_right), (-1, n_left)):
            if leg >= span:
                continue
            back = (n_dp - sign * leg) % n_dp
            slot = lax.rem(d + back, n_dp)
            if leg:
                arrive(slot)
                waited.add(back)
            for hop in range(1, min(reach, span - leg) + 1):
                peer = lax.rem(d + (n_dp + sign * hop) % n_dp, n_dp)
                copy = ag_copy(slot, len(sends), peer)
                copy.start()
                sends.append(copy)
        if leg == 0:
            lg = ln_out[...]
            own = ag_buf[d]
            part = jnp.sum(own * own) + (d == 0).astype(jnp.float32) * (
                jnp.sum(lg * lg) / float(n_row)
            )
            nbuf[me_rc] = jnp.full(nbuf.shape[1:], part, jnp.float32)
            for j in range(1, n_rc):
                copy = n_copy(j, lax.rem(me_rc + j, n_rc), me_rc)
                copy.start()
                n_copies.append(copy)

    for j in range(1, n_rc):
        sender = lax.rem(me_rc + n_rc - j, n_rc)
        n_copy(j, sender, sender).wait_recv()
    for copy in n_copies:
        copy.wait_send()
    pbuf[d] = jnp.sum(nbuf[...], axis=0)
    p_copies = []
    for j in range(1, n_dp):
        copy = p_copy(j, lax.rem(d + j, n_dp), d)
        copy.start()
        p_copies.append(copy)
    for back in range(1, n_dp):
        if back not in waited:
            arrive(lax.rem(d + back, n_dp))
    for copy in sends:
        copy.wait_send()
    for j in range(1, n_dp):
        sender = lax.rem(d + n_dp - j, n_dp)
        p_copy(j, sender, sender).wait_recv()
    for copy in p_copies:
        copy.wait_send()
    norm_total = jnp.sum(pbuf[...], axis=0)[0:1, 0:1]
    for k in range(n_dp):
        for q in range(n_col):
            g_out[
                pl.ds((k // halves) * depth, depth),
                pl.ds(q * halves * width + (k % halves) * width, width),
            ] = ag_buf[k, q]
    finish_part(n_col, g_out, m_ref, f_ref, s_ref, c_out, b_out, norm_total,
                mbuf, rbuf, m_send, m_recv)


def reduce_blocks(block, ln_part, master, first, second, average):
    n_dp, n_row, n_col = lax.axis_size("dp"), lax.axis_size("row"), lax.axis_size("col")
    rows, cols = block.shape
    quarter = rows // n_col
    width = 128
    halves = cols // width
    depth = quarter * halves // n_dp
    n = n_row * n_col
    vmem = pl.BlockSpec(memory_space=pltpu.VMEM)
    return pl.pallas_call(
        functools.partial(reduce_kernel, n_dp, n_row, n_col),
        out_shape=(
            jax.ShapeDtypeStruct((quarter, cols * n_col), jnp.float32),
            jax.ShapeDtypeStruct(ln_part.shape, jnp.float32),
            jax.ShapeDtypeStruct((8, 128), jnp.float32),
            jax.ShapeDtypeStruct(average.shape, jnp.float32),
        ),
        in_specs=[vmem] * 5,
        out_specs=(vmem, vmem, vmem, vmem),
        scratch_shapes=[
            pltpu.VMEM((n_dp, n_col, depth, width), block.dtype),
            pltpu.VMEM((n_dp, n_col, depth, width), jnp.float32),
            pltpu.VMEM((n_dp,) + ln_part.shape, ln_part.dtype),
            pltpu.SemaphoreType.DMA((n_dp * n_col,)),
            pltpu.SemaphoreType.DMA((n_dp * n_col,)),
            pltpu.SemaphoreType.DMA((n_dp,)),
            pltpu.SemaphoreType.DMA((n_dp,)),
            pltpu.SemaphoreType.DMA((n_dp,)),
            pltpu.SemaphoreType.DMA((n_dp,)),
            pltpu.VMEM((n, 8, 128), jnp.float32),
            pltpu.VMEM((n_col, master.shape[0], average.shape[1]), jnp.float32),
            pltpu.VMEM((n_col, master.shape[0], average.shape[1]), jnp.float32),
            pltpu.SemaphoreType.DMA((n,)),
            pltpu.SemaphoreType.DMA((n,)),
            pltpu.SemaphoreType.DMA((n_col,)),
            pltpu.SemaphoreType.DMA((n_col,)),
            pltpu.VMEM((n_dp, 8, 128), jnp.float32),
            pltpu.SemaphoreType.DMA((n_dp,)),
            pltpu.SemaphoreType.DMA((n_dp,)),
        ],
        compiler_params=pltpu.CompilerParams(collective_id=1, has_side_effects=True),
    )(block, ln_part, master, first, second)


def apply_kernel(c_ref, g_ref, m_ref, f_ref, s_ref, a_ref, b_ref, lg_ref, lm_ref, lf_ref, ls_ref,
                 la_ref, a_out, m_out, f_out, s_out, lm_out, lf_out, ls_out, la_out,
                 flat, block, small, sems):
    clip_scale = c_ref[0:1, 0:1]
    master_new, first_new, second_new = adam_step(
        g_ref[...], clip_scale, f_ref[...], s_ref[...], m_ref[...], decay_rate
    )
    flat[0] = master_new
    flat[1] = first_new
    flat[2] = second_new
    copies = [
        pltpu.make_async_copy(flat.at[0], m_out, sems.at[0]),
        pltpu.make_async_copy(flat.at[1], f_out, sems.at[1]),
        pltpu.make_async_copy(flat.at[2], s_out, sems.at[2]),
    ]
    for copy in copies:
        copy.start()
    block[...] = ema_keep * a_ref[...] + (1.0 - ema_keep) * b_ref[...]
    copy = pltpu.make_async_copy(block, a_out, sems.at[3])
    copy.start()
    copies.append(copy)
    ln_master_new, ln_first_new, ln_second_new = adam_step(
        lg_ref[...], clip_scale, lf_ref[...], ls_ref[...], lm_ref[...], 0.0
    )
    small[0] = ln_master_new
    small[1] = ln_first_new
    small[2] = ln_second_new
    small[3] = ema_keep * la_ref[...] + (1.0 - ema_keep) * ln_master_new
    for i, out in enumerate((lm_out, lf_out, ls_out, la_out)):
        copy = pltpu.make_async_copy(small.at[i], out, sems.at[4 + i])
        copy.start()
        copies.append(copy)
    for copy in copies:
        copy.wait()


def apply_update(clip_tile, gradient, master, first, second, average, block_master,
                 ln_gradient, ln_master, ln_first, ln_second, ln_average):
    vmem = pl.BlockSpec(memory_space=pltpu.VMEM)
    anywhere = pl.BlockSpec(memory_space=pl.ANY)
    outs = (average, master, first, second, ln_master, ln_first, ln_second, ln_average)
    return pl.pallas_call(
        apply_kernel,
        out_shape=tuple(jax.ShapeDtypeStruct(x.shape, jnp.float32) for x in outs),
        in_specs=[vmem] * 12,
        out_specs=tuple([anywhere] * 8),
        scratch_shapes=[
            pltpu.VMEM((3,) + master.shape, jnp.float32),
            pltpu.VMEM(average.shape, jnp.float32),
            pltpu.VMEM((4,) + ln_master.shape, jnp.float32),
            pltpu.SemaphoreType.DMA((8,)),
        ],
    )(clip_tile, gradient, master, first, second, average, block_master,
      ln_gradient, ln_master, ln_first, ln_second, ln_average)


def shards(
    grad_blocks,
    ln_grads,
    master,
    first_moment,
    second_moment,
    average,
    ln_master,
    ln_first,
    ln_second,
    ln_average,
):
    gradient, ln_gradient, clip_tile, block_master = reduce_blocks(
        grad_blocks[0], ln_grads[0], master, first_moment, second_moment, average
    )
    (
        average_new,
        master_new,
        first_new,
        second_new,
        ln_master_new,
        ln_first_new,
        ln_second_new,
        ln_average_new,
    ) = apply_update(
        clip_tile, gradient, master, first_moment, second_moment, average, block_master,
        ln_gradient, ln_master, ln_first, ln_second, ln_average,
    )
    return (
        average_new,
        master_new,
        first_new,
        second_new,
        ln_master_new,
        ln_first_new,
        ln_second_new,
        ln_average_new,
    )


def solution(mesh):
    placed = (
        P("dp", "row", "col"),
        P("dp", None, "col"),
        P(("row", "col"), None),
        P(("row", "col"), None),
        P(("row", "col"), None),
        P("row", "col"),
        P(None, "col"),
        P(None, "col"),
        P(None, "col"),
        P(None, "col"),
    )
    return jax.shard_map(
        shards,
        mesh=mesh,
        in_specs=placed,
        out_specs=(
            P("row", "col"),
            P(("row", "col"), None),
            P(("row", "col"), None),
            P(("row", "col"), None),
            P(None, "col"),
            P(None, "col"),
            P(None, "col"),
            P(None, "col"),
        ),
        check_vma=False,
    )
```

```python
import functools
import math

import jax
import jax.numpy as jnp
from jax import lax
from jax.experimental import pallas as pl
from jax.experimental.pallas import tpu as pltpu
from jax.sharding import PartitionSpec as P

MESH = pl.DeviceIdType.MESH

D = 1024
FF = 4096
STEP = 20


beta_one = 0.9
beta_two = 0.95
learn_rate = 0.02
decay_rate = 0.1
epsilon = 1e-08
clip_rms = 1.0
ema_keep = 0.9


def adam_step(gradient, clip_scale, first, second, master, decay_weight):
    clipped = clip_scale * gradient
    first_new = beta_one * first + (1.0 - beta_one) * clipped
    second_new = beta_two * second + (1.0 - beta_two) * clipped * clipped
    direction = (
        first_new
        / (1.0 - beta_one**STEP)
        / (jnp.sqrt(second_new / (1.0 - beta_two**STEP)) + epsilon)
    )
    master_new = master - learn_rate * (direction + decay_weight * master)
    return (master_new, first_new, second_new)


def clip_factor(norm_total):
    return jnp.minimum(1.0, clip_rms * math.sqrt(FF * D + 4 * D) / jnp.sqrt(norm_total))


def squares(gradient, ln_gradient, row_count):
    return jnp.sum(gradient * gradient) + jnp.sum(ln_gradient * ln_gradient) / row_count


def finish_part(n_col, g_ref, m_ref, f_ref, s_ref, c_out, b_out, norm_total,
                mbuf, rbuf, m_send, m_recv):
    d = lax.axis_index("dp")
    r = lax.axis_index("row")
    c = lax.axis_index("col")
    clip_scale = clip_factor(norm_total)
    c_out[...] = jnp.broadcast_to(clip_scale, c_out.shape)
    width = b_out.shape[1]

    def chunk(peer):
        cols = pl.ds(pl.multiple_of(peer * width, width), width)
        master_new, _, _ = adam_step(
            g_ref[:, cols], clip_scale, f_ref[:, cols], s_ref[:, cols], m_ref[:, cols], decay_rate
        )
        return master_new

    def m_copy(j, peer, slot):
        return pltpu.make_async_remote_copy(
            src_ref=mbuf.at[peer],
            dst_ref=rbuf.at[slot],
            send_sem=m_send.at[j],
            recv_sem=m_recv.at[slot],
            device_id=(d, r, peer),
            device_id_type=MESH,
        )

    copies = []
    for j in range(1, n_col):
        peer = lax.rem(c + j, n_col)
        mbuf[peer] = chunk(peer)
        copy = m_copy(j, peer, c)
        copy.start()
        copies.append(copy)
    rbuf[c] = chunk(c)
    for j in range(1, n_col):
        sender = lax.rem(c + n_col - j, n_col)
        m_copy(j, sender, sender).wait_recv()
    for copy in copies:
        copy.wait_send()
    depth = rbuf.shape[1]
    for q in range(n_col):
        b_out[pl.ds(q * depth, depth), :] = rbuf[q]


def reduce_kernel(n_dp, n_row, n_col, g_ref, ln_ref, m_ref, f_ref, s_ref,
                  g_out, ln_out, c_out, b_out, rs_buf, ag_buf, ln_buf,
                  rs_send, rs_recv, ag_send, ag_recv, ln_send, ln_recv,
                  nbuf, mbuf, rbuf, n_send, n_recv, m_send, m_recv, pbuf, p_send, p_recv):
    d = lax.axis_index("dp")
    r = lax.axis_index("row")
    c = lax.axis_index("col")
    n = n_dp * n_col
    me = d * n_col + c
    quarter = g_ref.shape[0] // n_col
    depth = rs_buf.shape[2]
    width = rs_buf.shape[3]
    halves = g_ref.shape[1] // width
    barrier = pltpu.get_barrier_semaphore()

    def greet(j, carry):
        peer = lax.rem(me + j, n)
        pl.semaphore_signal(
            barrier, inc=1, device_id=(peer // n_col, r, peer % n_col), device_id_type=MESH
        )
        return carry

    lax.fori_loop(1, n, greet, 0)

    def greet_row(j, carry):
        peer = lax.rem(r + 1 + j // n_col, n_row)
        pl.semaphore_signal(
            barrier, inc=1, device_id=(d, peer, j % n_col), device_id_type=MESH
        )
        return carry

    lax.fori_loop(0, (n_row - 1) * n_col, greet_row, 0)

    def piece(k, q):
        rows = pl.ds(pl.multiple_of(q * quarter + (k // halves) * depth, depth), depth)
        cols = pl.ds(pl.multiple_of((k % halves) * width, width), width)
        return g_ref.at[rows, cols]

    def rs_copy(j):
        peer = lax.rem(me + j, n)
        return pltpu.make_async_remote_copy(
            src_ref=piece(peer // n_col, peer % n_col),
            dst_ref=rs_buf.at[d, c],
            send_sem=rs_send.at[j],
            recv_sem=rs_recv.at[me],
            device_id=(peer // n_col, r, peer % n_col),
            device_id_type=MESH,
        )

    def ln_copy(j):
        peer = lax.rem(d + j, n_dp)
        return pltpu.make_async_remote_copy(
            src_ref=ln_ref,
            dst_ref=ln_buf.at[d],
            send_sem=ln_send.at[j],
            recv_sem=ln_recv.at[d],
            device_id=(peer, r, c),
            device_id_type=MESH,
        )

    def start_rs(j, carry):
        rs_copy(j).start()
        return carry

    def start_ln(j, carry):
        ln_copy(j).start()
        return carry

    rs_buf[d, c] = piece(d, c)[...]
    ln_buf[d] = ln_ref[...]
    pl.semaphore_wait(barrier, n - 1 + (n_row - 1) * n_col)
    lax.fori_loop(1, n_dp, start_ln, 0)
    lax.fori_loop(1, n, start_rs, 0)

    def wait_rs(j, carry):
        src = lax.rem(me + j, n)
        pltpu.make_async_remote_copy(
            src_ref=piece(0, 0),
            dst_ref=rs_buf.at[src // n_col, src % n_col],
            send_sem=rs_send.at[j],
            recv_sem=rs_recv.at[src],
            device_id=(src // n_col, r, src % n_col),
            device_id_type=MESH,
        ).wait_recv()
        rs_copy(j).wait_send()
        return carry

    lax.fori_loop(1, n, wait_rs, 0)
    def wait_ln(j, carry):
        src = lax.rem(d + j, n_dp)
        pltpu.make_async_remote_copy(
            src_ref=ln_ref,
            dst_ref=ln_buf.at[src],
            send_sem=ln_send.at[j],
            recv_sem=ln_recv.at[src],
            device_id=(src, r, c),
            device_id_type=MESH,
        ).wait_recv()
        ln_copy(j).wait_send()
        return carry

    lax.fori_loop(1, n_dp, wait_ln, 0)
    ln_out[...] = jnp.sum(ln_buf[...].astype(jnp.float32), axis=0)

    ag_buf[d] = jnp.sum(rs_buf[...].astype(jnp.float32), axis=0)

    def ag_copy(slot, j, peer):
        return pltpu.make_async_remote_copy(
            src_ref=ag_buf.at[slot],
            dst_ref=ag_buf.at[slot],
            send_sem=ag_send.at[j],
            recv_sem=ag_recv.at[slot],
            device_id=(peer, r, c),
            device_id_type=MESH,
        )

    def arrive(slot):
        ag_copy(slot, 0, slot).wait_recv()

    n_rc = n_row * n_col
    me_rc = r * n_col + c

    def n_copy(j, peer, slot):
        return pltpu.make_async_remote_copy(
            src_ref=nbuf.at[slot],
            dst_ref=nbuf.at[slot],
            send_sem=n_send.at[j],
            recv_sem=n_recv.at[slot],
            device_id=(d, peer // n_col, peer % n_col),
            device_id_type=MESH,
        )

    def p_copy(j, peer, slot):
        return pltpu.make_async_remote_copy(
            src_ref=pbuf.at[slot],
            dst_ref=pbuf.at[slot],
            send_sem=p_send.at[j],
            recv_sem=p_recv.at[slot],
            device_id=(peer, r, c),
            device_id_type=MESH,
        )

    reach = 3
    n_right = n_dp // 2
    n_left = n_dp - 1 - n_right
    sends = []
    waited = set()
    n_copies = []
    for leg in range(0, n_right, reach):
        for sign, span in ((1, n_right), (-1, n_left)):
            if leg >= span:
                continue
            back = (n_dp - sign * leg) % n_dp
            slot = lax.rem(d + back, n_dp)
            if leg:
                arrive(slot)
                waited.add(back)
            for hop in range(1, min(reach, span - leg) + 1):
                peer = lax.rem(d + (n_dp + sign * hop) % n_dp, n_dp)
                copy = ag_copy(slot, len(sends), peer)
                copy.start()
                sends.append(copy)
        if leg == 0:
            lg = ln_out[...]
            own = ag_buf[d]
            part = jnp.sum(own * own) + (d == 0).astype(jnp.float32) * (
                jnp.sum(lg * lg) / float(n_row)
            )
            nbuf[me_rc] = jnp.full(nbuf.shape[1:], part, jnp.float32)
            for j in range(1, n_rc):
                copy = n_copy(j, lax.rem(me_rc + j, n_rc), me_rc)
                copy.start()
                n_copies.append(copy)

    for j in range(1, n_rc):
        sender = lax.rem(me_rc + n_rc - j, n_rc)
        n_copy(j, sender, sender).wait_recv()
    for copy in n_copies:
        copy.wait_send()
    pbuf[d] = jnp.sum(nbuf[...], axis=0)
    p_copies = []
    for j in range(1, n_dp):
        copy = p_copy(j, lax.rem(d + j, n_dp), d)
        copy.start()
        p_copies.append(copy)
    for back in range(1, n_dp):
        if back not in waited:
            arrive(lax.rem(d + back, n_dp))
    for copy in sends:
        copy.wait_send()
    for j in range(1, n_dp):
        sender = lax.rem(d + n_dp - j, n_dp)
        p_copy(j, sender, sender).wait_recv()
    for copy in p_copies:
        copy.wait_send()
    norm_total = jnp.sum(pbuf[...], axis=0)[0:1, 0:1]
    for k in range(n_dp):
        for q in range(n_col):
            g_out[
                pl.ds((k // halves) * depth, depth),
                pl.ds(q * halves * width + (k % halves) * width, width),
            ] = ag_buf[k, q]
    finish_part(n_col, g_out, m_ref, f_ref, s_ref, c_out, b_out, norm_total,
                mbuf, rbuf, m_send, m_recv)


def reduce_blocks(block, ln_part, master, first, second, average):
    n_dp, n_row, n_col = lax.axis_size("dp"), lax.axis_size("row"), lax.axis_size("col")
    rows, cols = block.shape
    quarter = rows // n_col
    width = 128
    halves = cols // width
    depth = quarter * halves // n_dp
    n = n_row * n_col
    vmem = pl.BlockSpec(memory_space=pltpu.VMEM)
    return pl.pallas_call(
        functools.partial(reduce_kernel, n_dp, n_row, n_col),
        out_shape=(
            jax.ShapeDtypeStruct((quarter, cols * n_col), jnp.float32),
            jax.ShapeDtypeStruct(ln_part.shape, jnp.float32),
            jax.ShapeDtypeStruct((8, 128), jnp.float32),
            jax.ShapeDtypeStruct(average.shape, jnp.float32),
        ),
        in_specs=[vmem] * 5,
        out_specs=(vmem, vmem, vmem, vmem),
        scratch_shapes=[
            pltpu.VMEM((n_dp, n_col, depth, width), block.dtype),
            pltpu.VMEM((n_dp, n_col, depth, width), jnp.float32),
            pltpu.VMEM((n_dp,) + ln_part.shape, ln_part.dtype),
            pltpu.SemaphoreType.DMA((n_dp * n_col,)),
            pltpu.SemaphoreType.DMA((n_dp * n_col,)),
            pltpu.SemaphoreType.DMA((n_dp,)),
            pltpu.SemaphoreType.DMA((n_dp,)),
            pltpu.SemaphoreType.DMA((n_dp,)),
            pltpu.SemaphoreType.DMA((n_dp,)),
            pltpu.VMEM((n, 8, 128), jnp.float32),
            pltpu.VMEM((n_col, master.shape[0], average.shape[1]), jnp.float32),
            pltpu.VMEM((n_col, master.shape[0], average.shape[1]), jnp.float32),
            pltpu.SemaphoreType.DMA((n,)),
            pltpu.SemaphoreType.DMA((n,)),
            pltpu.SemaphoreType.DMA((n_col,)),
            pltpu.SemaphoreType.DMA((n_col,)),
            pltpu.VMEM((n_dp, 8, 128), jnp.float32),
            pltpu.SemaphoreType.DMA((n_dp,)),
            pltpu.SemaphoreType.DMA((n_dp,)),
        ],
        compiler_params=pltpu.CompilerParams(collective_id=1, has_side_effects=True),
    )(block, ln_part, master, first, second)


def apply_kernel(c_ref, g_ref, m_ref, f_ref, s_ref, a_ref, b_ref, lg_ref, lm_ref, lf_ref, ls_ref,
                 la_ref, a_out, m_out, f_out, s_out, lm_out, lf_out, ls_out, la_out,
                 flat, block, small, sems):
    clip_scale = c_ref[0:1, 0:1]
    master_new, first_new, second_new = adam_step(
        g_ref[...], clip_scale, f_ref[...], s_ref[...], m_ref[...], decay_rate
    )
    flat[0] = master_new
    flat[1] = first_new
    flat[2] = second_new
    copies = [
        pltpu.make_async_copy(flat.at[0], m_out, sems.at[0]),
        pltpu.make_async_copy(flat.at[1], f_out, sems.at[1]),
        pltpu.make_async_copy(flat.at[2], s_out, sems.at[2]),
    ]
    for copy in copies:
        copy.start()
    block[...] = ema_keep * a_ref[...] + (1.0 - ema_keep) * b_ref[...]
    copy = pltpu.make_async_copy(block, a_out, sems.at[3])
    copy.start()
    copies.append(copy)
    ln_master_new, ln_first_new, ln_second_new = adam_step(
        lg_ref[...], clip_scale, lf_ref[...], ls_ref[...], lm_ref[...], 0.0
    )
    small[0] = ln_master_new
    small[1] = ln_first_new
    small[2] = ln_second_new
    small[3] = ema_keep * la_ref[...] + (1.0 - ema_keep) * ln_master_new
    for i, out in enumerate((lm_out, lf_out, ls_out, la_out)):
        copy = pltpu.make_async_copy(small.at[i], out, sems.at[4 + i])
        copy.start()
        copies.append(copy)
    for copy in copies:
        copy.wait()


def apply_update(clip_tile, gradient, master, first, second, average, block_master,
                 ln_gradient, ln_master, ln_first, ln_second, ln_average):
    vmem = pl.BlockSpec(memory_space=pltpu.VMEM)
    anywhere = pl.BlockSpec(memory_space=pl.ANY)
    outs = (average, master, first, second, ln_master, ln_first, ln_second, ln_average)
    return pl.pallas_call(
        apply_kernel,
        out_shape=tuple(jax.ShapeDtypeStruct(x.shape, jnp.float32) for x in outs),
        in_specs=[vmem] * 12,
        out_specs=tuple([anywhere] * 8),
        scratch_shapes=[
            pltpu.VMEM((3,) + master.shape, jnp.float32),
            pltpu.VMEM(average.shape, jnp.float32),
            pltpu.VMEM((4,) + ln_master.shape, jnp.float32),
            pltpu.SemaphoreType.DMA((8,)),
        ],
    )(clip_tile, gradient, master, first, second, average, block_master,
      ln_gradient, ln_master, ln_first, ln_second, ln_average)


def shards(
    grad_blocks,
    ln_grads,
    master,
    first_moment,
    second_moment,
    average,
    ln_master,
    ln_first,
    ln_second,
    ln_average,
):
    gradient, ln_gradient, clip_tile, block_master = reduce_blocks(
        grad_blocks[0], ln_grads[0], master, first_moment, second_moment, average
    )
    (
        average_new,
        master_new,
        first_new,
        second_new,
        ln_master_new,
        ln_first_new,
        ln_second_new,
        ln_average_new,
    ) = apply_update(
        clip_tile, gradient, master, first_moment, second_moment, average, block_master,
        ln_gradient, ln_master, ln_first, ln_second, ln_average,
    )
    return (
        average_new,
        master_new,
        first_new,
        second_new,
        ln_master_new,
        ln_first_new,
        ln_second_new,
        ln_average_new,
    )


def solution(mesh):
    placed = (
        P("dp", "row", "col"),
        P("dp", None, "col"),
        P(("row", "col"), None),
        P(("row", "col"), None),
        P(("row", "col"), None),
        P("row", "col"),
        P(None, "col"),
        P(None, "col"),
        P(None, "col"),
        P(None, "col"),
    )
    return jax.shard_map(
        shards,
        mesh=mesh,
        in_specs=placed,
        out_specs=(
            P("row", "col"),
            P(("row", "col"), None),
            P(("row", "col"), None),
            P(("row", "col"), None),
            P(None, "col"),
            P(None, "col"),
            P(None, "col"),
            P(None, "col"),
        ),
        check_vma=False,
    )
```

```python
import functools
import math

import jax
import jax.numpy as jnp
from jax import lax
from jax.experimental import pallas as pl
from jax.experimental.pallas import tpu as pltpu
from jax.sharding import PartitionSpec as P

MESH = pl.DeviceIdType.MESH

D = 1024
FF = 4096
STEP = 20


beta_one = 0.9
beta_two = 0.95
learn_rate = 0.02
decay_rate = 0.1
epsilon = 1e-08
clip_rms = 1.0
ema_keep = 0.9


def adam_step(gradient, clip_scale, first, second, master, decay_weight):
    clipped = clip_scale * gradient
    first_new = beta_one * first + (1.0 - beta_one) * clipped
    second_new = beta_two * second + (1.0 - beta_two) * clipped * clipped
    direction = (
        first_new
        / (1.0 - beta_one**STEP)
        / (jnp.sqrt(second_new / (1.0 - beta_two**STEP)) + epsilon)
    )
    master_new = master - learn_rate * (direction + decay_weight * master)
    return (master_new, first_new, second_new)


def clip_factor(norm_total):
    return jnp.minimum(1.0, clip_rms * math.sqrt(FF * D + 4 * D) / jnp.sqrt(norm_total))


def squares(gradient, ln_gradient, row_count):
    return jnp.sum(gradient * gradient) + jnp.sum(ln_gradient * ln_gradient) / row_count


def finish_part(n_col, g_ref, m_ref, f_ref, s_ref, c_out, b_out, norm_total,
                mbuf, rbuf, m_send, m_recv):
    d = lax.axis_index("dp")
    r = lax.axis_index("row")
    c = lax.axis_index("col")
    clip_scale = clip_factor(norm_total)
    c_out[...] = jnp.broadcast_to(clip_scale, c_out.shape)
    width = b_out.shape[1]

    def chunk(peer):
        cols = pl.ds(pl.multiple_of(peer * width, width), width)
        master_new, _, _ = adam_step(
            g_ref[:, cols], clip_scale, f_ref[:, cols], s_ref[:, cols], m_ref[:, cols], decay_rate
        )
        return master_new

    def m_copy(j, peer, slot):
        return pltpu.make_async_remote_copy(
            src_ref=mbuf.at[peer],
            dst_ref=rbuf.at[slot],
            send_sem=m_send.at[j],
            recv_sem=m_recv.at[slot],
            device_id=(d, r, peer),
            device_id_type=MESH,
        )

    copies = []
    for j in range(1, n_col):
        peer = lax.rem(c + j, n_col)
        mbuf[peer] = chunk(peer)
        copy = m_copy(j, peer, c)
        copy.start()
        copies.append(copy)
    rbuf[c] = chunk(c)
    for j in range(1, n_col):
        sender = lax.rem(c + n_col - j, n_col)
        m_copy(j, sender, sender).wait_recv()
    for copy in copies:
        copy.wait_send()
    depth = rbuf.shape[1]
    for q in range(n_col):
        b_out[pl.ds(q * depth, depth), :] = rbuf[q]


def reduce_kernel(n_dp, n_row, n_col, g_ref, ln_ref, m_ref, f_ref, s_ref,
                  g_out, ln_out, c_out, b_out, rs_buf, ag_buf, ln_buf,
                  rs_send, rs_recv, ag_send, ag_recv, ln_send, ln_recv,
                  nbuf, mbuf, rbuf, n_send, n_recv, m_send, m_recv, pbuf, p_send, p_recv):
    d = lax.axis_index("dp")
    r = lax.axis_index("row")
    c = lax.axis_index("col")
    n = n_dp * n_col
    me = d * n_col + c
    quarter = g_ref.shape[0] // n_col
    depth = rs_buf.shape[2]
    width = rs_buf.shape[3]
    halves = g_ref.shape[1] // width
    barrier = pltpu.get_barrier_semaphore()

    def greet(j, carry):
        peer = lax.rem(me + j, n)
        pl.semaphore_signal(
            barrier, inc=1, device_id=(peer // n_col, r, peer % n_col), device_id_type=MESH
        )
        return carry

    lax.fori_loop(1, n, greet, 0)

    def greet_row(j, carry):
        peer = lax.rem(r + 1 + j // n_col, n_row)
        pl.semaphore_signal(
            barrier, inc=1, device_id=(d, peer, j % n_col), device_id_type=MESH
        )
        return carry

    lax.fori_loop(0, (n_row - 1) * n_col, greet_row, 0)
    pl.semaphore_wait(barrier, n - 1 + (n_row - 1) * n_col)

    def piece(k, q):
        rows = pl.ds(pl.multiple_of(q * quarter + (k // halves) * depth, depth), depth)
        cols = pl.ds(pl.multiple_of((k % halves) * width, width), width)
        return g_ref.at[rows, cols]

    def rs_copy(j):
        peer = lax.rem(me + j, n)
        return pltpu.make_async_remote_copy(
            src_ref=piece(peer // n_col, peer % n_col),
            dst_ref=rs_buf.at[d, c],
            send_sem=rs_send.at[j],
            recv_sem=rs_recv.at[me],
            device_id=(peer // n_col, r, peer % n_col),
            device_id_type=MESH,
        )

    def ln_copy(j):
        peer = lax.rem(d + j, n_dp)
        return pltpu.make_async_remote_copy(
            src_ref=ln_ref,
            dst_ref=ln_buf.at[d],
            send_sem=ln_send.at[j],
            recv_sem=ln_recv.at[d],
            device_id=(peer, r, c),
            device_id_type=MESH,
        )

    def start_rs(j, carry):
        rs_copy(j).start()
        return carry

    def start_ln(j, carry):
        ln_copy(j).start()
        return carry

    lax.fori_loop(1, n, start_rs, 0)
    lax.fori_loop(1, n_dp, start_ln, 0)
    rs_buf[d, c] = piece(d, c)[...]
    ln_buf[d] = ln_ref[...]

    def wait_rs(j, carry):
        src = lax.rem(me + j, n)
        pltpu.make_async_remote_copy(
            src_ref=piece(0, 0),
            dst_ref=rs_buf.at[src // n_col, src % n_col],
            send_sem=rs_send.at[j],
            recv_sem=rs_recv.at[src],
            device_id=(src // n_col, r, src % n_col),
            device_id_type=MESH,
        ).wait_recv()
        rs_copy(j).wait_send()
        return carry

    lax.fori_loop(1, n, wait_rs, 0)
    def wait_ln(j, carry):
        src = lax.rem(d + j, n_dp)
        pltpu.make_async_remote_copy(
            src_ref=ln_ref,
            dst_ref=ln_buf.at[src],
            send_sem=ln_send.at[j],
            recv_sem=ln_recv.at[src],
            device_id=(src, r, c),
            device_id_type=MESH,
        ).wait_recv()
        ln_copy(j).wait_send()
        return carry

    lax.fori_loop(1, n_dp, wait_ln, 0)
    ln_out[...] = jnp.sum(ln_buf[...].astype(jnp.float32), axis=0)

    ag_buf[d] = jnp.sum(rs_buf[...].astype(jnp.float32), axis=0)

    def ag_copy(slot, j, peer):
        return pltpu.make_async_remote_copy(
            src_ref=ag_buf.at[slot],
            dst_ref=ag_buf.at[slot],
            send_sem=ag_send.at[j],
            recv_sem=ag_recv.at[slot],
            device_id=(peer, r, c),
            device_id_type=MESH,
        )

    def arrive(slot):
        ag_copy(slot, 0, slot).wait_recv()

    n_rc = n_row * n_col
    me_rc = r * n_col + c

    def n_copy(j, peer, slot):
        return pltpu.make_async_remote_copy(
            src_ref=nbuf.at[slot],
            dst_ref=nbuf.at[slot],
            send_sem=n_send.at[j],
            recv_sem=n_recv.at[slot],
            device_id=(d, peer // n_col, peer % n_col),
            device_id_type=MESH,
        )

    def p_copy(j, peer, slot):
        return pltpu.make_async_remote_copy(
            src_ref=pbuf.at[slot],
            dst_ref=pbuf.at[slot],
            send_sem=p_send.at[j],
            recv_sem=p_recv.at[slot],
            device_id=(peer, r, c),
            device_id_type=MESH,
        )

    reach = 3
    n_right = n_dp // 2
    n_left = n_dp - 1 - n_right
    sends = []
    waited = set()
    n_copies = []
    for leg in range(0, n_right, reach):
        for sign, span in ((1, n_right), (-1, n_left)):
            if leg >= span:
                continue
            back = (n_dp - sign * leg) % n_dp
            slot = lax.rem(d + back, n_dp)
            if leg:
                arrive(slot)
                waited.add(back)
            for hop in range(1, min(reach, span - leg) + 1):
                peer = lax.rem(d + (n_dp + sign * hop) % n_dp, n_dp)
                copy = ag_copy(slot, len(sends), peer)
                copy.start()
                sends.append(copy)
        if leg == 0:
            lg = ln_out[...]
            own = ag_buf[d]
            part = jnp.sum(own * own) + (d == 0).astype(jnp.float32) * (
                jnp.sum(lg * lg) / float(n_row)
            )
            nbuf[me_rc] = jnp.full(nbuf.shape[1:], part, jnp.float32)
            for j in range(1, n_rc):
                copy = n_copy(j, lax.rem(me_rc + j, n_rc), me_rc)
                copy.start()
                n_copies.append(copy)

    for j in range(1, n_rc):
        sender = lax.rem(me_rc + n_rc - j, n_rc)
        n_copy(j, sender, sender).wait_recv()
    for copy in n_copies:
        copy.wait_send()
    pbuf[d] = jnp.sum(nbuf[...], axis=0)
    p_copies = []
    for j in range(1, n_dp):
        copy = p_copy(j, lax.rem(d + j, n_dp), d)
        copy.start()
        p_copies.append(copy)
    for back in range(1, n_dp):
        if back not in waited:
            arrive(lax.rem(d + back, n_dp))
    for copy in sends:
        copy.wait_send()
    for j in range(1, n_dp):
        sender = lax.rem(d + n_dp - j, n_dp)
        p_copy(j, sender, sender).wait_recv()
    for copy in p_copies:
        copy.wait_send()
    norm_total = jnp.sum(pbuf[...], axis=0)[0:1, 0:1]
    for k in range(n_dp):
        for q in range(n_col):
            g_out[
                pl.ds((k // halves) * depth, depth),
                pl.ds(q * halves * width + (k % halves) * width, width),
            ] = ag_buf[k, q]
    finish_part(n_col, g_out, m_ref, f_ref, s_ref, c_out, b_out, norm_total,
                mbuf, rbuf, m_send, m_recv)


def reduce_blocks(block, ln_part, master, first, second, average):
    n_dp, n_row, n_col = lax.axis_size("dp"), lax.axis_size("row"), lax.axis_size("col")
    rows, cols = block.shape
    quarter = rows // n_col
    width = 128
    halves = cols // width
    depth = quarter * halves // n_dp
    n = n_row * n_col
    vmem = pl.BlockSpec(memory_space=pltpu.VMEM)
    return pl.pallas_call(
        functools.partial(reduce_kernel, n_dp, n_row, n_col),
        out_shape=(
            jax.ShapeDtypeStruct((quarter, cols * n_col), jnp.float32),
            jax.ShapeDtypeStruct(ln_part.shape, jnp.float32),
            jax.ShapeDtypeStruct((8, 128), jnp.float32),
            jax.ShapeDtypeStruct(average.shape, jnp.float32),
        ),
        in_specs=[vmem] * 5,
        out_specs=(vmem, vmem, vmem, vmem),
        scratch_shapes=[
            pltpu.VMEM((n_dp, n_col, depth, width), block.dtype),
            pltpu.VMEM((n_dp, n_col, depth, width), jnp.float32),
            pltpu.VMEM((n_dp,) + ln_part.shape, ln_part.dtype),
            pltpu.SemaphoreType.DMA((n_dp * n_col,)),
            pltpu.SemaphoreType.DMA((n_dp * n_col,)),
            pltpu.SemaphoreType.DMA((n_dp,)),
            pltpu.SemaphoreType.DMA((n_dp,)),
            pltpu.SemaphoreType.DMA((n_dp,)),
            pltpu.SemaphoreType.DMA((n_dp,)),
            pltpu.VMEM((n, 8, 128), jnp.float32),
            pltpu.VMEM((n_col, master.shape[0], average.shape[1]), jnp.float32),
            pltpu.VMEM((n_col, master.shape[0], average.shape[1]), jnp.float32),
            pltpu.SemaphoreType.DMA((n,)),
            pltpu.SemaphoreType.DMA((n,)),
            pltpu.SemaphoreType.DMA((n_col,)),
            pltpu.SemaphoreType.DMA((n_col,)),
            pltpu.VMEM((n_dp, 8, 128), jnp.float32),
            pltpu.SemaphoreType.DMA((n_dp,)),
            pltpu.SemaphoreType.DMA((n_dp,)),
        ],
        compiler_params=pltpu.CompilerParams(collective_id=1, has_side_effects=True),
    )(block, ln_part, master, first, second)


def apply_kernel(c_ref, g_ref, m_ref, f_ref, s_ref, a_ref, b_ref, lg_ref, lm_ref, lf_ref, ls_ref,
                 la_ref, a_out, m_out, f_out, s_out, lm_out, lf_out, ls_out, la_out):
    clip_scale = c_ref[0:1, 0:1]
    master_new, first_new, second_new = adam_step(
        g_ref[...], clip_scale, f_ref[...], s_ref[...], m_ref[...], decay_rate
    )
    m_out[...] = master_new
    f_out[...] = first_new
    s_out[...] = second_new
    a_out[...] = ema_keep * a_ref[...] + (1.0 - ema_keep) * b_ref[...]
    ln_master_new, ln_first_new, ln_second_new = adam_step(
        lg_ref[...], clip_scale, lf_ref[...], ls_ref[...], lm_ref[...], 0.0
    )
    lm_out[...] = ln_master_new
    lf_out[...] = ln_first_new
    ls_out[...] = ln_second_new
    la_out[...] = ema_keep * la_ref[...] + (1.0 - ema_keep) * ln_master_new


def apply_update(clip_tile, gradient, master, first, second, average, block_master,
                 ln_gradient, ln_master, ln_first, ln_second, ln_average):
    steps = 4
    flat = pl.BlockSpec((master.shape[0] // steps, master.shape[1]), lambda i: (i, 0))
    block = pl.BlockSpec((average.shape[0] // steps, average.shape[1]), lambda i: (i, 0))
    whole = pl.BlockSpec(clip_tile.shape, lambda i: (0, 0))
    small = pl.BlockSpec(ln_master.shape, lambda i: (0, 0))
    outs = (average, master, first, second, ln_master, ln_first, ln_second, ln_average)
    return pl.pallas_call(
        apply_kernel,
        out_shape=tuple(jax.ShapeDtypeStruct(x.shape, jnp.float32) for x in outs),
        grid=(steps,),
        in_specs=[whole, flat, flat, flat, flat, block, block, small, small, small, small, small],
        out_specs=(block, flat, flat, flat, small, small, small, small),
    )(clip_tile, gradient, master, first, second, average, block_master,
      ln_gradient, ln_master, ln_first, ln_second, ln_average)


def shards(
    grad_blocks,
    ln_grads,
    master,
    first_moment,
    second_moment,
    average,
    ln_master,
    ln_first,
    ln_second,
    ln_average,
):
    gradient, ln_gradient, clip_tile, block_master = reduce_blocks(
        grad_blocks[0], ln_grads[0], master, first_moment, second_moment, average
    )
    (
        average_new,
        master_new,
        first_new,
        second_new,
        ln_master_new,
        ln_first_new,
        ln_second_new,
        ln_average_new,
    ) = apply_update(
        clip_tile, gradient, master, first_moment, second_moment, average, block_master,
        ln_gradient, ln_master, ln_first, ln_second, ln_average,
    )
    return (
        average_new,
        master_new,
        first_new,
        second_new,
        ln_master_new,
        ln_first_new,
        ln_second_new,
        ln_average_new,
    )


def solution(mesh):
    placed = (
        P("dp", "row", "col"),
        P("dp", None, "col"),
        P(("row", "col"), None),
        P(("row", "col"), None),
        P(("row", "col"), None),
        P("row", "col"),
        P(None, "col"),
        P(None, "col"),
        P(None, "col"),
        P(None, "col"),
    )
    return jax.shard_map(
        shards,
        mesh=mesh,
        in_specs=placed,
        out_specs=(
            P("row", "col"),
            P(("row", "col"), None),
            P(("row", "col"), None),
            P(("row", "col"), None),
            P(None, "col"),
            P(None, "col"),
            P(None, "col"),
            P(None, "col"),
        ),
        check_vma=False,
    )
```

```python
import functools
import math

import jax
import jax.numpy as jnp
from jax import lax
from jax.experimental import pallas as pl
from jax.experimental.pallas import tpu as pltpu
from jax.sharding import PartitionSpec as P

MESH = pl.DeviceIdType.MESH

D = 1024
FF = 4096
STEP = 20


beta_one = 0.9
beta_two = 0.95
learn_rate = 0.02
decay_rate = 0.1
epsilon = 1e-08
clip_rms = 1.0
ema_keep = 0.9


def adam_step(gradient, clip_scale, first, second, master, decay_weight):
    clipped = clip_scale * gradient
    first_new = beta_one * first + (1.0 - beta_one) * clipped
    second_new = beta_two * second + (1.0 - beta_two) * clipped * clipped
    direction = (
        first_new
        / (1.0 - beta_one**STEP)
        / (jnp.sqrt(second_new / (1.0 - beta_two**STEP)) + epsilon)
    )
    master_new = master - learn_rate * (direction + decay_weight * master)
    return (master_new, first_new, second_new)


def clip_factor(norm_total):
    return jnp.minimum(1.0, clip_rms * math.sqrt(FF * D + 4 * D) / jnp.sqrt(norm_total))


def squares(gradient, ln_gradient, row_count):
    return jnp.sum(gradient * gradient) + jnp.sum(ln_gradient * ln_gradient) / row_count


def finish_part(n_col, g_ref, m_ref, f_ref, s_ref, c_out, b_out, norm_total,
                mbuf, rbuf, m_send, m_recv):
    d = lax.axis_index("dp")
    r = lax.axis_index("row")
    c = lax.axis_index("col")
    clip_scale = clip_factor(norm_total)
    c_out[...] = jnp.broadcast_to(clip_scale, c_out.shape)
    width = b_out.shape[1]

    def chunk(peer):
        cols = pl.ds(pl.multiple_of(peer * width, width), width)
        master_new, _, _ = adam_step(
            g_ref[:, cols], clip_scale, f_ref[:, cols], s_ref[:, cols], m_ref[:, cols], decay_rate
        )
        return master_new

    def m_copy(j, peer, slot):
        return pltpu.make_async_remote_copy(
            src_ref=mbuf.at[peer],
            dst_ref=rbuf.at[slot],
            send_sem=m_send.at[j],
            recv_sem=m_recv.at[slot],
            device_id=(d, r, peer),
            device_id_type=MESH,
        )

    copies = []
    for j in range(1, n_col):
        peer = lax.rem(c + j, n_col)
        mbuf[peer] = chunk(peer)
        copy = m_copy(j, peer, c)
        copy.start()
        copies.append(copy)
    rbuf[c] = chunk(c)
    for j in range(1, n_col):
        sender = lax.rem(c + n_col - j, n_col)
        m_copy(j, sender, sender).wait_recv()
    for copy in copies:
        copy.wait_send()
    depth = rbuf.shape[1]
    for q in range(n_col):
        b_out[pl.ds(q * depth, depth), :] = rbuf[q]


def reduce_kernel(n_dp, n_row, n_col, g_ref, ln_ref, m_ref, f_ref, s_ref,
                  g_out, ln_out, c_out, b_out, rs_buf, ag_buf, ln_buf,
                  rs_send, rs_recv, ag_send, ag_recv, ln_send, ln_recv,
                  nbuf, mbuf, rbuf, n_send, n_recv, m_send, m_recv, pbuf, p_send, p_recv):
    d = lax.axis_index("dp")
    r = lax.axis_index("row")
    c = lax.axis_index("col")
    n = n_dp * n_col
    me = d * n_col + c
    quarter = g_ref.shape[0] // n_col
    depth = rs_buf.shape[2]
    width = rs_buf.shape[3]
    halves = g_ref.shape[1] // width
    barrier = pltpu.get_barrier_semaphore()

    def greet(j, carry):
        peer = lax.rem(me + j, n)
        pl.semaphore_signal(
            barrier, inc=1, device_id=(peer // n_col, r, peer % n_col), device_id_type=MESH
        )
        return carry

    lax.fori_loop(1, n, greet, 0)

    def greet_row(j, carry):
        peer = lax.rem(r + 1 + j, n_row)
        pl.semaphore_signal(barrier, inc=1, device_id=(d, peer, c), device_id_type=MESH)
        return carry

    lax.fori_loop(0, n_row - 1, greet_row, 0)
    pl.semaphore_wait(barrier, n - 1 + n_row - 1)

    def piece(k, q):
        rows = pl.ds(pl.multiple_of(q * quarter + (k // halves) * depth, depth), depth)
        cols = pl.ds(pl.multiple_of((k % halves) * width, width), width)
        return g_ref.at[rows, cols]

    def rs_copy(j):
        peer = lax.rem(me + j, n)
        return pltpu.make_async_remote_copy(
            src_ref=piece(peer // n_col, peer % n_col),
            dst_ref=rs_buf.at[d, c],
            send_sem=rs_send.at[j],
            recv_sem=rs_recv.at[me],
            device_id=(peer // n_col, r, peer % n_col),
            device_id_type=MESH,
        )

    def ln_copy(j):
        peer = lax.rem(d + j, n_dp)
        return pltpu.make_async_remote_copy(
            src_ref=ln_ref,
            dst_ref=ln_buf.at[d],
            send_sem=ln_send.at[j],
            recv_sem=ln_recv.at[d],
            device_id=(peer, r, c),
            device_id_type=MESH,
        )

    def start_rs(j, carry):
        rs_copy(j).start()
        return carry

    def start_ln(j, carry):
        ln_copy(j).start()
        return carry

    lax.fori_loop(1, n, start_rs, 0)
    lax.fori_loop(1, n_dp, start_ln, 0)
    rs_buf[d, c] = piece(d, c)[...]
    ln_buf[d] = ln_ref[...]

    def wait_rs(j, carry):
        src = lax.rem(me + j, n)
        pltpu.make_async_remote_copy(
            src_ref=piece(0, 0),
            dst_ref=rs_buf.at[src // n_col, src % n_col],
            send_sem=rs_send.at[j],
            recv_sem=rs_recv.at[src],
            device_id=(src // n_col, r, src % n_col),
            device_id_type=MESH,
        ).wait_recv()
        rs_copy(j).wait_send()
        return carry

    lax.fori_loop(1, n, wait_rs, 0)
    def wait_ln(j, carry):
        src = lax.rem(d + j, n_dp)
        pltpu.make_async_remote_copy(
            src_ref=ln_ref,
            dst_ref=ln_buf.at[src],
            send_sem=ln_send.at[j],
            recv_sem=ln_recv.at[src],
            device_id=(src, r, c),
            device_id_type=MESH,
        ).wait_recv()
        ln_copy(j).wait_send()
        return carry

    lax.fori_loop(1, n_dp, wait_ln, 0)
    ln_out[...] = jnp.sum(ln_buf[...].astype(jnp.float32), axis=0)

    ag_buf[d] = jnp.sum(rs_buf[...].astype(jnp.float32), axis=0)

    def ag_copy(slot, j, peer):
        return pltpu.make_async_remote_copy(
            src_ref=ag_buf.at[slot],
            dst_ref=ag_buf.at[slot],
            send_sem=ag_send.at[j],
            recv_sem=ag_recv.at[slot],
            device_id=(peer, r, c),
            device_id_type=MESH,
        )

    def arrive(slot):
        ag_copy(slot, 0, slot).wait_recv()

    n_rc = n_row * n_col
    me_rc = r * n_col + c

    def col_copy(j, peer, slot):
        return pltpu.make_async_remote_copy(
            src_ref=nbuf.at[slot],
            dst_ref=nbuf.at[slot],
            send_sem=n_send.at[j],
            recv_sem=n_recv.at[slot],
            device_id=(d, r, peer),
            device_id_type=MESH,
        )

    def row_copy(j, peer, slot):
        return pltpu.make_async_remote_copy(
            src_ref=nbuf.at[n_col + slot],
            dst_ref=nbuf.at[n_col + slot],
            send_sem=n_send.at[n_col + j],
            recv_sem=n_recv.at[n_col + slot],
            device_id=(d, peer, c),
            device_id_type=MESH,
        )

    def p_copy(j, peer, slot):
        return pltpu.make_async_remote_copy(
            src_ref=pbuf.at[slot],
            dst_ref=pbuf.at[slot],
            send_sem=p_send.at[j],
            recv_sem=p_recv.at[slot],
            device_id=(peer, r, c),
            device_id_type=MESH,
        )

    reach = 3
    n_right = n_dp // 2
    n_left = n_dp - 1 - n_right
    sends = []
    waited = set()
    n_copies = []
    for leg in range(0, n_right, reach):
        for sign, span in ((1, n_right), (-1, n_left)):
            if leg >= span:
                continue
            back = (n_dp - sign * leg) % n_dp
            slot = lax.rem(d + back, n_dp)
            if leg:
                arrive(slot)
                waited.add(back)
            for hop in range(1, min(reach, span - leg) + 1):
                peer = lax.rem(d + (n_dp + sign * hop) % n_dp, n_dp)
                copy = ag_copy(slot, len(sends), peer)
                copy.start()
                sends.append(copy)
        if leg == 0:
            lg = ln_out[...]
            own = ag_buf[d]
            part = jnp.sum(own * own) + (d == 0).astype(jnp.float32) * (
                jnp.sum(lg * lg) / float(n_row)
            )
            nbuf[c] = jnp.full(nbuf.shape[1:], part, jnp.float32)
            for j in range(1, n_col):
                copy = col_copy(j, lax.rem(c + j, n_col), c)
                copy.start()
                n_copies.append(copy)

    for j in range(1, n_col):
        sender = lax.rem(c + n_col - j, n_col)
        col_copy(j, sender, sender).wait_recv()
    for copy in n_copies:
        copy.wait_send()
    nbuf[n_col + r] = jnp.sum(nbuf[0:n_col], axis=0)
    n_copies = []
    for j in range(1, n_row):
        copy = row_copy(j, lax.rem(r + j, n_row), r)
        copy.start()
        n_copies.append(copy)
    for j in range(1, n_row):
        sender = lax.rem(r + n_row - j, n_row)
        row_copy(j, sender, sender).wait_recv()
    for copy in n_copies:
        copy.wait_send()
    pbuf[d] = jnp.sum(nbuf[n_col:n_col + n_row], axis=0)
    p_copies = []
    for j in range(1, n_dp):
        copy = p_copy(j, lax.rem(d + j, n_dp), d)
        copy.start()
        p_copies.append(copy)
    for back in range(1, n_dp):
        if back not in waited:
            arrive(lax.rem(d + back, n_dp))
    for copy in sends:
        copy.wait_send()
    for j in range(1, n_dp):
        sender = lax.rem(d + n_dp - j, n_dp)
        p_copy(j, sender, sender).wait_recv()
    for copy in p_copies:
        copy.wait_send()
    norm_total = jnp.sum(pbuf[...], axis=0)[0:1, 0:1]
    for k in range(n_dp):
        for q in range(n_col):
            g_out[
                pl.ds((k // halves) * depth, depth),
                pl.ds(q * halves * width + (k % halves) * width, width),
            ] = ag_buf[k, q]
    finish_part(n_col, g_out, m_ref, f_ref, s_ref, c_out, b_out, norm_total,
                mbuf, rbuf, m_send, m_recv)


def reduce_blocks(block, ln_part, master, first, second, average):
    n_dp, n_row, n_col = lax.axis_size("dp"), lax.axis_size("row"), lax.axis_size("col")
    rows, cols = block.shape
    quarter = rows // n_col
    width = 128
    halves = cols // width
    depth = quarter * halves // n_dp
    n = n_row * n_col
    vmem = pl.BlockSpec(memory_space=pltpu.VMEM)
    return pl.pallas_call(
        functools.partial(reduce_kernel, n_dp, n_row, n_col),
        out_shape=(
            jax.ShapeDtypeStruct((quarter, cols * n_col), jnp.float32),
            jax.ShapeDtypeStruct(ln_part.shape, jnp.float32),
            jax.ShapeDtypeStruct((8, 128), jnp.float32),
            jax.ShapeDtypeStruct(average.shape, jnp.float32),
        ),
        in_specs=[vmem] * 5,
        out_specs=(vmem, vmem, vmem, vmem),
        scratch_shapes=[
            pltpu.VMEM((n_dp, n_col, depth, width), block.dtype),
            pltpu.VMEM((n_dp, n_col, depth, width), jnp.float32),
            pltpu.VMEM((n_dp,) + ln_part.shape, ln_part.dtype),
            pltpu.SemaphoreType.DMA((n_dp * n_col,)),
            pltpu.SemaphoreType.DMA((n_dp * n_col,)),
            pltpu.SemaphoreType.DMA((n_dp,)),
            pltpu.SemaphoreType.DMA((n_dp,)),
            pltpu.SemaphoreType.DMA((n_dp,)),
            pltpu.SemaphoreType.DMA((n_dp,)),
            pltpu.VMEM((n, 8, 128), jnp.float32),
            pltpu.VMEM((n_col, master.shape[0], average.shape[1]), jnp.float32),
            pltpu.VMEM((n_col, master.shape[0], average.shape[1]), jnp.float32),
            pltpu.SemaphoreType.DMA((n,)),
            pltpu.SemaphoreType.DMA((n,)),
            pltpu.SemaphoreType.DMA((n_col,)),
            pltpu.SemaphoreType.DMA((n_col,)),
            pltpu.VMEM((n_dp, 8, 128), jnp.float32),
            pltpu.SemaphoreType.DMA((n_dp,)),
            pltpu.SemaphoreType.DMA((n_dp,)),
        ],
        compiler_params=pltpu.CompilerParams(collective_id=1, has_side_effects=True),
    )(block, ln_part, master, first, second)


def apply_kernel(c_ref, g_ref, m_ref, f_ref, s_ref, a_ref, b_ref, lg_ref, lm_ref, lf_ref, ls_ref,
                 la_ref, a_out, m_out, f_out, s_out, lm_out, lf_out, ls_out, la_out,
                 flat, block, small, sems):
    clip_scale = c_ref[0:1, 0:1]
    master_new, first_new, second_new = adam_step(
        g_ref[...], clip_scale, f_ref[...], s_ref[...], m_ref[...], decay_rate
    )
    flat[0] = master_new
    flat[1] = first_new
    flat[2] = second_new
    copies = [
        pltpu.make_async_copy(flat.at[0], m_out, sems.at[0]),
        pltpu.make_async_copy(flat.at[1], f_out, sems.at[1]),
        pltpu.make_async_copy(flat.at[2], s_out, sems.at[2]),
    ]
    for copy in copies:
        copy.start()
    block[...] = ema_keep * a_ref[...] + (1.0 - ema_keep) * b_ref[...]
    copy = pltpu.make_async_copy(block, a_out, sems.at[3])
    copy.start()
    copies.append(copy)
    ln_master_new, ln_first_new, ln_second_new = adam_step(
        lg_ref[...], clip_scale, lf_ref[...], ls_ref[...], lm_ref[...], 0.0
    )
    small[0] = ln_master_new
    small[1] = ln_first_new
    small[2] = ln_second_new
    small[3] = ema_keep * la_ref[...] + (1.0 - ema_keep) * ln_master_new
    for i, out in enumerate((lm_out, lf_out, ls_out, la_out)):
        copy = pltpu.make_async_copy(small.at[i], out, sems.at[4 + i])
        copy.start()
        copies.append(copy)
    for copy in copies:
        copy.wait()


def apply_update(clip_tile, gradient, master, first, second, average, block_master,
                 ln_gradient, ln_master, ln_first, ln_second, ln_average):
    vmem = pl.BlockSpec(memory_space=pltpu.VMEM)
    anywhere = pl.BlockSpec(memory_space=pl.ANY)
    outs = (average, master, first, second, ln_master, ln_first, ln_second, ln_average)
    return pl.pallas_call(
        apply_kernel,
        out_shape=tuple(jax.ShapeDtypeStruct(x.shape, jnp.float32) for x in outs),
        in_specs=[vmem] * 12,
        out_specs=tuple([anywhere] * 8),
        scratch_shapes=[
            pltpu.VMEM((3,) + master.shape, jnp.float32),
            pltpu.VMEM(average.shape, jnp.float32),
            pltpu.VMEM((4,) + ln_master.shape, jnp.float32),
            pltpu.SemaphoreType.DMA((8,)),
        ],
    )(clip_tile, gradient, master, first, second, average, block_master,
      ln_gradient, ln_master, ln_first, ln_second, ln_average)


def shards(
    grad_blocks,
    ln_grads,
    master,
    first_moment,
    second_moment,
    average,
    ln_master,
    ln_first,
    ln_second,
    ln_average,
):
    gradient, ln_gradient, clip_tile, block_master = reduce_blocks(
        grad_blocks[0], ln_grads[0], master, first_moment, second_moment, average
    )
    (
        average_new,
        master_new,
        first_new,
        second_new,
        ln_master_new,
        ln_first_new,
        ln_second_new,
        ln_average_new,
    ) = apply_update(
        clip_tile, gradient, master, first_moment, second_moment, average, block_master,
        ln_gradient, ln_master, ln_first, ln_second, ln_average,
    )
    return (
        average_new,
        master_new,
        first_new,
        second_new,
        ln_master_new,
        ln_first_new,
        ln_second_new,
        ln_average_new,
    )


def solution(mesh):
    placed = (
        P("dp", "row", "col"),
        P("dp", None, "col"),
        P(("row", "col"), None),
        P(("row", "col"), None),
        P(("row", "col"), None),
        P("row", "col"),
        P(None, "col"),
        P(None, "col"),
        P(None, "col"),
        P(None, "col"),
    )
    return jax.shard_map(
        shards,
        mesh=mesh,
        in_specs=placed,
        out_specs=(
            P("row", "col"),
            P(("row", "col"), None),
            P(("row", "col"), None),
            P(("row", "col"), None),
            P(None, "col"),
            P(None, "col"),
            P(None, "col"),
            P(None, "col"),
        ),
        check_vma=False,
    )
```

```python
import functools
import math

import jax
import jax.numpy as jnp
from jax import lax
from jax.experimental import pallas as pl
from jax.experimental.pallas import tpu as pltpu
from jax.sharding import PartitionSpec as P

MESH = pl.DeviceIdType.MESH

D = 1024
FF = 4096
STEP = 20


beta_one = 0.9
beta_two = 0.95
learn_rate = 0.02
decay_rate = 0.1
epsilon = 1e-08
clip_rms = 1.0
ema_keep = 0.9


def adam_step(gradient, clip_scale, first, second, master, decay_weight):
    clipped = clip_scale * gradient
    first_new = beta_one * first + (1.0 - beta_one) * clipped
    second_new = beta_two * second + (1.0 - beta_two) * clipped * clipped
    direction = (
        first_new
        / (1.0 - beta_one**STEP)
        / (jnp.sqrt(second_new / (1.0 - beta_two**STEP)) + epsilon)
    )
    master_new = master - learn_rate * (direction + decay_weight * master)
    return (master_new, first_new, second_new)


def clip_factor(norm_total):
    return jnp.minimum(1.0, clip_rms * math.sqrt(FF * D + 4 * D) / jnp.sqrt(norm_total))


def squares(gradient, ln_gradient, row_count):
    return jnp.sum(gradient * gradient) + jnp.sum(ln_gradient * ln_gradient) / row_count


def finish_part(n_col, g_ref, m_ref, f_ref, s_ref, c_out, b_out, norm_total,
                mbuf, rbuf, m_send, m_recv):
    d = lax.axis_index("dp")
    r = lax.axis_index("row")
    c = lax.axis_index("col")
    clip_scale = clip_factor(norm_total)
    c_out[...] = jnp.broadcast_to(clip_scale, c_out.shape)
    width = b_out.shape[1]

    def chunk(peer):
        cols = pl.ds(pl.multiple_of(peer * width, width), width)
        master_new, _, _ = adam_step(
            g_ref[:, cols], clip_scale, f_ref[:, cols], s_ref[:, cols], m_ref[:, cols], decay_rate
        )
        return master_new

    def m_copy(j, peer, slot):
        return pltpu.make_async_remote_copy(
            src_ref=mbuf.at[peer],
            dst_ref=rbuf.at[slot],
            send_sem=m_send.at[j],
            recv_sem=m_recv.at[slot],
            device_id=(d, r, peer),
            device_id_type=MESH,
        )

    copies = []
    for j in range(1, n_col):
        peer = lax.rem(c + j, n_col)
        mbuf[peer] = chunk(peer)
        copy = m_copy(j, peer, c)
        copy.start()
        copies.append(copy)
    rbuf[c] = chunk(c)
    for j in range(1, n_col):
        sender = lax.rem(c + n_col - j, n_col)
        m_copy(j, sender, sender).wait_recv()
    for copy in copies:
        copy.wait_send()
    depth = rbuf.shape[1]
    for q in range(n_col):
        b_out[pl.ds(q * depth, depth), :] = rbuf[q]


def reduce_kernel(n_dp, n_row, n_col, g_ref, ln_ref, m_ref, f_ref, s_ref,
                  g_out, ln_out, c_out, b_out, rs_buf, ag_buf, ln_buf,
                  rs_send, rs_recv, ag_send, ag_recv, ln_send, ln_recv,
                  nbuf, mbuf, rbuf, n_send, n_recv, m_send, m_recv, pbuf, p_send, p_recv):
    d = lax.axis_index("dp")
    r = lax.axis_index("row")
    c = lax.axis_index("col")
    n = n_dp * n_col
    me = d * n_col + c
    quarter = g_ref.shape[0] // n_col
    depth = rs_buf.shape[2]
    width = rs_buf.shape[3]
    halves = g_ref.shape[1] // width
    barrier = pltpu.get_barrier_semaphore()

    def greet(j, carry):
        peer = lax.rem(me + j, n)
        pl.semaphore_signal(
            barrier, inc=1, device_id=(peer // n_col, r, peer % n_col), device_id_type=MESH
        )
        return carry

    lax.fori_loop(1, n, greet, 0)

    def greet_row(j, carry):
        peer = lax.rem(r + 1 + j // n_col, n_row)
        pl.semaphore_signal(
            barrier, inc=1, device_id=(d, peer, j % n_col), device_id_type=MESH
        )
        return carry

    lax.fori_loop(0, (n_row - 1) * n_col, greet_row, 0)
    pl.semaphore_wait(barrier, n - 1 + (n_row - 1) * n_col)

    def piece(k, q):
        rows = pl.ds(pl.multiple_of(q * quarter + (k // halves) * depth, depth), depth)
        cols = pl.ds(pl.multiple_of((k % halves) * width, width), width)
        return g_ref.at[rows, cols]

    def rs_copy(j):
        peer = lax.rem(me + j, n)
        return pltpu.make_async_remote_copy(
            src_ref=piece(peer // n_col, peer % n_col),
            dst_ref=rs_buf.at[d, c],
            send_sem=rs_send.at[j],
            recv_sem=rs_recv.at[me],
            device_id=(peer // n_col, r, peer % n_col),
            device_id_type=MESH,
        )

    def ln_copy(j):
        peer = lax.rem(d + j, n_dp)
        return pltpu.make_async_remote_copy(
            src_ref=ln_ref,
            dst_ref=ln_buf.at[d],
            send_sem=ln_send.at[j],
            recv_sem=ln_recv.at[d],
            device_id=(peer, r, c),
            device_id_type=MESH,
        )

    def start_rs(j, carry):
        rs_copy(j).start()
        return carry

    def start_ln(j, carry):
        ln_copy(j).start()
        return carry

    lax.fori_loop(1, n, start_rs, 0)
    lax.fori_loop(1, n_dp, start_ln, 0)
    rs_buf[d, c] = piece(d, c)[...]
    ln_buf[d] = ln_ref[...]

    def wait_rs(j, carry):
        src = lax.rem(me + j, n)
        pltpu.make_async_remote_copy(
            src_ref=piece(0, 0),
            dst_ref=rs_buf.at[src // n_col, src % n_col],
            send_sem=rs_send.at[j],
            recv_sem=rs_recv.at[src],
            device_id=(src // n_col, r, src % n_col),
            device_id_type=MESH,
        ).wait_recv()
        rs_copy(j).wait_send()
        return carry

    lax.fori_loop(1, n, wait_rs, 0)
    def wait_ln(j, carry):
        src = lax.rem(d + j, n_dp)
        pltpu.make_async_remote_copy(
            src_ref=ln_ref,
            dst_ref=ln_buf.at[src],
            send_sem=ln_send.at[j],
            recv_sem=ln_recv.at[src],
            device_id=(src, r, c),
            device_id_type=MESH,
        ).wait_recv()
        ln_copy(j).wait_send()
        return carry

    lax.fori_loop(1, n_dp, wait_ln, 0)
    ln_out[...] = jnp.sum(ln_buf[...].astype(jnp.float32), axis=0)

    ag_buf[d] = jnp.sum(rs_buf[...].astype(jnp.float32), axis=0)

    def ag_copy(slot, j, peer):
        return pltpu.make_async_remote_copy(
            src_ref=ag_buf.at[slot],
            dst_ref=ag_buf.at[slot],
            send_sem=ag_send.at[j],
            recv_sem=ag_recv.at[slot],
            device_id=(peer, r, c),
            device_id_type=MESH,
        )

    def arrive(slot):
        ag_copy(slot, 0, slot).wait_recv()

    n_rc = n_row * n_col
    me_rc = r * n_col + c

    def n_copy(j, peer, slot):
        return pltpu.make_async_remote_copy(
            src_ref=nbuf.at[slot],
            dst_ref=nbuf.at[slot],
            send_sem=n_send.at[j],
            recv_sem=n_recv.at[slot],
            device_id=(d, peer // n_col, peer % n_col),
            device_id_type=MESH,
        )

    def p_copy(j, peer, slot):
        return pltpu.make_async_remote_copy(
            src_ref=pbuf.at[slot],
            dst_ref=pbuf.at[slot],
            send_sem=p_send.at[j],
            recv_sem=p_recv.at[slot],
            device_id=(peer, r, c),
            device_id_type=MESH,
        )

    reach = 3
    n_right = n_dp // 2
    n_left = n_dp - 1 - n_right
    sends = []
    waited = set()
    n_copies = []
    turn = 1 - 2 * (r % 2)
    for leg in range(0, n_right, reach):
        for sign, span in ((1, n_right), (-1, n_left)):
            if leg >= span:
                continue
            back = (n_dp - sign * leg) % n_dp
            slot = lax.rem(d + n_dp - sign * leg * turn, n_dp)
            if leg:
                arrive(slot)
                waited.add(back)
            for hop in range(1, min(reach, span - leg) + 1):
                peer = lax.rem(d + n_dp + sign * hop * turn, n_dp)
                copy = ag_copy(slot, len(sends), peer)
                copy.start()
                sends.append(copy)
        if leg == 0:
            lg = ln_out[...]
            own = ag_buf[d]
            part = jnp.sum(own * own) + (d == 0).astype(jnp.float32) * (
                jnp.sum(lg * lg) / float(n_row)
            )
            nbuf[me_rc] = jnp.full(nbuf.shape[1:], part, jnp.float32)
            for j in range(1, n_rc):
                copy = n_copy(j, lax.rem(me_rc + j, n_rc), me_rc)
                copy.start()
                n_copies.append(copy)

    for j in range(1, n_rc):
        sender = lax.rem(me_rc + n_rc - j, n_rc)
        n_copy(j, sender, sender).wait_recv()
    for copy in n_copies:
        copy.wait_send()
    pbuf[d] = jnp.sum(nbuf[...], axis=0)
    p_copies = []
    for j in range(1, n_dp):
        copy = p_copy(j, lax.rem(d + j, n_dp), d)
        copy.start()
        p_copies.append(copy)
    for back in range(1, n_dp):
        if back not in waited:
            arrive(lax.rem(d + back, n_dp))
    for copy in sends:
        copy.wait_send()
    for j in range(1, n_dp):
        sender = lax.rem(d + n_dp - j, n_dp)
        p_copy(j, sender, sender).wait_recv()
    for copy in p_copies:
        copy.wait_send()
    norm_total = jnp.sum(pbuf[...], axis=0)[0:1, 0:1]
    for k in range(n_dp):
        for q in range(n_col):
            g_out[
                pl.ds((k // halves) * depth, depth),
                pl.ds(q * halves * width + (k % halves) * width, width),
            ] = ag_buf[k, q]
    finish_part(n_col, g_out, m_ref, f_ref, s_ref, c_out, b_out, norm_total,
                mbuf, rbuf, m_send, m_recv)


def reduce_blocks(block, ln_part, master, first, second, average):
    n_dp, n_row, n_col = lax.axis_size("dp"), lax.axis_size("row"), lax.axis_size("col")
    rows, cols = block.shape
    quarter = rows // n_col
    width = 128
    halves = cols // width
    depth = quarter * halves // n_dp
    n = n_row * n_col
    vmem = pl.BlockSpec(memory_space=pltpu.VMEM)
    return pl.pallas_call(
        functools.partial(reduce_kernel, n_dp, n_row, n_col),
        out_shape=(
            jax.ShapeDtypeStruct((quarter, cols * n_col), jnp.float32),
            jax.ShapeDtypeStruct(ln_part.shape, jnp.float32),
            jax.ShapeDtypeStruct((8, 128), jnp.float32),
            jax.ShapeDtypeStruct(average.shape, jnp.float32),
        ),
        in_specs=[vmem] * 5,
        out_specs=(vmem, vmem, vmem, vmem),
        scratch_shapes=[
            pltpu.VMEM((n_dp, n_col, depth, width), block.dtype),
            pltpu.VMEM((n_dp, n_col, depth, width), jnp.float32),
            pltpu.VMEM((n_dp,) + ln_part.shape, ln_part.dtype),
            pltpu.SemaphoreType.DMA((n_dp * n_col,)),
            pltpu.SemaphoreType.DMA((n_dp * n_col,)),
            pltpu.SemaphoreType.DMA((n_dp,)),
            pltpu.SemaphoreType.DMA((n_dp,)),
            pltpu.SemaphoreType.DMA((n_dp,)),
            pltpu.SemaphoreType.DMA((n_dp,)),
            pltpu.VMEM((n, 8, 128), jnp.float32),
            pltpu.VMEM((n_col, master.shape[0], average.shape[1]), jnp.float32),
            pltpu.VMEM((n_col, master.shape[0], average.shape[1]), jnp.float32),
            pltpu.SemaphoreType.DMA((n,)),
            pltpu.SemaphoreType.DMA((n,)),
            pltpu.SemaphoreType.DMA((n_col,)),
            pltpu.SemaphoreType.DMA((n_col,)),
            pltpu.VMEM((n_dp, 8, 128), jnp.float32),
            pltpu.SemaphoreType.DMA((n_dp,)),
            pltpu.SemaphoreType.DMA((n_dp,)),
        ],
        compiler_params=pltpu.CompilerParams(collective_id=1, has_side_effects=True),
    )(block, ln_part, master, first, second)


def apply_kernel(c_ref, g_ref, m_ref, f_ref, s_ref, a_ref, b_ref, lg_ref, lm_ref, lf_ref, ls_ref,
                 la_ref, a_out, m_out, f_out, s_out, lm_out, lf_out, ls_out, la_out,
                 flat, block, small, sems):
    clip_scale = c_ref[0:1, 0:1]
    master_new, first_new, second_new = adam_step(
        g_ref[...], clip_scale, f_ref[...], s_ref[...], m_ref[...], decay_rate
    )
    flat[0] = master_new
    flat[1] = first_new
    flat[2] = second_new
    copies = [
        pltpu.make_async_copy(flat.at[0], m_out, sems.at[0]),
        pltpu.make_async_copy(flat.at[1], f_out, sems.at[1]),
        pltpu.make_async_copy(flat.at[2], s_out, sems.at[2]),
    ]
    for copy in copies:
        copy.start()
    block[...] = ema_keep * a_ref[...] + (1.0 - ema_keep) * b_ref[...]
    copy = pltpu.make_async_copy(block, a_out, sems.at[3])
    copy.start()
    copies.append(copy)
    ln_master_new, ln_first_new, ln_second_new = adam_step(
        lg_ref[...], clip_scale, lf_ref[...], ls_ref[...], lm_ref[...], 0.0
    )
    small[0] = ln_master_new
    small[1] = ln_first_new
    small[2] = ln_second_new
    small[3] = ema_keep * la_ref[...] + (1.0 - ema_keep) * ln_master_new
    for i, out in enumerate((lm_out, lf_out, ls_out, la_out)):
        copy = pltpu.make_async_copy(small.at[i], out, sems.at[4 + i])
        copy.start()
        copies.append(copy)
    for copy in copies:
        copy.wait()


def apply_update(clip_tile, gradient, master, first, second, average, block_master,
                 ln_gradient, ln_master, ln_first, ln_second, ln_average):
    vmem = pl.BlockSpec(memory_space=pltpu.VMEM)
    anywhere = pl.BlockSpec(memory_space=pl.ANY)
    outs = (average, master, first, second, ln_master, ln_first, ln_second, ln_average)
    return pl.pallas_call(
        apply_kernel,
        out_shape=tuple(jax.ShapeDtypeStruct(x.shape, jnp.float32) for x in outs),
        in_specs=[vmem] * 12,
        out_specs=tuple([anywhere] * 8),
        scratch_shapes=[
            pltpu.VMEM((3,) + master.shape, jnp.float32),
            pltpu.VMEM(average.shape, jnp.float32),
            pltpu.VMEM((4,) + ln_master.shape, jnp.float32),
            pltpu.SemaphoreType.DMA((8,)),
        ],
    )(clip_tile, gradient, master, first, second, average, block_master,
      ln_gradient, ln_master, ln_first, ln_second, ln_average)


def shards(
    grad_blocks,
    ln_grads,
    master,
    first_moment,
    second_moment,
    average,
    ln_master,
    ln_first,
    ln_second,
    ln_average,
):
    gradient, ln_gradient, clip_tile, block_master = reduce_blocks(
        grad_blocks[0], ln_grads[0], master, first_moment, second_moment, average
    )
    (
        average_new,
        master_new,
        first_new,
        second_new,
        ln_master_new,
        ln_first_new,
        ln_second_new,
        ln_average_new,
    ) = apply_update(
        clip_tile, gradient, master, first_moment, second_moment, average, block_master,
        ln_gradient, ln_master, ln_first, ln_second, ln_average,
    )
    return (
        average_new,
        master_new,
        first_new,
        second_new,
        ln_master_new,
        ln_first_new,
        ln_second_new,
        ln_average_new,
    )


def solution(mesh):
    placed = (
        P("dp", "row", "col"),
        P("dp", None, "col"),
        P(("row", "col"), None),
        P(("row", "col"), None),
        P(("row", "col"), None),
        P("row", "col"),
        P(None, "col"),
        P(None, "col"),
        P(None, "col"),
        P(None, "col"),
    )
    return jax.shard_map(
        shards,
        mesh=mesh,
        in_specs=placed,
        out_specs=(
            P("row", "col"),
            P(("row", "col"), None),
            P(("row", "col"), None),
            P(("row", "col"), None),
            P(None, "col"),
            P(None, "col"),
            P(None, "col"),
            P(None, "col"),
        ),
        check_vma=False,
    )
```
